512 devices in a mesh: lon: 32 (over y_lo, z), sec: 4 (over y_hi, core), rad: 4 (over x).
Axes of the slice: x: 4, y: 8 (y_hi: 2, y_lo: 4; y = y_hi * 4 + y_lo), z: 8, core: 2. Of those that a mesh axis runs over, the one named last changes fastest.
Arguments:
- plasma_fields: float32 [8, 64, 128, 512], P(None, 'sec', 'lon', 'rad'), may hold values from -6 to 6
- velocity: bfloat16 [3, 64, 128, 512], P(None, 'sec', 'lon', 'rad'), may hold values from -1 to 1
- resistivity: bfloat16 [64, 128, 512], P('sec', 'lon', 'rad'), may hold values from 0.0049743652 to 0.039794922
- conductance: float32 [128, 512], P('lon', 'rad'), may hold values from 0.5 to 5
- foot_map: int32 [65536, 256], P(('lon', 'sec', 'rad')), may hold values from 0 to 511
- foot_owner: int32 [65536, 1], P(('lon', 'sec', 'rad')), may hold values from 0 to 127; in each aligned block of 128 rows (0 to 127, 128 to 255, ...) at most 2 rows name the same one
- foot_row: int32 [65536], P(('lon', 'sec', 'rad')), may hold values from 0 to 31
Outputs:
- advanced_fields: float32 [8, 64, 128, 512], P(None, 'sec', 'lon', 'rad')
- potential: float32 [128, 512], P('lon', 'rad')
- foot_table: float32 [16384, 256], P(('lon', 'sec', 'rad'))
The draws below stay inside these ranges and needn't reach their ends.
Inputs may be any that keep to these rules, and one draw needn't show every extreme that they name: `foot_owner`: in each aligned block of 128 rows (the records of one device) no owner index appears more than 2 times.
All inputs are finite; a program needn't handle non-finite values.
Results may differ from the reference program's by a relative error of at most 0.0003.
Values sent between devices are 32-bit elements; how exact they have to be, the bound alone decides.
No kernel may reach another device: no remote copies, remote signals or barrier semaphores. Data moves between devices by JAX's collectives and lax.ppermute only.
A program may use at most 128 MiB of HBM per device.

```python
import math
import jax
import jax.numpy as jnp
import numpy as np
from jax import lax

LON_DEV = 4
LAT_DEV = 128
PHASES = 4
SWEEPS = 8
POINTS = 256
REC_DEV = 128
ROWS_OWN = 32
NR = 64
NLON = 128
NLAT = 512
RECORDS = 65536
CAP = 2
N_LON = 32
N_SEC = 4
N_RAD = 4


def plant(values, stream_key, smallest, high):
    shape = values.shape
    index_at = [jax.random.randint(jax.random.fold_in(stream_key, axis), (), 0, shape[axis]) for axis in range(len(shape))]
    values = values.at[tuple(index_at)].set(smallest)
    longest = shape.index(max(shape))
    index_at[longest] = (index_at[longest] + 1) % shape[longest]
    return values.at[tuple(index_at)].set(high)


def level_of(rng, dims, shards, least, largest):
    def one(dim, blocks):
        draws = jax.random.uniform(jax.random.fold_in(jax.random.fold_in(rng, 6), dim), (blocks,), jnp.float32, least / len(shards), largest / len(shards))
        return jnp.repeat(jnp.exp(draws), dims[dim] // blocks).reshape((-1,) + (1,) * (len(dims) - dim - 1))

    factor_of = one(*shards[0])
    for cut in shards[1:]:
        factor_of = factor_of * one(*cut)
    return factor_of


def shared_out(own_key, own, number, rows, amount, top, reach, lean):
    sequence = jax.random.permutation(own_key, amount)
    heavy_load, common = shares(amount, rows * top, reach, lean, True), shares(amount, rows * top, reach, lean, False)
    places = jnp.arange(amount)

    def named(lengths, turn):
        used = int((lengths > 0).sum())
        fixed = max(1, used // 4)
        passed = fixed + (places - fixed + turn * (used - fixed)) % max(1, amount - fixed)
        return jnp.zeros((amount,), jnp.int32).at[sequence[jnp.where(places < fixed, places, passed)]].set(jnp.asarray(lengths, jnp.int32))

    lengths = jnp.where(number % 4 == 0, named(heavy_load, number // 4), named(common, number - number // 4 - 1))
    mixed = jax.random.permutation(jax.random.fold_in(own, 3), amount)
    giver, taker = mixed[0:amount // 2 * 2:2], mixed[1:amount // 2 * 2:2]
    room = jnp.minimum(lengths[giver] - 1, reach - lengths[taker]) // 2
    room = jnp.where((giver == sequence[0]) | (taker == sequence[0]) | (lengths[taker] == 0), 0, jnp.maximum(room, 0))
    passed = jax.random.randint(jax.random.fold_in(own, 4), (amount // 2,), 0, 1 << 20) % (room + 1)
    lengths = lengths.at[giver].add(-passed).at[taker].add(passed)
    members = jnp.searchsorted(jnp.cumsum(lengths), jnp.arange(rows * top), side="right").astype(jnp.int32)
    table = members.reshape(top, rows).T
    table = table[jax.random.permutation(jax.random.fold_in(own, 1), rows)]
    turn = jax.random.randint(jax.random.fold_in(own, 2), (rows, 1), 0, top)
    return jnp.take_along_axis(table, (jnp.arange(top)[None, :] + turn) % top, axis=1)


def shares(amount, total, bound, skew, full):
    portions = [(1 << 20) // math.isqrt(standing ** skew) + 1 for standing in range(1, amount + 1)]
    largest = bound if full else min(bound, max(-(-total // amount), total * portions[0] // sum(portions)))
    least = 1 if total - largest >= amount - 1 else 0
    given, spare = [largest] + [least] * (amount - 1), total - largest - least * (amount - 1)
    while spare > 0:
        movable = [i for i in range(1, amount) if given[i] < largest] or [i for i in range(1, amount) if given[i] < bound]
        mass, remaining = sum([portions[i] for i in movable]), spare
        for i in movable:
            more = min(bound - given[i], max(1, remaining * portions[i] // mass), spare)
            given[i] = given[i] + more
            spare = spare - more
    return np.array(given)


def bell_draw(own_key, extent, scale, limit, pieces=(), held_as=jnp.bfloat16):
    drawn = jax.random.normal(own_key, extent, jnp.float32) * scale
    if len(pieces) > 0:
        drawn = level_of(own_key, extent, pieces, -0.22, 0.18) * drawn
    return jnp.clip(drawn, min=-limit, max=limit).astype(held_as)


def setup_inputs(seed: int = 0) -> dict:
    arg_keys = jax.random.split(jax.random.key(seed), 8)
    plasma_fields = bell_draw(arg_keys[0], (8, NR, NLON, NLAT), 1.0, 6.0, ((1, 4), (2, 32), (3, 4)), jnp.float32)
    velocity = jnp.clip(jax.random.uniform(arg_keys[1], (3, NR, NLON, NLAT), jnp.float32, -1.0, 1.0) * level_of(arg_keys[1], (3, NR, NLON, NLAT), ((1, 4), (2, 32), (3, 4)), -0.4, 0.0), -1.0, 1.0).astype(jnp.bfloat16)
    resistivity = jnp.clip(jnp.exp(math.log(0.039794922) - 2.0794415 * jax.random.uniform(arg_keys[2], (NR, NLON, NLAT), jnp.float32) ** level_of(arg_keys[2], (NR, NLON, NLAT), ((0, 4), (1, 32), (2, 4)), -0.2, 0.2)), 0.0049743652, 0.039794922).astype(jnp.bfloat16)
    conductance = jnp.clip(jnp.exp(math.log(5.0) - 2.3025851 * jax.random.uniform(arg_keys[3], (NLON, NLAT), jnp.float32) ** level_of(arg_keys[3], (NLON, NLAT), ((0, 32), (1, 4)), -0.2, 0.2)), 0.5, 5.0)
    foot_map = plant(jax.random.randint(arg_keys[4], (RECORDS, POINTS), 0, LON_DEV * LAT_DEV), jax.random.fold_in(arg_keys[4], 1), 0, (LON_DEV * LAT_DEV) - 1).astype(jnp.int32)
    foot_owner_keys = jax.random.split(jax.random.fold_in(arg_keys[5], 1), RECORDS // REC_DEV)
    foot_owner_turns = jax.random.permutation(jax.random.fold_in(arg_keys[5], 3), RECORDS // REC_DEV)
    foot_owner = jax.vmap(lambda own, number: shared_out(jax.random.fold_in(arg_keys[5], 2), own, number, REC_DEV, N_LON * N_RAD, 1, CAP, 2))(foot_owner_keys, foot_owner_turns).reshape((RECORDS, 1))
    foot_row = plant(jax.random.randint(arg_keys[6], (RECORDS,), 0, ROWS_OWN), jax.random.fold_in(arg_keys[6], 1), 0, ROWS_OWN - 1).astype(jnp.int32)
    return {"plasma_fields": plasma_fields, "velocity": velocity, "resistivity": resistivity, "conductance": conductance, "foot_map": foot_map, "foot_owner": foot_owner, "foot_row": foot_row}


COURANT = 0.25
DAMPING = 0.05
RELAX = 0.8


def advance(padded, velocity_f, resist_f):
    centre = padded[:, 1:-1, 1:-1, 1:-1]
    shell_lo = padded[:, :-2, 1:-1, 1:-1]
    shell_hi = padded[:, 2:, 1:-1, 1:-1]
    lon_lo = padded[:, 1:-1, :-2, 1:-1]
    lon_hi = padded[:, 1:-1, 2:, 1:-1]
    lat_lo = padded[:, 1:-1, 1:-1, :-2]
    lat_hi = padded[:, 1:-1, 1:-1, 2:]

    def upwind(component, lower_side, upper_side):
        return jnp.maximum(component, 0.0) * (centre - lower_side) + jnp.minimum(component, 0.0) * (upper_side - centre)

    transport = upwind(velocity_f[0], shell_lo, shell_hi) + upwind(velocity_f[1], lon_lo, lon_hi) + upwind(velocity_f[2], lat_lo, lat_hi)
    spread = shell_lo + shell_hi + lon_lo + lon_hi + lat_lo + lat_hi - 6.0 * centre
    return centre - COURANT * transport + resist_f * spread


def frame_plane(values):
    wrapped = jnp.concatenate([values[..., -1:, :], values, values[..., :1, :]], axis=-2)
    widths = [(0, 0)] * (values.ndim - 1) + [(1, 1)]
    return jnp.pad(wrapped, widths)


def reference(plasma_fields, velocity, resistivity, conductance, foot_map, foot_owner, foot_row):
    velocity_f = velocity.astype(jnp.float32)
    resist_f = resistivity.astype(jnp.float32)

    def one_field(single):
        current = single
        for step_index in range(PHASES):
            wrapped = jnp.concatenate([current[:, -1:, :], current, current[:, :1, :]], axis=1)
            padded = jnp.pad(wrapped, ((1, 1), (0, 0), (1, 1)))
            current = advance(padded[None], velocity_f, resist_f)[0]
        return current

    advanced = lax.map(one_field, plasma_fields)
    base = jnp.concatenate([advanced[5:7, 0], conductance[None]], axis=0)
    framed = frame_plane(base)
    field_lon = framed[0]
    field_lat = framed[1]
    cond_all = framed[2]
    source = (field_lat[2:, 1:-1] - field_lat[:-2, 1:-1]) - (field_lon[1:-1, 2:] - field_lon[1:-1, :-2])
    middle = cond_all[1:-1, 1:-1]
    east = 0.5 * (middle + cond_all[2:, 1:-1])
    west = 0.5 * (middle + cond_all[:-2, 1:-1])
    north = 0.5 * (middle + cond_all[1:-1, 2:])
    south = 0.5 * (middle + cond_all[1:-1, :-2])
    diagonal = DAMPING * middle + east + west + north + south
    potential = jnp.zeros_like(conductance)
    for sweep_index in range(SWEEPS):
        framed_phi = frame_plane(potential)
        centre = framed_phi[1:-1, 1:-1]
        image = diagonal * centre - (east * framed_phi[2:, 1:-1] + west * framed_phi[:-2, 1:-1] + north * framed_phi[1:-1, 2:] + south * framed_phi[1:-1, :-2])
        potential = centre + RELAX * (source - image) / diagonal
    blocks = potential.reshape(N_LON, LON_DEV, N_RAD, LAT_DEV).transpose(0, 2, 1, 3).reshape(N_LON * N_RAD, LON_DEV * LAT_DEV)
    device = (jnp.arange(RECORDS) // REC_DEV).astype(jnp.int32)
    lon_of = device // (N_SEC * N_RAD)
    sec_of = (device // N_RAD) % N_SEC
    rad_of = device % N_RAD
    records = blocks[(lon_of * N_RAD + rad_of)[:, None], foot_map]
    target = foot_owner[:, 0]
    owner = (target // N_RAD) * (N_SEC * N_RAD) + sec_of * N_RAD + target % N_RAD
    foot_table = jax.ops.segment_sum(records, owner * ROWS_OWN + foot_row, num_segments=N_LON * N_SEC * N_RAD * ROWS_OWN)
    return advanced, potential, foot_table
```

```python
import jax
import jax.numpy as jnp
from jax import lax
from jax.experimental import pallas as pl
from jax.experimental.pallas import tpu as pltpu
from jax.sharding import PartitionSpec as P

PHASES = 4
SWEEPS = 8
ROWS_OWN = 32
COURANT = 0.25
DAMPING = 0.05
RELAX = 0.8

FIELDS = 8
PLANES = FIELDS + 4
SHELLS = 16
LONS = 4
LATS = 128
WIDE = 3 * LONS
TALL = SHELLS + 2 * PHASES
F32 = jnp.float32


def call(body, out_shape, args, scratch=(), smem=(), flops=10**6, traffic=10**6):
    specs = [
        pl.BlockSpec(memory_space=pltpu.SMEM if i in smem else pltpu.VMEM)
        for i in range(len(args))
    ]
    many = isinstance(out_shape, (tuple, list))
    vmem = pl.BlockSpec(memory_space=pltpu.VMEM)
    return pl.pallas_call(
        body,
        out_shape=out_shape,
        in_specs=specs,
        out_specs=[vmem] * len(out_shape) if many else vmem,
        scratch_shapes=list(scratch),
        compiler_params=pltpu.CompilerParams(vmem_limit_bytes=40 * 2**20),
        cost_estimate=pl.CostEstimate(flops=flops, bytes_accessed=traffic, transcendentals=0),
    )(*args)


def arr(*shape):
    return jax.ShapeDtypeStruct(shape, F32)


def shift(axis, step, closed):
    count = lax.axis_size(axis)
    return [
        (i, (i + step) % count) for i in range(count) if closed or 0 <= i + step < count
    ]


def stage_body(fields, speeds, out):
    for plane in range(PLANES):
        for lon in range(LONS):
            rows = pl.ds(lon, SHELLS, stride=LONS)
            if plane < FIELDS:
                out[plane, lon] = fields[plane, rows, :]
            else:
                out[plane, lon] = speeds[plane - FIELDS, rows, :]


def edge_body(low, own, high, out):
    group = lax.broadcasted_iota(jnp.int32, (SHELLS, LATS), 1) // 8
    for plane in range(PLANES):
        packed = jnp.zeros((SHELLS, LATS), F32)
        for wide in range(1, WIDE - 1):
            ref = (low, own, high)[wide // LONS]
            turned = pltpu.roll(ref[plane, wide % LONS], 8 * wide + 4, axis=1)
            packed = jnp.where(group == wide, turned, packed)
        out[plane] = packed


def halo_lanes(edges, wide):
    lane = lax.broadcasted_iota(jnp.int32, edges.shape, 1)
    turned = pltpu.roll(edges, (LATS - 8 * wide - 4) % LATS, axis=1)
    return jnp.where((lane < 4) | (lane >= LATS - 4), turned, 0.0)


def weights(speeds, resist):
    out = []
    total = None
    for speed in speeds:
        lower = COURANT * jnp.maximum(speed, 0.0) + resist
        upper = resist - COURANT * jnp.minimum(speed, 0.0)
        out += [lower, upper]
        total = lower + upper if total is None else total + lower + upper
    return [1.0 - total] + out


def blend(w, centre, shell_lo, shell_hi, lon_lo, lon_hi, lat_lo, lat_hi):
    return (
        w[0] * centre
        + (w[1] * shell_lo + w[2] * shell_hi)
        + (w[3] * lon_lo + w[4] * lon_hi)
        + (w[5] * lat_lo + w[6] * lat_hi)
    )


def inner_body(spot, low, own, high, from_low, from_high, conductance, out, rows):
    lane = lax.broadcasted_iota(jnp.int32, (8, LATS), 1)
    bottom = lax.broadcasted_iota(jnp.int32, (8, 2 * LATS), 0) == 0

    def plane_of(plane):
        edges = jnp.where(lane % 8 < 4, from_low[plane, :8, :], from_high[plane, :8, :])
        made = []
        for wide in range(WIDE):
            ref = (low, own, high)[wide // LONS]
            if 0 < wide < WIDE - 1:
                tail = halo_lanes(edges, wide)
            else:
                tail = jnp.zeros((8, LATS), F32)
            made.append(jnp.concatenate([ref[plane, wide % LONS, :8, :], tail], axis=1))
        return made

    speeds = [plane_of(FIELDS + d) for d in range(4)]
    w = [None] + [
        weights([speeds[d][wide] for d in range(3)], speeds[3][wide])
        for wide in range(1, WIDE - 1)
    ]
    for part in range(2):
        cells = plane_of(5 + part)
        for phase in range(PHASES):
            fresh = list(cells)
            for wide in range(phase + 1, WIDE - 1 - phase):
                c = cells[wide]
                fresh[wide] = blend(
                    w[wide],
                    c,
                    jnp.where(bottom, 0.0, pltpu.roll(c, 1, axis=0)),
                    pltpu.roll(c, 7, axis=0),
                    cells[wide - 1],
                    cells[wide + 1],
                    pltpu.roll(c, 1, axis=1),
                    pltpu.roll(c, 2 * LATS - 1, axis=1),
                )
            cells = fresh
        for lon in range(LONS):
            row = part * LONS + lon
            rows[row : row + 1, :] = cells[LONS + lon][0:1, :LATS]
    rows[8:12, :] = conductance[...]
    rows[12:16, :] = jnp.zeros((4, LATS), F32)
    mine = rows[...]
    for rad in range(4):
        kept = jnp.where((spot[0] == 0) & (spot[1] == rad), mine, 0.0)
        out[rad * 12 : rad * 12 + 12, :] = kept[:12]


def chunks():
    found = []
    at = 0
    for wide in range(1, WIDE - 1):
        far = max(LONS - wide, wide - 2 * LONS + 1, 0)
        count = PHASES - far
        found.append((wide, at, count))
        at += count
    return found, at


def pack_body(low, own, high, from_low, from_high, up, down):
    found, at = chunks()
    lane = lax.broadcasted_iota(jnp.int32, (8, LATS), 1)
    for plane in range(PLANES):
        for wide, start, count in found:
            ref = (low, own, high)[wide // LONS]
            up[plane, start : start + count, :] = ref[plane, wide % LONS, SHELLS - count :, :]
            down[plane, start : start + count, :] = ref[plane, wide % LONS, :count, :]
        first = jnp.where(lane % 8 < 4, from_low[plane, :8, :], from_high[plane, :8, :])
        last = jnp.where(lane % 8 < 4, from_low[plane, 8:, :], from_high[plane, 8:, :])
        up[plane, at : at + 4, :] = last[4:]
        down[plane, at : at + 4, :] = first[:4]


def main_body(low, own, high, from_low, from_high, above, below, out, cells, w, speeds, edges):
    found, at = chunks()
    lane = lax.broadcasted_iota(jnp.int32, (SHELLS, LATS), 1)

    def fill(plane, target):
        edges[:SHELLS, :] = jnp.where(lane % 8 < 4, from_low[plane], from_high[plane])
        edges[SHELLS : SHELLS + 4, :] = above[plane, at : at + 4, :]
        edges[SHELLS + 4 :, :] = below[plane, at : at + 4, :]
        strip = edges[...]
        for wide in range(WIDE):
            ref = (low, own, high)[wide // LONS]
            target[wide, :SHELLS, :LATS] = ref[plane, wide % LONS]
            target[wide, SHELLS:, :LATS] = jnp.zeros((8, LATS), F32)
            if 0 < wide < WIDE - 1:
                target[wide, :, LATS:] = halo_lanes(strip, wide)
            else:
                target[wide, :, LATS:] = jnp.zeros((TALL, LATS), F32)
        for wide, start, count in found:
            target[wide, SHELLS : SHELLS + count, :LATS] = above[plane, start : start + count, :]
            target[wide, TALL - count :, :LATS] = below[plane, start : start + count, :]

    for d in range(4):
        fill(FIELDS + d, speeds.at[d])
    for wide in range(1, WIDE - 1):
        made = weights([speeds[d, wide] for d in range(3)], speeds[3, wide])
        for i in range(7):
            w[i, wide] = made[i]

    def one(field, carry):
        fill(field, cells.at[0])
        for phase in range(PHASES):
            old = cells.at[phase % 2]
            new = cells.at[(phase + 1) % 2]
            for wide in range(phase + 1, WIDE - 1 - phase):
                c = old[wide]
                made = blend(
                    [w[i, wide] for i in range(7)],
                    c,
                    pltpu.roll(c, 1, axis=0),
                    pltpu.roll(c, TALL - 1, axis=0),
                    old[wide - 1],
                    old[wide + 1],
                    pltpu.roll(c, 1, axis=1),
                    pltpu.roll(c, 2 * LATS - 1, axis=1),
                )
                if phase == PHASES - 1:
                    out[field, pl.ds(wide - LONS, SHELLS, stride=LONS), :] = made[:SHELLS, :LATS]
                else:
                    new[wide] = made
        return carry

    lax.fori_loop(0, FIELDS, one, 0)


def slot_body(owners, rows, maps, out):
    count = owners.shape[1]
    here = lax.broadcasted_iota(jnp.int32, (count, count), 0)
    there = lax.broadcasted_iota(jnp.int32, (count, count), 1)
    aimed = here == owners[...]
    earlier = jnp.dot(
        aimed.astype(jnp.bfloat16), (here < there).astype(jnp.bfloat16), preferred_element_type=F32
    )
    cell = maps[...]
    small = (cell & 127).astype(F32).astype(jnp.bfloat16)
    large = (cell >> 7).astype(F32).astype(jnp.bfloat16)
    row = (rows[...] + 1).astype(F32)
    marks = []
    for slot in range(2):
        chosen = jnp.where(aimed & (earlier == float(slot)), 1.0, 0.0)
        marks.append(jnp.sum(chosen * row, axis=1, keepdims=True) - 1.0)
        pick = chosen.astype(jnp.bfloat16)
        made = jnp.dot(pick, small, preferred_element_type=F32) + 128.0 * jnp.dot(
            pick, large, preferred_element_type=F32
        )
        for half in range(2):
            out[pl.ds(2 * slot + half, count, stride=8), :] = made[:, 128 * half : 128 * half + 128]
    out[pl.ds(4, count, stride=8), :] = jnp.where(there < 64, marks[0], marks[1])
    for spare in range(5, 8):
        out[pl.ds(spare, count, stride=8), :] = jnp.zeros((count, count), F32)


def final_body(spot, planes, maps, pot, foot, phi, east_w, west_w, north_w, south_w, start, picked, hot):
    devs, rads = 32, 4
    wide = rads * LATS
    lane = lax.broadcasted_iota(jnp.int32, (devs, wide), 1)

    def gather(part):
        return [
            jnp.concatenate(
                [
                    planes[pl.ds(rad * 12 + part * LONS + lon, devs, stride=48), :]
                    for rad in range(rads)
                ],
                axis=1,
            )
            for lon in range(LONS)
        ]

    def lon_up(values, lon):
        return values[lon + 1] if lon < LONS - 1 else pltpu.roll(values[0], devs - 1, axis=0)

    def lon_down(values, lon):
        return values[lon - 1] if lon > 0 else pltpu.roll(values[LONS - 1], 1, axis=0)

    def lat_up(value):
        return pltpu.roll(value, wide - 1, axis=1)

    def lat_down(value):
        return pltpu.roll(value, 1, axis=1)

    blon, blat, cond = gather(0), gather(1), gather(2)
    last, first = lane == wide - 1, lane == 0
    for lon in range(LONS):
        source = (
            lon_up(blat, lon)
            - lon_down(blat, lon)
            - (
                jnp.where(last, 0.0, lat_up(blon[lon]))
                - jnp.where(first, 0.0, lat_down(blon[lon]))
            )
        )
        c = cond[lon]
        east = 0.5 * (c + lon_up(cond, lon))
        west = 0.5 * (c + lon_down(cond, lon))
        north = 0.5 * (c + jnp.where(last, 0.0, lat_up(c)))
        south = 0.5 * (c + jnp.where(first, 0.0, lat_down(c)))
        scale = RELAX / (DAMPING * c + east + west + north + south)
        east_w[lon] = east * scale
        west_w[lon] = west * scale
        north_w[lon] = jnp.where(last, 0.0, north * scale)
        south_w[lon] = jnp.where(first, 0.0, south * scale)
        start[lon] = source * scale
        phi[0, lon] = source * scale

    def sweep(old, new):
        values = [phi[old, lon] for lon in range(LONS)]
        for lon in range(LONS):
            c = values[lon]
            phi[new, lon] = (
                (1.0 - RELAX) * c
                + start[lon]
                + (east_w[lon] * lon_up(values, lon) + west_w[lon] * lon_down(values, lon))
                + (north_w[lon] * lat_up(c) + south_w[lon] * lat_down(c))
            )

    for turn in range(SWEEPS - 1):
        sweep(turn % 2, (turn + 1) % 2)
    done = (SWEEPS - 1) % 2
    at_lon = lax.broadcasted_iota(jnp.int32, (devs, LATS), 0) == spot[2]
    for rad in range(rads):

        @pl.when(spot[1] == rad)
        def _():
            for lon in range(LONS):
                block = phi[done, lon, :, rad * LATS : (rad + 1) * LATS]
                pot[lon : lon + 1, :] = jnp.sum(
                    jnp.where(at_lon, block, 0.0), axis=0, keepdims=True
                )

    slot_lane = lax.broadcasted_iota(jnp.int32, (devs, LATS), 1).astype(F32)
    for rad in range(rads):
        table = [phi[done, lon, :, rad * LATS : (rad + 1) * LATS] for lon in range(LONS)]
        marks = maps[pl.ds(rad * 8 + 4, devs, stride=32), :]
        for slot in range(2):
            at = (slot * rads + rad) * devs
            row = marks if slot == 0 else pltpu.roll(marks, 64, axis=1)
            hot[at : at + devs, :] = jnp.where(row == slot_lane, 1.0, 0.0)
            for half in range(2):
                cell = maps[pl.ds(rad * 8 + 2 * slot + half, devs, stride=32), :].astype(jnp.int32)
                place, lon_at = cell & 127, cell >> 7
                value = jnp.zeros((devs, LATS), F32)
                for lon in range(LONS):
                    found = jnp.take_along_axis(
                        table[lon], place, axis=1, mode="promise_in_bounds"
                    )
                    value = jnp.where(lon_at == lon, found, value)
                picked[at : at + devs, 128 * half : 128 * half + 128] = value
    summed = lax.dot_general(
        hot[...],
        picked[...],
        (((0,), (0,)), ((), ())),
        precision=lax.Precision.HIGHEST,
        preferred_element_type=F32,
    )
    foot[...] = summed[:ROWS_OWN]


def shards(plasma_fields, velocity, resistivity, conductance, foot_map, foot_owner, foot_row):
    spot = jnp.stack([lax.axis_index("sec"), lax.axis_index("rad"), lax.axis_index("lon")])
    speeds = (
        jnp.concatenate([velocity, resistivity[None]], axis=0)
        .astype(F32)
        .reshape(4, SHELLS * LONS, LATS)
    )
    own = call(
        stage_body,
        arr(PLANES, LONS, SHELLS, LATS),
        (plasma_fields.reshape(FIELDS, SHELLS * LONS, LATS), speeds),
    )
    low = lax.ppermute(own, "lon", shift("lon", 1, True))
    high = lax.ppermute(own, "lon", shift("lon", -1, True))

    slots = call(
        slot_body,
        arr(128 * 8, 128),
        (foot_owner.reshape(1, -1), foot_row.reshape(1, -1), foot_map),
    )
    maps = lax.all_to_all(
        slots.reshape(128, 8, 128), ("lon", "rad"), split_axis=0, concat_axis=0, tiled=True
    )

    edges = call(edge_body, arr(PLANES, SHELLS, LATS), (low, own, high))
    from_low = lax.ppermute(edges, "rad", shift("rad", 1, False))
    from_high = lax.ppermute(edges, "rad", shift("rad", -1, False))
    blocks = (low, own, high, from_low, from_high)

    inner = call(
        inner_body,
        arr(48, LATS),
        (spot,) + blocks + (conductance,),
        scratch=(pltpu.VMEM((16, LATS), F32),),
        smem=(0,),
    )
    inner = lax.psum(inner, ("sec", "rad"))
    planes = lax.all_to_all(
        jnp.broadcast_to(inner[None], (32, 48, LATS)),
        "lon",
        split_axis=0,
        concat_axis=0,
        tiled=True,
    )

    up, down = call(pack_body, (arr(PLANES, 32, LATS), arr(PLANES, 32, LATS)), blocks)
    below = lax.ppermute(up, "sec", shift("sec", 1, False))
    above = lax.ppermute(down, "sec", shift("sec", -1, False))
    advanced = call(
        main_body,
        arr(FIELDS, SHELLS * LONS, LATS),
        blocks + (above, below),
        scratch=(
            pltpu.VMEM((2, WIDE, TALL, 2 * LATS), F32),
            pltpu.VMEM((7, WIDE, TALL, 2 * LATS), F32),
            pltpu.VMEM((4, WIDE, TALL, 2 * LATS), F32),
            pltpu.VMEM((TALL, LATS), F32),
        ),
    ).reshape(FIELDS, SHELLS, LONS, LATS)

    plane = pltpu.VMEM((LONS, 32, 4 * LATS), F32)
    potential, foot_table = call(
        final_body,
        (arr(LONS, LATS), arr(ROWS_OWN, 256)),
        (spot, planes.reshape(32 * 48, LATS), maps.reshape(128 * 8, 128)),
        scratch=(
            pltpu.VMEM((2, LONS, 32, 4 * LATS), F32),
            plane,
            plane,
            plane,
            plane,
            plane,
            pltpu.VMEM((256, 256), F32),
            pltpu.VMEM((256, 128), F32),
        ),
        smem=(0,),
    )
    return (advanced, potential, foot_table)


def solution(mesh):
    in_specs = (
        P(None, "sec", "lon", "rad"),
        P(None, "sec", "lon", "rad"),
        P("sec", "lon", "rad"),
        P("lon", "rad"),
        P(("lon", "sec", "rad"), None),
        P(("lon", "sec", "rad"), None),
        P(("lon", "sec", "rad")),
    )
    out_specs = (P(None, "sec", "lon", "rad"), P("lon", "rad"), P(("lon", "sec", "rad"), None))
    return jax.shard_map(shards, mesh=mesh, in_specs=in_specs, out_specs=out_specs, check_vma=False)
```

```python
import jax
import jax.numpy as jnp
from jax import lax
from jax.experimental import pallas as pl
from jax.experimental.pallas import tpu as pltpu
from jax.sharding import PartitionSpec as P

PHASES = 4
SWEEPS = 8
ROWS_OWN = 32
COURANT = 0.25
DAMPING = 0.05
RELAX = 0.8

FIELDS = 8
PLANES = FIELDS + 4
SHELLS = 16
LONS = 4
LATS = 128
WIDE = 3 * LONS
JOINED = 72
TALL = SHELLS + 2 * PHASES
F32 = jnp.float32


def call(body, out_shape, args, scratch=(), smem=(), flops=10**6, traffic=10**6):
    specs = [
        pl.BlockSpec(memory_space=pltpu.SMEM if i in smem else pltpu.VMEM)
        for i in range(len(args))
    ]
    many = isinstance(out_shape, (tuple, list))
    vmem = pl.BlockSpec(memory_space=pltpu.VMEM)
    return pl.pallas_call(
        body,
        out_shape=out_shape,
        in_specs=specs,
        out_specs=[vmem] * len(out_shape) if many else vmem,
        scratch_shapes=list(scratch),
        compiler_params=pltpu.CompilerParams(vmem_limit_bytes=40 * 2**20),
        cost_estimate=pl.CostEstimate(flops=flops, bytes_accessed=traffic, transcendentals=0),
    )(*args)


def arr(*shape):
    return jax.ShapeDtypeStruct(shape, F32)


def shift(axis, step, closed):
    count = lax.axis_size(axis)
    return [
        (i, (i + step) % count) for i in range(count) if closed or 0 <= i + step < count
    ]


def stage_body(fields, speeds, out):
    for plane in range(PLANES):
        for lon in range(LONS):
            rows = pl.ds(lon, SHELLS, stride=LONS)
            if plane < FIELDS:
                out[plane, lon] = fields[plane, rows, :]
            else:
                out[plane, lon] = speeds[plane - FIELDS, rows, :]


def edge_body(low, own, high, out):
    group = lax.broadcasted_iota(jnp.int32, (SHELLS, LATS), 1) // 8
    for plane in range(PLANES):
        packed = jnp.zeros((SHELLS, LATS), F32)
        for wide in range(1, WIDE - 1):
            ref = (low, own, high)[wide // LONS]
            turned = pltpu.roll(ref[plane, wide % LONS], 8 * wide + 4, axis=1)
            packed = jnp.where(group == wide, turned, packed)
        out[plane] = packed


def halo_lanes(edges, wide):
    lane = lax.broadcasted_iota(jnp.int32, edges.shape, 1)
    turned = pltpu.roll(edges, (LATS - 8 * wide - 4) % LATS, axis=1)
    return jnp.where((lane < 4) | (lane >= LATS - 4), turned, 0.0)


def weights(speeds, resist):
    out = []
    total = None
    for speed in speeds:
        lower = COURANT * jnp.maximum(speed, 0.0) + resist
        upper = resist - COURANT * jnp.minimum(speed, 0.0)
        out += [lower, upper]
        total = lower + upper if total is None else total + lower + upper
    return [1.0 - total] + out


def blend(w, centre, shell_lo, shell_hi, lon_lo, lon_hi, lat_lo, lat_hi):
    return (
        w[0] * centre
        + (w[1] * shell_lo + w[2] * shell_hi)
        + (w[3] * lon_lo + w[4] * lon_hi)
        + (w[5] * lat_lo + w[6] * lat_hi)
    )


def inner_body(low, own, high, from_low, from_high, conductance, out, rows):
    lane = lax.broadcasted_iota(jnp.int32, (8, LATS), 1)
    bottom = lax.broadcasted_iota(jnp.int32, (8, 2 * LATS), 0) == 0

    def plane_of(plane):
        edges = jnp.where(lane % 8 < 4, from_low[plane, :8, :], from_high[plane, :8, :])
        made = []
        for wide in range(WIDE):
            ref = (low, own, high)[wide // LONS]
            if 0 < wide < WIDE - 1:
                tail = halo_lanes(edges, wide)
            else:
                tail = jnp.zeros((8, LATS), F32)
            made.append(jnp.concatenate([ref[plane, wide % LONS, :8, :], tail], axis=1))
        return made

    speeds = [plane_of(FIELDS + d) for d in range(4)]
    w = [None] + [
        weights([speeds[d][wide] for d in range(3)], speeds[3][wide])
        for wide in range(1, WIDE - 1)
    ]
    for part in range(2):
        cells = plane_of(5 + part)
        for phase in range(PHASES):
            fresh = list(cells)
            for wide in range(phase + 1, WIDE - 1 - phase):
                c = cells[wide]
                fresh[wide] = blend(
                    w[wide],
                    c,
                    jnp.where(bottom, 0.0, pltpu.roll(c, 1, axis=0)),
                    pltpu.roll(c, 7, axis=0),
                    cells[wide - 1],
                    cells[wide + 1],
                    pltpu.roll(c, 1, axis=1),
                    pltpu.roll(c, 2 * LATS - 1, axis=1),
                )
            cells = fresh
        for lon in range(LONS):
            row = part * LONS + lon
            rows[row : row + 1, :] = cells[LONS + lon][0:1, :LATS]
    rows[8:12, :] = conductance[...]
    rows[12:16, :] = jnp.zeros((4, LATS), F32)
    mine = rows[...]
    for block in range(16):
        out[block * 16 : block * 16 + 16, :] = mine


def join_body(planes, maps, out):
    for rad in range(4):
        for row in range(12):
            line = jnp.broadcast_to(planes[rad * 16 + row : rad * 16 + row + 1, :], (32, LATS))
            out[pl.ds(rad * 12 + row, 32, stride=JOINED), :] = line
        for row in range(5):
            at = (rad * 5 + row) * 32
            out[pl.ds(48 + rad * 5 + row, 32, stride=JOINED), :] = maps[at : at + 32, :]
    for spare in range(68, JOINED):
        out[pl.ds(spare, 32, stride=JOINED), :] = jnp.zeros((32, LATS), F32)


def chunks():
    found = []
    at = 0
    for wide in range(1, WIDE - 1):
        far = max(LONS - wide, wide - 2 * LONS + 1, 0)
        count = PHASES - far
        found.append((wide, at, count))
        at += count
    return found, at


def pack_body(low, own, high, from_low, from_high, up, down):
    found, at = chunks()
    lane = lax.broadcasted_iota(jnp.int32, (8, LATS), 1)
    for plane in range(PLANES):
        for wide, start, count in found:
            ref = (low, own, high)[wide // LONS]
            up[plane, start : start + count, :] = ref[plane, wide % LONS, SHELLS - count :, :]
            down[plane, start : start + count, :] = ref[plane, wide % LONS, :count, :]
        first = jnp.where(lane % 8 < 4, from_low[plane, :8, :], from_high[plane, :8, :])
        last = jnp.where(lane % 8 < 4, from_low[plane, 8:, :], from_high[plane, 8:, :])
        up[plane, at : at + 4, :] = last[4:]
        down[plane, at : at + 4, :] = first[:4]


def main_body(low, own, high, from_low, from_high, above, below, out, cells, w, speeds, edges):
    found, at = chunks()
    lane = lax.broadcasted_iota(jnp.int32, (SHELLS, LATS), 1)

    def fill(plane, target):
        edges[:SHELLS, :] = jnp.where(lane % 8 < 4, from_low[plane], from_high[plane])
        edges[SHELLS : SHELLS + 4, :] = above[plane, at : at + 4, :]
        edges[SHELLS + 4 :, :] = below[plane, at : at + 4, :]
        strip = edges[...]
        for wide in range(WIDE):
            ref = (low, own, high)[wide // LONS]
            target[wide, :SHELLS, :LATS] = ref[plane, wide % LONS]
            target[wide, SHELLS:, :LATS] = jnp.zeros((8, LATS), F32)
            if 0 < wide < WIDE - 1:
                target[wide, :, LATS:] = halo_lanes(strip, wide)
            else:
                target[wide, :, LATS:] = jnp.zeros((TALL, LATS), F32)
        for wide, start, count in found:
            target[wide, SHELLS : SHELLS + count, :LATS] = above[plane, start : start + count, :]
            target[wide, TALL - count :, :LATS] = below[plane, start : start + count, :]

    for d in range(4):
        fill(FIELDS + d, speeds.at[d])
    for wide in range(1, WIDE - 1):
        made = weights([speeds[d, wide] for d in range(3)], speeds[3, wide])
        for i in range(7):
            w[i, wide] = made[i]

    def one(field, carry):
        fill(field, cells.at[0])
        for phase in range(PHASES):
            old = cells.at[phase % 2]
            new = cells.at[(phase + 1) % 2]
            for wide in range(phase + 1, WIDE - 1 - phase):
                c = old[wide]
                made = blend(
                    [w[i, wide] for i in range(7)],
                    c,
                    pltpu.roll(c, 1, axis=0),
                    pltpu.roll(c, TALL - 1, axis=0),
                    old[wide - 1],
                    old[wide + 1],
                    pltpu.roll(c, 1, axis=1),
                    pltpu.roll(c, 2 * LATS - 1, axis=1),
                )
                if phase == PHASES - 1:
                    out[field, pl.ds(wide - LONS, SHELLS, stride=LONS), :] = made[:SHELLS, :LATS]
                else:
                    new[wide] = made
        return carry

    lax.fori_loop(0, FIELDS, one, 0)


def slot_body(owners, rows, maps, out):
    count = owners.shape[1]
    here = lax.broadcasted_iota(jnp.int32, (count, count), 0)
    there = lax.broadcasted_iota(jnp.int32, (count, count), 1)
    aimed = (here % 32) * 4 + here // 32 == owners[...]
    earlier = jnp.dot(
        aimed.astype(jnp.bfloat16), (here < there).astype(jnp.bfloat16), preferred_element_type=F32
    )
    cell = maps[...]
    small = (cell & 127).astype(F32).astype(jnp.bfloat16)
    large = (cell >> 7).astype(F32).astype(jnp.bfloat16)
    row = (rows[...] + 1).astype(F32)
    marks = []
    lines = []
    for slot in range(2):
        chosen = jnp.where(aimed & (earlier == float(slot)), 1.0, 0.0)
        marks.append(jnp.sum(chosen * row, axis=1, keepdims=True) - 1.0)
        pick = chosen.astype(jnp.bfloat16)
        made = jnp.dot(pick, small, preferred_element_type=F32) + 128.0 * jnp.dot(
            pick, large, preferred_element_type=F32
        )
        lines += [made[:, :128], made[:, 128:]]
    lines.append(jnp.where(there < 64, marks[0], marks[1]))
    for rad in range(4):
        for j in range(5):
            out[(rad * 5 + j) * 32 : (rad * 5 + j) * 32 + 32, :] = lines[j][rad * 32 : rad * 32 + 32]


def final_body(spot, planes, pot, foot, phi, east_w, west_w, north_w, south_w, start, picked, hot):
    devs, rads = 32, 4
    wide = rads * LATS
    lane = lax.broadcasted_iota(jnp.int32, (devs, wide), 1)

    def gather(part):
        return [
            jnp.concatenate(
                [
                    planes[pl.ds(rad * 12 + part * LONS + lon, devs, stride=JOINED), :]
                    for rad in range(rads)
                ],
                axis=1,
            )
            for lon in range(LONS)
        ]

    def lon_up(values, lon):
        return values[lon + 1] if lon < LONS - 1 else pltpu.roll(values[0], devs - 1, axis=0)

    def lon_down(values, lon):
        return values[lon - 1] if lon > 0 else pltpu.roll(values[LONS - 1], 1, axis=0)

    def lat_up(value):
        return pltpu.roll(value, wide - 1, axis=1)

    def lat_down(value):
        return pltpu.roll(value, 1, axis=1)

    blon, blat, cond = gather(0), gather(1), gather(2)
    last, first = lane == wide - 1, lane == 0
    for lon in range(LONS):
        source = (
            lon_up(blat, lon)
            - lon_down(blat, lon)
            - (
                jnp.where(last, 0.0, lat_up(blon[lon]))
                - jnp.where(first, 0.0, lat_down(blon[lon]))
            )
        )
        c = cond[lon]
        east = 0.5 * (c + lon_up(cond, lon))
        west = 0.5 * (c + lon_down(cond, lon))
        north = 0.5 * (c + jnp.where(last, 0.0, lat_up(c)))
        south = 0.5 * (c + jnp.where(first, 0.0, lat_down(c)))
        scale = RELAX / (DAMPING * c + east + west + north + south)
        east_w[lon] = east * scale
        west_w[lon] = west * scale
        north_w[lon] = jnp.where(last, 0.0, north * scale)
        south_w[lon] = jnp.where(first, 0.0, south * scale)
        start[lon] = source * scale
        phi[0, lon] = source * scale

    def sweep(old, new):
        values = [phi[old, lon] for lon in range(LONS)]
        for lon in range(LONS):
            c = values[lon]
            phi[new, lon] = (
                (1.0 - RELAX) * c
                + start[lon]
                + (east_w[lon] * lon_up(values, lon) + west_w[lon] * lon_down(values, lon))
                + (north_w[lon] * lat_up(c) + south_w[lon] * lat_down(c))
            )

    for turn in range(SWEEPS - 1):
        sweep(turn % 2, (turn + 1) % 2)
    done = (SWEEPS - 1) % 2
    at_lon = lax.broadcasted_iota(jnp.int32, (devs, LATS), 0) == spot[2]
    for rad in range(rads):

        @pl.when(spot[1] == rad)
        def _():
            for lon in range(LONS):
                block = phi[done, lon, :, rad * LATS : (rad + 1) * LATS]
                pot[lon : lon + 1, :] = jnp.sum(
                    jnp.where(at_lon, block, 0.0), axis=0, keepdims=True
                )

    slot_lane = lax.broadcasted_iota(jnp.int32, (devs, LATS), 1).astype(F32)
    for rad in range(rads):
        table = [phi[done, lon, :, rad * LATS : (rad + 1) * LATS] for lon in range(LONS)]
        marks = planes[pl.ds(48 + rad * 5 + 4, devs, stride=JOINED), :]
        for slot in range(2):
            at = (slot * rads + rad) * devs
            row = marks if slot == 0 else pltpu.roll(marks, 64, axis=1)
            hot[at : at + devs, :] = jnp.where(row == slot_lane, 1.0, 0.0)
            for half in range(2):
                cell = planes[
                    pl.ds(48 + rad * 5 + 2 * slot + half, devs, stride=JOINED), :
                ].astype(jnp.int32)
                place, lon_at = cell & 127, cell >> 7
                value = jnp.zeros((devs, LATS), F32)
                for lon in range(LONS):
                    found = jnp.take_along_axis(
                        table[lon], place, axis=1, mode="promise_in_bounds"
                    )
                    value = jnp.where(lon_at == lon, found, value)
                picked[at : at + devs, 128 * half : 128 * half + 128] = value
    summed = lax.dot_general(
        hot[...],
        picked[...],
        (((0,), (0,)), ((), ())),
        precision=lax.Precision.HIGHEST,
        preferred_element_type=F32,
    )
    foot[...] = summed[:ROWS_OWN]


def shards(plasma_fields, velocity, resistivity, conductance, foot_map, foot_owner, foot_row):
    spot = jnp.stack([lax.axis_index("sec"), lax.axis_index("rad"), lax.axis_index("lon")])
    speeds = (
        jnp.concatenate([velocity, resistivity[None]], axis=0)
        .astype(F32)
        .reshape(4, SHELLS * LONS, LATS)
    )
    own = call(
        stage_body,
        arr(PLANES, LONS, SHELLS, LATS),
        (plasma_fields.reshape(FIELDS, SHELLS * LONS, LATS), speeds),
    )
    low = lax.ppermute(own, "lon", shift("lon", 1, True))
    high = lax.ppermute(own, "lon", shift("lon", -1, True))

    slots = call(
        slot_body,
        arr(4 * 160, LATS),
        (foot_owner.reshape(1, -1), foot_row.reshape(1, -1), foot_map),
    )
    maps = lax.all_to_all(
        slots.reshape(4, 160, LATS), "rad", split_axis=0, concat_axis=0, tiled=True
    )

    edges = call(edge_body, arr(PLANES, SHELLS, LATS), (low, own, high))
    from_low = lax.ppermute(edges, "rad", shift("rad", 1, False))
    from_high = lax.ppermute(edges, "rad", shift("rad", -1, False))
    blocks = (low, own, high, from_low, from_high)

    inner = call(
        inner_body,
        arr(256, LATS),
        blocks + (conductance,),
        scratch=(pltpu.VMEM((16, LATS), F32),),
    )
    inner = lax.all_to_all(
        inner.reshape(16, 16, LATS), ("sec", "rad"), split_axis=0, concat_axis=0, tiled=True
    )
    joined = call(
        join_body, arr(32 * JOINED, LATS), (inner.reshape(256, LATS), maps.reshape(640, LATS))
    )
    planes = lax.all_to_all(
        joined.reshape(32, JOINED, LATS), "lon", split_axis=0, concat_axis=0, tiled=True
    )

    up, down = call(pack_body, (arr(PLANES, 32, LATS), arr(PLANES, 32, LATS)), blocks)
    below = lax.ppermute(up, "sec", shift("sec", 1, False))
    above = lax.ppermute(down, "sec", shift("sec", -1, False))
    advanced = call(
        main_body,
        arr(FIELDS, SHELLS * LONS, LATS),
        blocks + (above, below),
        scratch=(
            pltpu.VMEM((2, WIDE, TALL, 2 * LATS), F32),
            pltpu.VMEM((7, WIDE, TALL, 2 * LATS), F32),
            pltpu.VMEM((4, WIDE, TALL, 2 * LATS), F32),
            pltpu.VMEM((TALL, LATS), F32),
        ),
    ).reshape(FIELDS, SHELLS, LONS, LATS)

    plane = pltpu.VMEM((LONS, 32, 4 * LATS), F32)
    potential, foot_table = call(
        final_body,
        (arr(LONS, LATS), arr(ROWS_OWN, 256)),
        (spot, planes.reshape(32 * JOINED, LATS)),
        scratch=(
            pltpu.VMEM((2, LONS, 32, 4 * LATS), F32),
            plane,
            plane,
            plane,
            plane,
            plane,
            pltpu.VMEM((256, 256), F32),
            pltpu.VMEM((256, 128), F32),
        ),
        smem=(0,),
    )
    return (advanced, potential, foot_table)


def solution(mesh):
    in_specs = (
        P(None, "sec", "lon", "rad"),
        P(None, "sec", "lon", "rad"),
        P("sec", "lon", "rad"),
        P("lon", "rad"),
        P(("lon", "sec", "rad"), None),
        P(("lon", "sec", "rad"), None),
        P(("lon", "sec", "rad")),
    )
    out_specs = (P(None, "sec", "lon", "rad"), P("lon", "rad"), P(("lon", "sec", "rad"), None))
    return jax.shard_map(shards, mesh=mesh, in_specs=in_specs, out_specs=out_specs, check_vma=False)
```

```python
import jax
import jax.numpy as jnp
from jax import lax
from jax.experimental import pallas as pl
from jax.experimental.pallas import tpu as pltpu
from jax.sharding import PartitionSpec as P

PHASES = 4
SWEEPS = 8
ROWS_OWN = 32
COURANT = 0.25
DAMPING = 0.05
RELAX = 0.8

FIELDS = 8
PLANES = FIELDS + 4
SHELLS = 16
LONS = 4
LATS = 128
WIDE = 3 * LONS
EARLY = 40
LATE = 24
SENT = 168
TALL = SHELLS + 2 * PHASES
F32 = jnp.float32


def call(body, out_shape, args, scratch=(), smem=(), flops=10**6, traffic=10**6):
    specs = [
        pl.BlockSpec(memory_space=pltpu.SMEM if i in smem else pltpu.VMEM)
        for i in range(len(args))
    ]
    many = isinstance(out_shape, (tuple, list))
    vmem = pl.BlockSpec(memory_space=pltpu.VMEM)
    return pl.pallas_call(
        body,
        out_shape=out_shape,
        in_specs=specs,
        out_specs=[vmem] * len(out_shape) if many else vmem,
        scratch_shapes=list(scratch),
        compiler_params=pltpu.CompilerParams(vmem_limit_bytes=40 * 2**20),
        cost_estimate=pl.CostEstimate(flops=flops, bytes_accessed=traffic, transcendentals=0),
    )(*args)


def arr(*shape):
    return jax.ShapeDtypeStruct(shape, F32)


def shift(axis, step, closed):
    count = lax.axis_size(axis)
    return [
        (i, (i + step) % count) for i in range(count) if closed or 0 <= i + step < count
    ]


def stage_body(fields, speeds, out):
    for plane in range(PLANES):
        for lon in range(LONS):
            rows = pl.ds(lon, SHELLS, stride=LONS)
            if plane < FIELDS:
                out[plane, lon] = fields[plane, rows, :]
            else:
                out[plane, lon] = speeds[plane - FIELDS, rows, :]


def edge_body(low, own, high, out):
    group = lax.broadcasted_iota(jnp.int32, (SHELLS, LATS), 1) // 8
    for plane in range(PLANES):
        packed = jnp.zeros((SHELLS, LATS), F32)
        for wide in range(1, WIDE - 1):
            ref = (low, own, high)[wide // LONS]
            turned = pltpu.roll(ref[plane, wide % LONS], 8 * wide + 4, axis=1)
            packed = jnp.where(group == wide, turned, packed)
        out[plane] = packed


def halo_lanes(edges, wide):
    lane = lax.broadcasted_iota(jnp.int32, edges.shape, 1)
    turned = pltpu.roll(edges, (LATS - 8 * wide - 4) % LATS, axis=1)
    return jnp.where((lane < 4) | (lane >= LATS - 4), turned, 0.0)


def weights(speeds, resist):
    out = []
    total = None
    for speed in speeds:
        lower = COURANT * jnp.maximum(speed, 0.0) + resist
        upper = resist - COURANT * jnp.minimum(speed, 0.0)
        out += [lower, upper]
        total = lower + upper if total is None else total + lower + upper
    return [1.0 - total] + out


def blend(w, centre, shell_lo, shell_hi, lon_lo, lon_hi, lat_lo, lat_hi):
    return (
        w[0] * centre
        + (w[1] * shell_lo + w[2] * shell_hi)
        + (w[3] * lon_lo + w[4] * lon_hi)
        + (w[5] * lat_lo + w[6] * lat_hi)
    )


def inner_body(low, own, high, from_low, from_high, out):
    lane = lax.broadcasted_iota(jnp.int32, (8, LATS), 1)
    bottom = lax.broadcasted_iota(jnp.int32, (8, 2 * LATS), 0) == 0

    def plane_of(plane):
        edges = jnp.where(lane % 8 < 4, from_low[plane, :8, :], from_high[plane, :8, :])
        made = []
        for wide in range(WIDE):
            ref = (low, own, high)[wide // LONS]
            if 0 < wide < WIDE - 1:
                tail = halo_lanes(edges, wide)
            else:
                tail = jnp.zeros((8, LATS), F32)
            made.append(jnp.concatenate([ref[plane, wide % LONS, :8, :], tail], axis=1))
        return made

    speeds = [plane_of(FIELDS + d) for d in range(4)]
    w = [None] + [
        weights([speeds[d][wide] for d in range(3)], speeds[3][wide])
        for wide in range(1, WIDE - 1)
    ]
    for part in range(2):
        cells = plane_of(5 + part)
        for phase in range(PHASES):
            fresh = list(cells)
            for wide in range(phase + 1, WIDE - 1 - phase):
                c = cells[wide]
                fresh[wide] = blend(
                    w[wide],
                    c,
                    jnp.where(bottom, 0.0, pltpu.roll(c, 1, axis=0)),
                    pltpu.roll(c, 7, axis=0),
                    cells[wide - 1],
                    cells[wide + 1],
                    pltpu.roll(c, 1, axis=1),
                    pltpu.roll(c, 2 * LATS - 1, axis=1),
                )
            cells = fresh
        for lon in range(LONS):
            row = part * LONS + lon
            out[row : row + 1, :] = cells[LONS + lon][0:1, :LATS]


def early_body(sent, out):
    for rad in range(4):
        for row in range(5):
            at = rad * SENT + row * 32
            out[pl.ds(rad * 5 + row, 32, stride=EARLY), :] = sent[at : at + 32, :]
        for lon in range(LONS):
            line = sent[rad * SENT + 160 + lon : rad * SENT + 161 + lon, :]
            out[pl.ds(20 + rad * 4 + lon, 32, stride=EARLY), :] = jnp.broadcast_to(line, (32, LATS))
    for spare in range(36, EARLY):
        out[pl.ds(spare, 32, stride=EARLY), :] = jnp.zeros((32, LATS), F32)


def late_body(planes, out, block):
    wide = 4 * LATS
    lane = lax.broadcasted_iota(jnp.int32, (LONS, wide), 1)
    lon = lax.broadcasted_iota(jnp.int32, (LONS, wide), 0)
    blon = jnp.concatenate([planes[r * 8 : r * 8 + 4, :] for r in range(4)], axis=1)
    blat = jnp.concatenate([planes[r * 8 + 4 : r * 8 + 8, :] for r in range(4)], axis=1)
    upper = jnp.concatenate([blat[1:], blat[:1]], axis=0)
    lower = jnp.concatenate([blat[3:], blat[:3]], axis=0)
    north = jnp.where(lane == wide - 1, 0.0, pltpu.roll(blon, wide - 1, axis=1))
    south = jnp.where(lane == 0, 0.0, pltpu.roll(blon, 1, axis=1))
    source = (
        jnp.where(lon == LONS - 1, 0.0, upper) - jnp.where(lon == 0, 0.0, lower) - (north - south)
    )
    for rad in range(4):
        part = slice(rad * LATS, (rad + 1) * LATS)
        block[rad * 4 : rad * 4 + 4, :] = source[:, part]
        block[16 + rad : 17 + rad, :] = blat[0:1, part]
        block[20 + rad : 21 + rad, :] = blat[3:4, part]
    mine = block[...]
    for owner in range(32):
        out[owner * LATE : owner * LATE + LATE, :] = mine


def chunks():
    found = []
    at = 0
    for wide in range(1, WIDE - 1):
        far = max(LONS - wide, wide - 2 * LONS + 1, 0)
        count = PHASES - far
        found.append((wide, at, count))
        at += count
    return found, at


def pack_body(low, own, high, from_low, from_high, up, down):
    found, at = chunks()
    lane = lax.broadcasted_iota(jnp.int32, (8, LATS), 1)
    for plane in range(PLANES):
        for wide, start, count in found:
            ref = (low, own, high)[wide // LONS]
            up[plane, start : start + count, :] = ref[plane, wide % LONS, SHELLS - count :, :]
            down[plane, start : start + count, :] = ref[plane, wide % LONS, :count, :]
        first = jnp.where(lane % 8 < 4, from_low[plane, :8, :], from_high[plane, :8, :])
        last = jnp.where(lane % 8 < 4, from_low[plane, 8:, :], from_high[plane, 8:, :])
        up[plane, at : at + 4, :] = last[4:]
        down[plane, at : at + 4, :] = first[:4]


def main_body(low, own, high, from_low, from_high, above, below, out, cells, w, speeds, edges):
    found, at = chunks()
    lane = lax.broadcasted_iota(jnp.int32, (SHELLS, LATS), 1)

    def fill(plane, target):
        edges[:SHELLS, :] = jnp.where(lane % 8 < 4, from_low[plane], from_high[plane])
        edges[SHELLS : SHELLS + 4, :] = above[plane, at : at + 4, :]
        edges[SHELLS + 4 :, :] = below[plane, at : at + 4, :]
        strip = edges[...]
        for wide in range(WIDE):
            ref = (low, own, high)[wide // LONS]
            target[wide, :SHELLS, :LATS] = ref[plane, wide % LONS]
            target[wide, SHELLS:, :LATS] = jnp.zeros((8, LATS), F32)
            if 0 < wide < WIDE - 1:
                target[wide, :, LATS:] = halo_lanes(strip, wide)
            else:
                target[wide, :, LATS:] = jnp.zeros((TALL, LATS), F32)
        for wide, start, count in found:
            target[wide, SHELLS : SHELLS + count, :LATS] = above[plane, start : start + count, :]
            target[wide, TALL - count :, :LATS] = below[plane, start : start + count, :]

    for d in range(4):
        fill(FIELDS + d, speeds.at[d])
    for wide in range(1, WIDE - 1):
        made = weights([speeds[d, wide] for d in range(3)], speeds[3, wide])
        for i in range(7):
            w[i, wide] = made[i]

    def one(field, carry):
        fill(field, cells.at[0])
        for phase in range(PHASES):
            old = cells.at[phase % 2]
            new = cells.at[(phase + 1) % 2]
            for wide in range(phase + 1, WIDE - 1 - phase):
                c = old[wide]
                made = blend(
                    [w[i, wide] for i in range(7)],
                    c,
                    pltpu.roll(c, 1, axis=0),
                    pltpu.roll(c, TALL - 1, axis=0),
                    old[wide - 1],
                    old[wide + 1],
                    pltpu.roll(c, 1, axis=1),
                    pltpu.roll(c, 2 * LATS - 1, axis=1),
                )
                if phase == PHASES - 1:
                    out[field, pl.ds(wide - LONS, SHELLS, stride=LONS), :] = made[:SHELLS, :LATS]
                else:
                    new[wide] = made
        return carry

    lax.fori_loop(0, FIELDS, one, 0)


def slot_body(owners, rows, maps, conductance, out):
    count = owners.shape[1]
    here = lax.broadcasted_iota(jnp.int32, (count, count), 0)
    there = lax.broadcasted_iota(jnp.int32, (count, count), 1)
    aimed = (here % 32) * 4 + here // 32 == owners[...]
    earlier = jnp.dot(
        aimed.astype(jnp.bfloat16), (here < there).astype(jnp.bfloat16), preferred_element_type=F32
    )
    cell = maps[...]
    small = (cell & 127).astype(F32).astype(jnp.bfloat16)
    large = (cell >> 7).astype(F32).astype(jnp.bfloat16)
    row = (rows[...] + 1).astype(F32)
    marks = []
    lines = []
    for slot in range(2):
        chosen = jnp.where(aimed & (earlier == float(slot)), 1.0, 0.0)
        marks.append(jnp.sum(chosen * row, axis=1, keepdims=True) - 1.0)
        pick = chosen.astype(jnp.bfloat16)
        made = jnp.dot(pick, small, preferred_element_type=F32) + 128.0 * jnp.dot(
            pick, large, preferred_element_type=F32
        )
        lines += [made[:, :128], made[:, 128:]]
    lines.append(jnp.where(there < 64, marks[0], marks[1]))
    for rad in range(4):
        for j in range(5):
            at = rad * SENT + j * 32
            out[at : at + 32, :] = lines[j][rad * 32 : rad * 32 + 32]
        at = rad * SENT + 160
        out[at : at + 4, :] = conductance[...]
        out[at + 4 : at + 8, :] = jnp.zeros((4, LATS), F32)


def final_body(spot, early, late, pot, foot, phi, east_w, west_w, north_w, south_w, start, picked, hot):
    devs, rads = 32, 4
    wide = rads * LATS
    lane = lax.broadcasted_iota(jnp.int32, (devs, wide), 1)

    def gather(ref, at, step, stride):
        return jnp.concatenate(
            [ref[pl.ds(at + rad * step, devs, stride=stride), :] for rad in range(rads)], axis=1
        )

    def lon_up(values, lon):
        return values[lon + 1] if lon < LONS - 1 else pltpu.roll(values[0], devs - 1, axis=0)

    def lon_down(values, lon):
        return values[lon - 1] if lon > 0 else pltpu.roll(values[LONS - 1], 1, axis=0)

    def lat_up(value):
        return pltpu.roll(value, wide - 1, axis=1)

    def lat_down(value):
        return pltpu.roll(value, 1, axis=1)

    cond = [gather(early, 20 + lon, 4, EARLY) for lon in range(LONS)]
    sources = [gather(late, lon, 4, LATE) for lon in range(LONS)]
    sources[LONS - 1] += pltpu.roll(gather(late, 16, 1, LATE), devs - 1, axis=0)
    sources[0] -= pltpu.roll(gather(late, 20, 1, LATE), 1, axis=0)
    last, first = lane == wide - 1, lane == 0
    for lon in range(LONS):
        source = sources[lon]
        c = cond[lon]
        east = 0.5 * (c + lon_up(cond, lon))
        west = 0.5 * (c + lon_down(cond, lon))
        north = 0.5 * (c + jnp.where(last, 0.0, lat_up(c)))
        south = 0.5 * (c + jnp.where(first, 0.0, lat_down(c)))
        scale = RELAX / (DAMPING * c + east + west + north + south)
        east_w[lon] = east * scale
        west_w[lon] = west * scale
        north_w[lon] = jnp.where(last, 0.0, north * scale)
        south_w[lon] = jnp.where(first, 0.0, south * scale)
        start[lon] = source * scale
        phi[0, lon] = source * scale

    def sweep(old, new):
        values = [phi[old, lon] for lon in range(LONS)]
        for lon in range(LONS):
            c = values[lon]
            phi[new, lon] = (
                (1.0 - RELAX) * c
                + start[lon]
                + (east_w[lon] * lon_up(values, lon) + west_w[lon] * lon_down(values, lon))
                + (north_w[lon] * lat_up(c) + south_w[lon] * lat_down(c))
            )

    for turn in range(SWEEPS - 1):
        sweep(turn % 2, (turn + 1) % 2)
    done = (SWEEPS - 1) % 2
    at_lon = lax.broadcasted_iota(jnp.int32, (devs, LATS), 0) == spot[2]
    for rad in range(rads):

        @pl.when(spot[1] == rad)
        def _():
            for lon in range(LONS):
                block = phi[done, lon, :, rad * LATS : (rad + 1) * LATS]
                pot[lon : lon + 1, :] = jnp.sum(
                    jnp.where(at_lon, block, 0.0), axis=0, keepdims=True
                )

    slot_lane = lax.broadcasted_iota(jnp.int32, (devs, LATS), 1).astype(F32)
    for rad in range(rads):
        table = [phi[done, lon, :, rad * LATS : (rad + 1) * LATS] for lon in range(LONS)]
        marks = early[pl.ds(rad * 5 + 4, devs, stride=EARLY), :]
        for slot in range(2):
            at = (slot * rads + rad) * devs
            row = marks if slot == 0 else pltpu.roll(marks, 64, axis=1)
            hot[at : at + devs, :] = jnp.where(row == slot_lane, 1.0, 0.0)
            for half in range(2):
                cell = early[pl.ds(rad * 5 + 2 * slot + half, devs, stride=EARLY), :].astype(jnp.int32)
                place, lon_at = cell & 127, cell >> 7
                value = jnp.zeros((devs, LATS), F32)
                for lon in range(LONS):
                    found = jnp.take_along_axis(
                        table[lon], place, axis=1, mode="promise_in_bounds"
                    )
                    value = jnp.where(lon_at == lon, found, value)
                picked[at : at + devs, 128 * half : 128 * half + 128] = value
    summed = lax.dot_general(
        hot[...],
        picked[...],
        (((0,), (0,)), ((), ())),
        precision=lax.Precision.HIGHEST,
        preferred_element_type=F32,
    )
    foot[...] = summed[:ROWS_OWN]


def shards(plasma_fields, velocity, resistivity, conductance, foot_map, foot_owner, foot_row):
    spot = jnp.stack([lax.axis_index("sec"), lax.axis_index("rad"), lax.axis_index("lon")])
    speeds = (
        jnp.concatenate([velocity, resistivity[None]], axis=0)
        .astype(F32)
        .reshape(4, SHELLS * LONS, LATS)
    )
    own = call(
        stage_body,
        arr(PLANES, LONS, SHELLS, LATS),
        (plasma_fields.reshape(FIELDS, SHELLS * LONS, LATS), speeds),
    )
    low = lax.ppermute(own, "lon", shift("lon", 1, True))
    high = lax.ppermute(own, "lon", shift("lon", -1, True))

    slots = call(
        slot_body,
        arr(4 * SENT, LATS),
        (foot_owner.reshape(1, -1), foot_row.reshape(1, -1), foot_map, conductance),
    )
    sent = lax.all_to_all(
        slots.reshape(4, SENT, LATS), "rad", split_axis=0, concat_axis=0, tiled=True
    )

    low, high, sent = lax.optimization_barrier((low, high, sent))
    edges = call(edge_body, arr(PLANES, SHELLS, LATS), (low, own, high))
    early = call(early_body, arr(32 * EARLY, LATS), (sent.reshape(4 * SENT, LATS),))
    edges, early = lax.optimization_barrier((edges, early))
    early = lax.all_to_all(
        early.reshape(32, EARLY, LATS), "lon", split_axis=0, concat_axis=0, tiled=True
    )
    from_low = lax.ppermute(edges, "rad", shift("rad", 1, False))
    from_high = lax.ppermute(edges, "rad", shift("rad", -1, False))
    blocks = (low, own, high, from_low, from_high)

    inner = call(inner_body, arr(8, LATS), blocks)
    copies = [lax.ppermute(inner, "sec", [(0, sec)]) for sec in range(1, 4)]
    inner = jnp.where(lax.axis_index("sec") == 0, inner, copies[0] + copies[1] + copies[2])
    inner = lax.all_gather(inner, "rad")
    up, down = call(pack_body, (arr(PLANES, 32, LATS), arr(PLANES, 32, LATS)), blocks)

    late = call(
        late_body,
        arr(32 * LATE, LATS),
        (inner.reshape(32, LATS),),
        scratch=(pltpu.VMEM((LATE, LATS), F32),),
    )
    late, early, up, down = lax.optimization_barrier((late, early, up, down))
    below = lax.ppermute(up, "sec", shift("sec", 1, False))
    above = lax.ppermute(down, "sec", shift("sec", -1, False))
    late = lax.all_to_all(
        late.reshape(32, LATE, LATS), "lon", split_axis=0, concat_axis=0, tiled=True
    )

    advanced = call(
        main_body,
        arr(FIELDS, SHELLS * LONS, LATS),
        blocks + (above, below),
        scratch=(
            pltpu.VMEM((2, WIDE, TALL, 2 * LATS), F32),
            pltpu.VMEM((7, WIDE, TALL, 2 * LATS), F32),
            pltpu.VMEM((4, WIDE, TALL, 2 * LATS), F32),
            pltpu.VMEM((TALL, LATS), F32),
        ),
    ).reshape(FIELDS, SHELLS, LONS, LATS)

    plane = pltpu.VMEM((LONS, 32, 4 * LATS), F32)
    potential, foot_table = call(
        final_body,
        (arr(LONS, LATS), arr(ROWS_OWN, 256)),
        (spot, early.reshape(32 * EARLY, LATS), late.reshape(32 * LATE, LATS)),
        scratch=(
            pltpu.VMEM((2, LONS, 32, 4 * LATS), F32),
            plane,
            plane,
            plane,
            plane,
            plane,
            pltpu.VMEM((256, 256), F32),
            pltpu.VMEM((256, 128), F32),
        ),
        smem=(0,),
    )
    return (advanced, potential, foot_table)


def solution(mesh):
    in_specs = (
        P(None, "sec", "lon", "rad"),
        P(None, "sec", "lon", "rad"),
        P("sec", "lon", "rad"),
        P("lon", "rad"),
        P(("lon", "sec", "rad"), None),
        P(("lon", "sec", "rad"), None),
        P(("lon", "sec", "rad")),
    )
    out_specs = (P(None, "sec", "lon", "rad"), P("lon", "rad"), P(("lon", "sec", "rad"), None))
    return jax.shard_map(shards, mesh=mesh, in_specs=in_specs, out_specs=out_specs, check_vma=False)
```

```python
import jax
import jax.numpy as jnp
from jax import lax
from jax.experimental import pallas as pl
from jax.experimental.pallas import tpu as pltpu
from jax.sharding import PartitionSpec as P

PHASES = 4
SWEEPS = 8
ROWS_OWN = 32
COURANT = 0.25
DAMPING = 0.05
RELAX = 0.8

FIELDS = 8
PLANES = FIELDS + 4
SHELLS = 16
LONS = 4
LATS = 128
WIDE = 3 * LONS
LATE = 64
RAW = 192
SENT = 168
TALL = SHELLS + 2 * PHASES
F32 = jnp.float32


def call(body, out_shape, args, scratch=(), smem=(), flops=10**6, traffic=10**6):
    specs = [
        pl.BlockSpec(memory_space=pltpu.SMEM if i in smem else pltpu.VMEM)
        for i in range(len(args))
    ]
    many = isinstance(out_shape, (tuple, list))
    vmem = pl.BlockSpec(memory_space=pltpu.VMEM)
    return pl.pallas_call(
        body,
        out_shape=out_shape,
        in_specs=specs,
        out_specs=[vmem] * len(out_shape) if many else vmem,
        scratch_shapes=list(scratch),
        compiler_params=pltpu.CompilerParams(vmem_limit_bytes=40 * 2**20),
        cost_estimate=pl.CostEstimate(flops=flops, bytes_accessed=traffic, transcendentals=0),
    )(*args)


def arr(*shape):
    return jax.ShapeDtypeStruct(shape, F32)


def shift(axis, step, closed):
    count = lax.axis_size(axis)
    return [
        (i, (i + step) % count) for i in range(count) if closed or 0 <= i + step < count
    ]


def stage_body(fields, speeds, out):
    for plane in range(PLANES):
        for lon in range(LONS):
            rows = pl.ds(lon, SHELLS, stride=LONS)
            if plane < FIELDS:
                out[plane, lon] = fields[plane, rows, :]
            else:
                out[plane, lon] = speeds[plane - FIELDS, rows, :]


def edge_body(low, own, high, out):
    group = lax.broadcasted_iota(jnp.int32, (SHELLS, LATS), 1) // 8
    for plane in range(PLANES):
        packed = jnp.zeros((SHELLS, LATS), F32)
        for wide in range(1, WIDE - 1):
            ref = (low, own, high)[wide // LONS]
            turned = pltpu.roll(ref[plane, wide % LONS], 8 * wide + 4, axis=1)
            packed = jnp.where(group == wide, turned, packed)
        out[plane] = packed


def halo_lanes(edges, wide):
    lane = lax.broadcasted_iota(jnp.int32, edges.shape, 1)
    turned = pltpu.roll(edges, (LATS - 8 * wide - 4) % LATS, axis=1)
    return jnp.where((lane < 4) | (lane >= LATS - 4), turned, 0.0)


def weights(speeds, resist):
    out = []
    total = None
    for speed in speeds:
        lower = COURANT * jnp.maximum(speed, 0.0) + resist
        upper = resist - COURANT * jnp.minimum(speed, 0.0)
        out += [lower, upper]
        total = lower + upper if total is None else total + lower + upper
    return [1.0 - total] + out


def blend(w, centre, shell_lo, shell_hi, lon_lo, lon_hi, lat_lo, lat_hi):
    return (
        w[0] * centre
        + (w[1] * shell_lo + w[2] * shell_hi)
        + (w[3] * lon_lo + w[4] * lon_hi)
        + (w[5] * lat_lo + w[6] * lat_hi)
    )


def raw_chunks():
    found = []
    at = 0
    for plane in (5, 6, 8, 9, 10, 11):
        reach = PHASES + 1 if plane < FIELDS else PHASES
        for wide in range(WIDE):
            count = reach - max(LONS - wide, wide - 2 * LONS + 1, 0)
            if count > 0:
                found.append((plane, wide, at, count))
                at += count
    return found


def raw_body(low, own, high, out):
    for plane, wide, at, count in raw_chunks():
        ref = (low, own, high)[wide // LONS]
        out[at : at + count, :] = ref[plane, wide % LONS, :count, :]


def inner_body(raw, out, cells):
    span = 4 * LATS
    lane = lax.broadcasted_iota(jnp.int32, (8, span), 1)
    bottom = lax.broadcasted_iota(jnp.int32, (8, span), 0) == 0
    first, last = lane == 0, lane == span - 1
    cells[...] = jnp.zeros(cells.shape, F32)
    order = (5, 6, 8, 9, 10, 11)
    for plane, wide, at, count in raw_chunks():
        for rad in range(4):
            cells[order.index(plane), wide, :count, rad * LATS : (rad + 1) * LATS] = raw[
                rad * RAW + at : rad * RAW + at + count, :
            ]
    w = [None] + [
        weights([cells[2 + d, wide] for d in range(3)], cells[5, wide])
        for wide in range(1, WIDE - 1)
    ]
    made = []
    for part in range(2):
        now = [cells[part, wide] for wide in range(WIDE)]
        for phase in range(PHASES):
            fresh = list(now)
            for wide in range(phase + 1, WIDE - 1 - phase):
                c = now[wide]
                fresh[wide] = blend(
                    w[wide],
                    c,
                    jnp.where(bottom, 0.0, pltpu.roll(c, 1, axis=0)),
                    pltpu.roll(c, 7, axis=0),
                    now[wide - 1],
                    now[wide + 1],
                    jnp.where(first, 0.0, pltpu.roll(c, 1, axis=1)),
                    jnp.where(last, 0.0, pltpu.roll(c, span - 1, axis=1)),
                )
            now = fresh
        made.append(now[LONS : 2 * LONS])
    blon, blat = made
    for lon in range(LONS):
        c = blon[lon]
        source = jnp.where(first, 0.0, pltpu.roll(c, 1, axis=1)) - jnp.where(
            last, 0.0, pltpu.roll(c, span - 1, axis=1)
        )
        if lon < LONS - 1:
            source = source + blat[lon + 1]
        if lon > 0:
            source = source - blat[lon - 1]
        for rad in range(4):
            part = slice(rad * LATS, (rad + 1) * LATS)
            out[rad * 4 + lon : rad * 4 + lon + 1, :] = source[0:1, part]
            if lon == 0:
                out[16 + rad : 17 + rad, :] = blat[0][0:1, part]
            if lon == LONS - 1:
                out[20 + rad : 21 + rad, :] = blat[LONS - 1][0:1, part]


def join_body(spot, own, one, two, three, sent, out):
    source = jnp.where(spot[0] == 0, own[...], one[...] + two[...] + three[...])
    for owner in range(32):
        out[owner * LATE : owner * LATE + 24, :] = source
    for rad in range(4):
        for lon in range(LONS):
            line = sent[rad * SENT + 160 + lon : rad * SENT + 161 + lon, :]
            out[pl.ds(24 + rad * 4 + lon, 32, stride=LATE), :] = jnp.broadcast_to(line, (32, LATS))
        for row in range(5):
            at = rad * SENT + row * 32
            out[pl.ds(40 + rad * 5 + row, 32, stride=LATE), :] = sent[at : at + 32, :]
    for spare in range(60, LATE):
        out[pl.ds(spare, 32, stride=LATE), :] = jnp.zeros((32, LATS), F32)


def chunks():
    found = []
    at = 0
    for wide in range(1, WIDE - 1):
        far = max(LONS - wide, wide - 2 * LONS + 1, 0)
        count = PHASES - far
        found.append((wide, at, count))
        at += count
    return found, at


def pack_body(low, own, high, from_low, from_high, up, down):
    found, at = chunks()
    lane = lax.broadcasted_iota(jnp.int32, (8, LATS), 1)
    for plane in range(PLANES):
        for wide, start, count in found:
            ref = (low, own, high)[wide // LONS]
            up[plane, start : start + count, :] = ref[plane, wide % LONS, SHELLS - count :, :]
            down[plane, start : start + count, :] = ref[plane, wide % LONS, :count, :]
        first = jnp.where(lane % 8 < 4, from_low[plane, :8, :], from_high[plane, :8, :])
        last = jnp.where(lane % 8 < 4, from_low[plane, 8:, :], from_high[plane, 8:, :])
        up[plane, at : at + 4, :] = last[4:]
        down[plane, at : at + 4, :] = first[:4]


def main_body(low, own, high, from_low, from_high, above, below, out, cells, w, speeds, edges):
    found, at = chunks()
    lane = lax.broadcasted_iota(jnp.int32, (SHELLS, LATS), 1)

    def fill(plane, target):
        edges[:SHELLS, :] = jnp.where(lane % 8 < 4, from_low[plane], from_high[plane])
        edges[SHELLS : SHELLS + 4, :] = above[plane, at : at + 4, :]
        edges[SHELLS + 4 :, :] = below[plane, at : at + 4, :]
        strip = edges[...]
        for wide in range(WIDE):
            ref = (low, own, high)[wide // LONS]
            target[wide, :SHELLS, :LATS] = ref[plane, wide % LONS]
            target[wide, SHELLS:, :LATS] = jnp.zeros((8, LATS), F32)
            if 0 < wide < WIDE - 1:
                target[wide, :, LATS:] = halo_lanes(strip, wide)
            else:
                target[wide, :, LATS:] = jnp.zeros((TALL, LATS), F32)
        for wide, start, count in found:
            target[wide, SHELLS : SHELLS + count, :LATS] = above[plane, start : start + count, :]
            target[wide, TALL - count :, :LATS] = below[plane, start : start + count, :]

    for d in range(4):
        fill(FIELDS + d, speeds.at[d])
    for wide in range(1, WIDE - 1):
        made = weights([speeds[d, wide] for d in range(3)], speeds[3, wide])
        for i in range(7):
            w[i, wide] = made[i]

    def one(field, carry):
        fill(field, cells.at[0])
        for phase in range(PHASES):
            old = cells.at[phase % 2]
            new = cells.at[(phase + 1) % 2]
            for wide in range(phase + 1, WIDE - 1 - phase):
                c = old[wide]
                made = blend(
                    [w[i, wide] for i in range(7)],
                    c,
                    pltpu.roll(c, 1, axis=0),
                    pltpu.roll(c, TALL - 1, axis=0),
                    old[wide - 1],
                    old[wide + 1],
                    pltpu.roll(c, 1, axis=1),
                    pltpu.roll(c, 2 * LATS - 1, axis=1),
                )
                if phase == PHASES - 1:
                    out[field, pl.ds(wide - LONS, SHELLS, stride=LONS), :] = made[:SHELLS, :LATS]
                else:
                    new[wide] = made
        return carry

    lax.fori_loop(0, FIELDS, one, 0)


def slot_body(owners, rows, maps, conductance, out):
    count = owners.shape[1]
    here = lax.broadcasted_iota(jnp.int32, (count, count), 0)
    there = lax.broadcasted_iota(jnp.int32, (count, count), 1)
    aimed = (here % 32) * 4 + here // 32 == owners[...]
    earlier = jnp.dot(
        aimed.astype(jnp.bfloat16), (here < there).astype(jnp.bfloat16), preferred_element_type=F32
    )
    cell = maps[...]
    small = (cell & 127).astype(F32).astype(jnp.bfloat16)
    large = (cell >> 7).astype(F32).astype(jnp.bfloat16)
    row = (rows[...] + 1).astype(F32)
    marks = []
    lines = []
    for slot in range(2):
        chosen = jnp.where(aimed & (earlier == float(slot)), 1.0, 0.0)
        marks.append(jnp.sum(chosen * row, axis=1, keepdims=True) - 1.0)
        pick = chosen.astype(jnp.bfloat16)
        made = jnp.dot(pick, small, preferred_element_type=F32) + 128.0 * jnp.dot(
            pick, large, preferred_element_type=F32
        )
        lines += [made[:, :128], made[:, 128:]]
    lines.append(jnp.where(there < 64, marks[0], marks[1]))
    for rad in range(4):
        for j in range(5):
            at = rad * SENT + j * 32
            out[at : at + 32, :] = lines[j][rad * 32 : rad * 32 + 32]
        at = rad * SENT + 160
        out[at : at + 4, :] = conductance[...]
        out[at + 4 : at + 8, :] = jnp.zeros((4, LATS), F32)


def final_body(spot, late, pot, foot, phi, east_w, west_w, north_w, south_w, start, picked, hot):
    devs, rads = 32, 4
    wide = rads * LATS
    lane = lax.broadcasted_iota(jnp.int32, (devs, wide), 1)

    def gather(ref, at, step, stride):
        return jnp.concatenate(
            [ref[pl.ds(at + rad * step, devs, stride=stride), :] for rad in range(rads)], axis=1
        )

    def lon_up(values, lon):
        return values[lon + 1] if lon < LONS - 1 else pltpu.roll(values[0], devs - 1, axis=0)

    def lon_down(values, lon):
        return values[lon - 1] if lon > 0 else pltpu.roll(values[LONS - 1], 1, axis=0)

    def lat_up(value):
        return pltpu.roll(value, wide - 1, axis=1)

    def lat_down(value):
        return pltpu.roll(value, 1, axis=1)

    cond = [gather(late, 24 + lon, 4, LATE) for lon in range(LONS)]
    sources = [gather(late, lon, 4, LATE) for lon in range(LONS)]
    sources[LONS - 1] += pltpu.roll(gather(late, 16, 1, LATE), devs - 1, axis=0)
    sources[0] -= pltpu.roll(gather(late, 20, 1, LATE), 1, axis=0)
    last, first = lane == wide - 1, lane == 0
    for lon in range(LONS):
        source = sources[lon]
        c = cond[lon]
        east = 0.5 * (c + lon_up(cond, lon))
        west = 0.5 * (c + lon_down(cond, lon))
        north = 0.5 * (c + jnp.where(last, 0.0, lat_up(c)))
        south = 0.5 * (c + jnp.where(first, 0.0, lat_down(c)))
        scale = RELAX / (DAMPING * c + east + west + north + south)
        east_w[lon] = east * scale
        west_w[lon] = west * scale
        north_w[lon] = jnp.where(last, 0.0, north * scale)
        south_w[lon] = jnp.where(first, 0.0, south * scale)
        start[lon] = source * scale
        phi[0, lon] = source * scale

    def sweep(old, new):
        values = [phi[old, lon] for lon in range(LONS)]
        for lon in range(LONS):
            c = values[lon]
            phi[new, lon] = (
                (1.0 - RELAX) * c
                + start[lon]
                + (east_w[lon] * lon_up(values, lon) + west_w[lon] * lon_down(values, lon))
                + (north_w[lon] * lat_up(c) + south_w[lon] * lat_down(c))
            )

    for turn in range(SWEEPS - 1):
        sweep(turn % 2, (turn + 1) % 2)
    done = (SWEEPS - 1) % 2
    at_lon = lax.broadcasted_iota(jnp.int32, (devs, LATS), 0) == spot[2]
    for rad in range(rads):

        @pl.when(spot[1] == rad)
        def _():
            for lon in range(LONS):
                block = phi[done, lon, :, rad * LATS : (rad + 1) * LATS]
                pot[lon : lon + 1, :] = jnp.sum(
                    jnp.where(at_lon, block, 0.0), axis=0, keepdims=True
                )

    slot_lane = lax.broadcasted_iota(jnp.int32, (devs, LATS), 1).astype(F32)
    for rad in range(rads):
        table = [phi[done, lon, :, rad * LATS : (rad + 1) * LATS] for lon in range(LONS)]
        marks = late[pl.ds(40 + rad * 5 + 4, devs, stride=LATE), :]
        for slot in range(2):
            at = (slot * rads + rad) * devs
            row = marks if slot == 0 else pltpu.roll(marks, 64, axis=1)
            hot[at : at + devs, :] = jnp.where(row == slot_lane, 1.0, 0.0)
            for half in range(2):
                cell = late[pl.ds(40 + rad * 5 + 2 * slot + half, devs, stride=LATE), :].astype(jnp.int32)
                place, lon_at = cell & 127, cell >> 7
                value = jnp.zeros((devs, LATS), F32)
                for lon in range(LONS):
                    found = jnp.take_along_axis(
                        table[lon], place, axis=1, mode="promise_in_bounds"
                    )
                    value = jnp.where(lon_at == lon, found, value)
                picked[at : at + devs, 128 * half : 128 * half + 128] = value
    summed = lax.dot_general(
        hot[...],
        picked[...],
        (((0,), (0,)), ((), ())),
        precision=lax.Precision.HIGHEST,
        preferred_element_type=F32,
    )
    foot[...] = summed[:ROWS_OWN]


def shards(plasma_fields, velocity, resistivity, conductance, foot_map, foot_owner, foot_row):
    spot = jnp.stack([lax.axis_index("sec"), lax.axis_index("rad"), lax.axis_index("lon")])
    speeds = (
        jnp.concatenate([velocity, resistivity[None]], axis=0)
        .astype(F32)
        .reshape(4, SHELLS * LONS, LATS)
    )
    own = call(
        stage_body,
        arr(PLANES, LONS, SHELLS, LATS),
        (plasma_fields.reshape(FIELDS, SHELLS * LONS, LATS), speeds),
    )
    low = lax.ppermute(own, "lon", shift("lon", 1, True))
    high = lax.ppermute(own, "lon", shift("lon", -1, True))

    slots = call(
        slot_body,
        arr(4 * SENT, LATS),
        (foot_owner.reshape(1, -1), foot_row.reshape(1, -1), foot_map, conductance),
    )
    sent = lax.all_to_all(
        slots.reshape(4, SENT, LATS), "rad", split_axis=0, concat_axis=0, tiled=True
    )

    low, high, sent = lax.optimization_barrier((low, high, sent))
    raw = call(raw_body, arr(RAW, LATS), (low, own, high))
    raw = lax.all_gather(raw, "rad")
    inner = call(
        inner_body,
        arr(24, LATS),
        (raw.reshape(4 * RAW, LATS),),
        scratch=(pltpu.VMEM((6, WIDE, 8, 4 * LATS), F32),),
    )
    copies = [lax.ppermute(inner, "sec", [(0, sec)]) for sec in range(1, 4)]
    late = call(
        join_body,
        arr(32 * LATE, LATS),
        (spot, inner, *copies, sent.reshape(4 * SENT, LATS)),
        smem=(0,),
    )
    late, low, high = lax.optimization_barrier((late, low, high))

    edges = call(edge_body, arr(PLANES, SHELLS, LATS), (low, own, high))
    from_low = lax.ppermute(edges, "rad", shift("rad", 1, False))
    from_high = lax.ppermute(edges, "rad", shift("rad", -1, False))
    blocks = (low, own, high, from_low, from_high)
    up, down = call(pack_body, (arr(PLANES, 32, LATS), arr(PLANES, 32, LATS)), blocks)
    below = lax.ppermute(up, "sec", shift("sec", 1, False))
    above = lax.ppermute(down, "sec", shift("sec", -1, False))
    late = lax.all_to_all(
        late.reshape(32, LATE, LATS), "lon", split_axis=0, concat_axis=0, tiled=True
    )

    advanced = call(
        main_body,
        arr(FIELDS, SHELLS * LONS, LATS),
        blocks + (above, below),
        scratch=(
            pltpu.VMEM((2, WIDE, TALL, 2 * LATS), F32),
            pltpu.VMEM((7, WIDE, TALL, 2 * LATS), F32),
            pltpu.VMEM((4, WIDE, TALL, 2 * LATS), F32),
            pltpu.VMEM((TALL, LATS), F32),
        ),
    ).reshape(FIELDS, SHELLS, LONS, LATS)

    plane = pltpu.VMEM((LONS, 32, 4 * LATS), F32)
    potential, foot_table = call(
        final_body,
        (arr(LONS, LATS), arr(ROWS_OWN, 256)),
        (spot, late.reshape(32 * LATE, LATS)),
        scratch=(
            pltpu.VMEM((2, LONS, 32, 4 * LATS), F32),
            plane,
            plane,
            plane,
            plane,
            plane,
            pltpu.VMEM((256, 256), F32),
            pltpu.VMEM((256, 128), F32),
        ),
        smem=(0,),
    )
    return (advanced, potential, foot_table)


def solution(mesh):
    in_specs = (
        P(None, "sec", "lon", "rad"),
        P(None, "sec", "lon", "rad"),
        P("sec", "lon", "rad"),
        P("lon", "rad"),
        P(("lon", "sec", "rad"), None),
        P(("lon", "sec", "rad"), None),
        P(("lon", "sec", "rad")),
    )
    out_specs = (P(None, "sec", "lon", "rad"), P("lon", "rad"), P(("lon", "sec", "rad"), None))
    return jax.shard_map(shards, mesh=mesh, in_specs=in_specs, out_specs=out_specs, check_vma=False)
```

```python
import jax
import jax.numpy as jnp
from jax import lax
from jax.experimental import pallas as pl
from jax.experimental.pallas import tpu as pltpu
from jax.sharding import PartitionSpec as P

PHASES = 4
SWEEPS = 8
ROWS_OWN = 32
COURANT = 0.25
DAMPING = 0.05
RELAX = 0.8

FIELDS = 8
PLANES = FIELDS + 4
SHELLS = 16
LONS = 4
LATS = 128
WIDE = 3 * LONS
LATE = 64
RAW = 192
SENT = 168
TALL = SHELLS + 2 * PHASES
F32 = jnp.float32


def call(body, out_shape, args, scratch=(), smem=(), flops=10**6, traffic=10**6):
    specs = [
        pl.BlockSpec(memory_space=pltpu.SMEM if i in smem else pltpu.VMEM)
        for i in range(len(args))
    ]
    many = isinstance(out_shape, (tuple, list))
    vmem = pl.BlockSpec(memory_space=pltpu.VMEM)
    return pl.pallas_call(
        body,
        out_shape=out_shape,
        in_specs=specs,
        out_specs=[vmem] * len(out_shape) if many else vmem,
        scratch_shapes=list(scratch),
        compiler_params=pltpu.CompilerParams(vmem_limit_bytes=16 * 2**20),
        cost_estimate=pl.CostEstimate(flops=flops, bytes_accessed=traffic, transcendentals=0),
    )(*args)


def arr(*shape):
    return jax.ShapeDtypeStruct(shape, F32)


def shift(axis, step, closed):
    count = lax.axis_size(axis)
    return [
        (i, (i + step) % count) for i in range(count) if closed or 0 <= i + step < count
    ]


def stage_body(fields, speeds, out):
    for plane in range(PLANES):
        for lon in range(LONS):
            rows = pl.ds(lon, SHELLS, stride=LONS)
            if plane < FIELDS:
                out[plane, lon] = fields[plane, rows, :]
            else:
                out[plane, lon] = speeds[plane - FIELDS, rows, :]


def edge_body(low, own, high, above, below, edges, tall):
    found, _ = chunks()
    group = lax.broadcasted_iota(jnp.int32, (TALL, LATS), 1) // 8
    for plane in range(PLANES):
        for wide in range(WIDE):
            ref = (low, own, high)[wide // LONS]
            tall[plane, wide, :SHELLS, :] = ref[plane, wide % LONS]
            tall[plane, wide, SHELLS:, :] = jnp.zeros((TALL - SHELLS, LATS), F32)
        for wide, start, count in found:
            tall[plane, wide, SHELLS : SHELLS + count, :] = above[plane, start : start + count, :]
            tall[plane, wide, TALL - count :, :] = below[plane, start : start + count, :]
    for plane in range(PLANES):
        packed = jnp.zeros((TALL, LATS), F32)
        for wide in range(1, WIDE - 1):
            turned = pltpu.roll(tall[plane, wide], 8 * wide + 4, axis=1)
            packed = jnp.where(group == wide, turned, packed)
        edges[plane] = packed


def halo_lanes(edges, wide):
    lane = lax.broadcasted_iota(jnp.int32, edges.shape, 1)
    turned = pltpu.roll(edges, (LATS - 8 * wide - 4) % LATS, axis=1)
    return jnp.where((lane < 4) | (lane >= LATS - 4), turned, 0.0)


def weights(speeds, resist):
    out = []
    total = None
    for speed in speeds:
        lower = COURANT * jnp.maximum(speed, 0.0) + resist
        upper = resist - COURANT * jnp.minimum(speed, 0.0)
        out += [lower, upper]
        total = lower + upper if total is None else total + lower + upper
    return [1.0 - total] + out


def blend(w, centre, shell_lo, shell_hi, lon_lo, lon_hi, lat_lo, lat_hi):
    return (
        w[0] * centre
        + (w[1] * shell_lo + w[2] * shell_hi)
        + (w[3] * lon_lo + w[4] * lon_hi)
        + (w[5] * lat_lo + w[6] * lat_hi)
    )


def raw_chunks():
    found = []
    at = 0
    for plane in (5, 6, 8, 9, 10, 11):
        reach = PHASES + 1 if plane < FIELDS else PHASES
        for wide in range(WIDE):
            count = reach - max(LONS - wide, wide - 2 * LONS + 1, 0)
            if count > 0:
                found.append((plane, wide, at, count))
                at += count
    return found


def raw_body(low, own, high, out):
    for plane, wide, at, count in raw_chunks():
        ref = (low, own, high)[wide // LONS]
        out[at : at + count, :] = ref[plane, wide % LONS, :count, :]


def inner_body(raw, out, cells):
    span = 4 * LATS
    lane = lax.broadcasted_iota(jnp.int32, (8, span), 1)
    bottom = lax.broadcasted_iota(jnp.int32, (8, span), 0) == 0
    first, last = lane == 0, lane == span - 1
    cells[...] = jnp.zeros(cells.shape, F32)
    order = (5, 6, 8, 9, 10, 11)
    for plane, wide, at, count in raw_chunks():
        for rad in range(4):
            cells[order.index(plane), wide, :count, rad * LATS : (rad + 1) * LATS] = raw[
                rad * RAW + at : rad * RAW + at + count, :
            ]
    w = [None] + [
        weights([cells[2 + d, wide] for d in range(3)], cells[5, wide])
        for wide in range(1, WIDE - 1)
    ]
    made = []
    for part in range(2):
        now = [cells[part, wide] for wide in range(WIDE)]
        for phase in range(PHASES):
            fresh = list(now)
            for wide in range(phase + 1, WIDE - 1 - phase):
                c = now[wide]
                fresh[wide] = blend(
                    w[wide],
                    c,
                    jnp.where(bottom, 0.0, pltpu.roll(c, 1, axis=0)),
                    pltpu.roll(c, 7, axis=0),
                    now[wide - 1],
                    now[wide + 1],
                    jnp.where(first, 0.0, pltpu.roll(c, 1, axis=1)),
                    jnp.where(last, 0.0, pltpu.roll(c, span - 1, axis=1)),
                )
            now = fresh
        made.append(now[LONS : 2 * LONS])
    blon, blat = made
    for lon in range(LONS):
        c = blon[lon]
        source = jnp.where(first, 0.0, pltpu.roll(c, 1, axis=1)) - jnp.where(
            last, 0.0, pltpu.roll(c, span - 1, axis=1)
        )
        if lon < LONS - 1:
            source = source + blat[lon + 1]
        if lon > 0:
            source = source - blat[lon - 1]
        for rad in range(4):
            part = slice(rad * LATS, (rad + 1) * LATS)
            out[rad * 4 + lon : rad * 4 + lon + 1, :] = source[0:1, part]
            if lon == 0:
                out[16 + rad : 17 + rad, :] = blat[0][0:1, part]
            if lon == LONS - 1:
                out[20 + rad : 21 + rad, :] = blat[LONS - 1][0:1, part]


def base_body(sent, out):
    step = LATE - 24
    for rad in range(4):
        for lon in range(LONS):
            line = sent[rad * SENT + 160 + lon : rad * SENT + 161 + lon, :]
            out[pl.ds(rad * 4 + lon, 32, stride=step), :] = jnp.broadcast_to(line, (32, LATS))
        for row in range(5):
            at = rad * SENT + row * 32
            out[pl.ds(16 + rad * 5 + row, 32, stride=step), :] = sent[at : at + 32, :]
    for spare in range(36, step):
        out[pl.ds(spare, 32, stride=step), :] = jnp.zeros((32, LATS), F32)


def join_body(one, two, base, out, copies, sems):
    rest = pltpu.make_async_copy(base, out.at[:, pl.ds(24, LATE - 24), :], sems.at[0])
    rest.start()
    source = one[...] + two[...]
    for owner in range(32):
        copies[owner] = source
    move = pltpu.make_async_copy(copies, out.at[:, pl.ds(0, 24), :], sems.at[1])
    move.start()
    move.wait()
    rest.wait()


def join(one, two, base):
    vmem = pl.BlockSpec(memory_space=pltpu.VMEM)
    plain = pl.BlockSpec(memory_space=pl.ANY)
    return pl.pallas_call(
        join_body,
        out_shape=arr(32, LATE, LATS),
        in_specs=[vmem, vmem, plain],
        out_specs=plain,
        scratch_shapes=[pltpu.VMEM((32, 24, LATS), F32), pltpu.SemaphoreType.DMA((2,))],
        compiler_params=pltpu.CompilerParams(vmem_limit_bytes=4 * 2**20),
        cost_estimate=pl.CostEstimate(flops=10**5, bytes_accessed=10**6, transcendentals=0),
    )(one, two, base)


def chunks():
    found = []
    at = 0
    for wide in range(1, WIDE - 1):
        far = max(LONS - wide, wide - 2 * LONS + 1, 0)
        count = PHASES - far
        found.append((wide, at, count))
        at += count
    return found, at


def pack_body(low, own, high, up, down):
    found, rows = chunks()
    for plane in range(PLANES):
        for wide, start, count in found:
            ref = (low, own, high)[wide // LONS]
            up[plane, start : start + count, :] = ref[plane, wide % LONS, SHELLS - count :, :]
            down[plane, start : start + count, :] = ref[plane, wide % LONS, :count, :]
        up[plane, rows:, :] = jnp.zeros((32 - rows, LATS), F32)
        down[plane, rows:, :] = jnp.zeros((32 - rows, LATS), F32)


def main_body(low, own, high, above, below, from_low, from_high, out, cells, w, speeds):
    found, _ = chunks()
    lane = lax.broadcasted_iota(jnp.int32, (TALL, LATS), 1)

    def fill(plane, target):
        strip = jnp.where(lane % 8 < 4, from_low[plane], from_high[plane])
        for wide in range(WIDE):
            ref = (low, own, high)[wide // LONS]
            target[wide, :SHELLS, :LATS] = ref[plane, wide % LONS]
            target[wide, SHELLS:, :LATS] = jnp.zeros((TALL - SHELLS, LATS), F32)
            if 0 < wide < WIDE - 1:
                target[wide, :, LATS:] = halo_lanes(strip, wide)
            else:
                target[wide, :, LATS:] = jnp.zeros((TALL, LATS), F32)
        for wide, start, count in found:
            target[wide, SHELLS : SHELLS + count, :LATS] = above[plane, start : start + count, :]
            target[wide, TALL - count :, :LATS] = below[plane, start : start + count, :]

    for d in range(4):
        fill(FIELDS + d, speeds.at[d])
    for wide in range(1, WIDE - 1):
        made = weights([speeds[d, wide] for d in range(3)], speeds[3, wide])
        for i in range(7):
            w[i, wide] = made[i]

    def one(field, carry):
        fill(field, cells.at[0])
        for phase in range(PHASES):
            old = cells.at[phase % 2]
            new = cells.at[(phase + 1) % 2]
            for wide in range(phase + 1, WIDE - 1 - phase):
                c = old[wide]
                made = blend(
                    [w[i, wide] for i in range(7)],
                    c,
                    pltpu.roll(c, 1, axis=0),
                    pltpu.roll(c, TALL - 1, axis=0),
                    old[wide - 1],
                    old[wide + 1],
                    pltpu.roll(c, 1, axis=1),
                    pltpu.roll(c, 2 * LATS - 1, axis=1),
                )
                if phase == PHASES - 1:
                    out[field, pl.ds(wide - LONS, SHELLS, stride=LONS), :] = made[:SHELLS, :LATS]
                else:
                    new[wide] = made
        return carry

    lax.fori_loop(0, FIELDS, one, 0)


def slot_body(owners, rows, maps, conductance, out):
    count = owners.shape[1]
    here = lax.broadcasted_iota(jnp.int32, (count, count), 0)
    there = lax.broadcasted_iota(jnp.int32, (count, count), 1)
    aimed = (here % 32) * 4 + here // 32 == owners[...]
    earlier = jnp.dot(
        aimed.astype(jnp.bfloat16), (here < there).astype(jnp.bfloat16), preferred_element_type=F32
    )
    cell = maps[...]
    small = (cell & 127).astype(F32).astype(jnp.bfloat16)
    large = (cell >> 7).astype(F32).astype(jnp.bfloat16)
    row = (rows[...] + 1).astype(F32)
    marks = []
    lines = []
    for slot in range(2):
        chosen = jnp.where(aimed & (earlier == float(slot)), 1.0, 0.0)
        marks.append(jnp.sum(chosen * row, axis=1, keepdims=True) - 1.0)
        pick = chosen.astype(jnp.bfloat16)
        made = jnp.dot(pick, small, preferred_element_type=F32) + 128.0 * jnp.dot(
            pick, large, preferred_element_type=F32
        )
        lines += [made[:, :128], made[:, 128:]]
    lines.append(jnp.where(there < 64, marks[0], marks[1]))
    for rad in range(4):
        for j in range(5):
            at = rad * SENT + j * 32
            out[at : at + 32, :] = lines[j][rad * 32 : rad * 32 + 32]
        at = rad * SENT + 160
        out[at : at + 4, :] = conductance[...]
        out[at + 4 : at + 8, :] = jnp.zeros((4, LATS), F32)


def final_body(spot, late, pot, foot, phi, east_w, west_w, north_w, south_w, start, picked, hot):
    devs, rads = 32, 4
    wide = rads * LATS
    lane = lax.broadcasted_iota(jnp.int32, (devs, wide), 1)

    def gather(ref, at, step, stride):
        return jnp.concatenate(
            [ref[pl.ds(at + rad * step, devs, stride=stride), :] for rad in range(rads)], axis=1
        )

    def lon_up(values, lon):
        return values[lon + 1] if lon < LONS - 1 else pltpu.roll(values[0], devs - 1, axis=0)

    def lon_down(values, lon):
        return values[lon - 1] if lon > 0 else pltpu.roll(values[LONS - 1], 1, axis=0)

    def lat_up(value):
        return pltpu.roll(value, wide - 1, axis=1)

    def lat_down(value):
        return pltpu.roll(value, 1, axis=1)

    cond = [gather(late, 24 + lon, 4, LATE) for lon in range(LONS)]
    sources = [gather(late, lon, 4, LATE) for lon in range(LONS)]
    sources[LONS - 1] += pltpu.roll(gather(late, 16, 1, LATE), devs - 1, axis=0)
    sources[0] -= pltpu.roll(gather(late, 20, 1, LATE), 1, axis=0)
    last, first = lane == wide - 1, lane == 0
    for lon in range(LONS):
        source = sources[lon]
        c = cond[lon]
        east = 0.5 * (c + lon_up(cond, lon))
        west = 0.5 * (c + lon_down(cond, lon))
        north = 0.5 * (c + jnp.where(last, 0.0, lat_up(c)))
        south = 0.5 * (c + jnp.where(first, 0.0, lat_down(c)))
        scale = RELAX / (DAMPING * c + east + west + north + south)
        east_w[lon] = east * scale
        west_w[lon] = west * scale
        north_w[lon] = jnp.where(last, 0.0, north * scale)
        south_w[lon] = jnp.where(first, 0.0, south * scale)
        start[lon] = source * scale
        phi[0, lon] = source * scale

    def sweep(old, new):
        values = [phi[old, lon] for lon in range(LONS)]
        for lon in range(LONS):
            c = values[lon]
            phi[new, lon] = (
                (1.0 - RELAX) * c
                + start[lon]
                + (east_w[lon] * lon_up(values, lon) + west_w[lon] * lon_down(values, lon))
                + (north_w[lon] * lat_up(c) + south_w[lon] * lat_down(c))
            )

    for turn in range(SWEEPS - 1):
        sweep(turn % 2, (turn + 1) % 2)
    done = (SWEEPS - 1) % 2
    at_lon = lax.broadcasted_iota(jnp.int32, (devs, LATS), 0) == spot[2]
    for rad in range(rads):

        @pl.when(spot[1] == rad)
        def _():
            for lon in range(LONS):
                block = phi[done, lon, :, rad * LATS : (rad + 1) * LATS]
                pot[lon : lon + 1, :] = jnp.sum(
                    jnp.where(at_lon, block, 0.0), axis=0, keepdims=True
                )

    slot_lane = lax.broadcasted_iota(jnp.int32, (devs, LATS), 1).astype(F32)
    for rad in range(rads):
        table = [phi[done, lon, :, rad * LATS : (rad + 1) * LATS] for lon in range(LONS)]
        marks = late[pl.ds(40 + rad * 5 + 4, devs, stride=LATE), :]
        for slot in range(2):
            at = (slot * rads + rad) * devs
            row = marks if slot == 0 else pltpu.roll(marks, 64, axis=1)
            hot[at : at + devs, :] = jnp.where(row == slot_lane, 1.0, 0.0)
            for half in range(2):
                cell = late[pl.ds(40 + rad * 5 + 2 * slot + half, devs, stride=LATE), :].astype(jnp.int32)
                place, lon_at = cell & 127, cell >> 7
                value = jnp.zeros((devs, LATS), F32)
                for lon in range(LONS):
                    found = jnp.take_along_axis(
                        table[lon], place, axis=1, mode="promise_in_bounds"
                    )
                    value = jnp.where(lon_at == lon, found, value)
                picked[at : at + devs, 128 * half : 128 * half + 128] = value
    summed = lax.dot_general(
        hot[...],
        picked[...],
        (((0,), (0,)), ((), ())),
        precision=lax.Precision.HIGHEST,
        preferred_element_type=F32,
    )
    foot[...] = summed[:ROWS_OWN]


def shards(plasma_fields, velocity, resistivity, conductance, foot_map, foot_owner, foot_row):
    spot = jnp.stack([lax.axis_index("sec"), lax.axis_index("rad"), lax.axis_index("lon")])
    speeds = (
        jnp.concatenate([velocity, resistivity[None]], axis=0)
        .astype(F32)
        .reshape(4, SHELLS * LONS, LATS)
    )
    own = call(
        stage_body,
        arr(PLANES, LONS, SHELLS, LATS),
        (plasma_fields.reshape(FIELDS, SHELLS * LONS, LATS), speeds),
    )
    low = lax.ppermute(own, "lon", shift("lon", 1, True))
    high = lax.ppermute(own, "lon", shift("lon", -1, True))

    slots = call(
        slot_body,
        arr(4 * SENT, LATS),
        (foot_owner.reshape(1, -1), foot_row.reshape(1, -1), foot_map, conductance),
    )
    sent = lax.all_to_all(
        slots.reshape(4, SENT, LATS), "rad", split_axis=0, concat_axis=0, tiled=True
    )

    low, high, sent = lax.optimization_barrier((low, high, sent))
    up, down = call(pack_body, (arr(PLANES, 32, LATS), arr(PLANES, 32, LATS)), (low, own, high))
    below = lax.ppermute(up, "sec", shift("sec", 1, False))
    above = lax.ppermute(down, "sec", shift("sec", -1, False))
    raw = call(raw_body, arr(RAW, LATS), (low, own, high))
    raw = lax.all_gather(raw, "rad")
    raw, above, below = lax.optimization_barrier((raw, above, below))
    inner = call(
        inner_body,
        arr(24, LATS),
        (raw.reshape(4 * RAW, LATS),),
        scratch=(pltpu.VMEM((6, WIDE, 8, 4 * LATS), F32),),
    )
    far = lax.ppermute(inner, "sec", [(0, 3)])
    far = jnp.where(lax.axis_index("sec") == 0, inner, far)
    near = lax.ppermute(far, "sec", [(0, 1), (3, 2)])
    base = call(base_body, arr(32 * (LATE - 24), LATS), (sent.reshape(4 * SENT, LATS),))
    late = join(far, near, base.reshape(32, LATE - 24, LATS))
    late, low, high = lax.optimization_barrier((late, low, high))

    blocks = (low, own, high, above, below)
    edges = call(
        edge_body,
        arr(PLANES, TALL, LATS),
        blocks,
        scratch=(pltpu.VMEM((PLANES, WIDE, TALL, LATS), F32),),
    )
    from_low = lax.ppermute(edges, "rad", shift("rad", 1, False))
    from_high = lax.ppermute(edges, "rad", shift("rad", -1, False))
    late = lax.all_to_all(
        late, "lon", split_axis=0, concat_axis=0, tiled=True
    )

    advanced = call(
        main_body,
        arr(FIELDS, SHELLS * LONS, LATS),
        blocks + (from_low, from_high),
        scratch=(
            pltpu.VMEM((2, WIDE, TALL, 2 * LATS), F32),
            pltpu.VMEM((7, WIDE, TALL, 2 * LATS), F32),
            pltpu.VMEM((4, WIDE, TALL, 2 * LATS), F32),
        ),
    ).reshape(FIELDS, SHELLS, LONS, LATS)

    plane = pltpu.VMEM((LONS, 32, 4 * LATS), F32)
    potential, foot_table = call(
        final_body,
        (arr(LONS, LATS), arr(ROWS_OWN, 256)),
        (spot, late.reshape(32 * LATE, LATS)),
        scratch=(
            pltpu.VMEM((2, LONS, 32, 4 * LATS), F32),
            plane,
            plane,
            plane,
            plane,
            plane,
            pltpu.VMEM((256, 256), F32),
            pltpu.VMEM((256, 128), F32),
        ),
        smem=(0,),
    )
    return (advanced, potential, foot_table)


def solution(mesh):
    in_specs = (
        P(None, "sec", "lon", "rad"),
        P(None, "sec", "lon", "rad"),
        P("sec", "lon", "rad"),
        P("lon", "rad"),
        P(("lon", "sec", "rad"), None),
        P(("lon", "sec", "rad"), None),
        P(("lon", "sec", "rad")),
    )
    out_specs = (P(None, "sec", "lon", "rad"), P("lon", "rad"), P(("lon", "sec", "rad"), None))
    return jax.shard_map(shards, mesh=mesh, in_specs=in_specs, out_specs=out_specs, check_vma=False)
```

```python
import jax
import jax.numpy as jnp
from jax import lax
from jax.experimental import pallas as pl
from jax.experimental.pallas import tpu as pltpu
from jax.sharding import PartitionSpec as P

PHASES = 4
SWEEPS = 8
ROWS_OWN = 32
COURANT = 0.25
DAMPING = 0.05
RELAX = 0.8

FIELDS = 8
PLANES = FIELDS + 4
SHELLS = 16
LONS = 4
LATS = 128
WIDE = 3 * LONS
LATE = 40
HALF = 24
RAW = 192
SENT = 168
TALL = SHELLS + 2 * PHASES
F32 = jnp.float32


def call(body, out_shape, args, scratch=(), smem=(), flops=10**6, traffic=10**6):
    specs = [
        pl.BlockSpec(memory_space=pltpu.SMEM if i in smem else pltpu.VMEM)
        for i in range(len(args))
    ]
    many = isinstance(out_shape, (tuple, list))
    vmem = pl.BlockSpec(memory_space=pltpu.VMEM)
    return pl.pallas_call(
        body,
        out_shape=out_shape,
        in_specs=specs,
        out_specs=[vmem] * len(out_shape) if many else vmem,
        scratch_shapes=list(scratch),
        compiler_params=pltpu.CompilerParams(vmem_limit_bytes=16 * 2**20),
        cost_estimate=pl.CostEstimate(flops=flops, bytes_accessed=traffic, transcendentals=0),
    )(*args)


def arr(*shape):
    return jax.ShapeDtypeStruct(shape, F32)


def shift(axis, step, closed):
    count = lax.axis_size(axis)
    return [
        (i, (i + step) % count) for i in range(count) if closed or 0 <= i + step < count
    ]


def stage_body(fields, speeds, out):
    for plane in range(PLANES):
        for lon in range(LONS):
            rows = pl.ds(lon, SHELLS, stride=LONS)
            if plane < FIELDS:
                out[plane, lon] = fields[plane, rows, :]
            else:
                out[plane, lon] = speeds[plane - FIELDS, rows, :]


def edge_body(low, own, high, above, below, edges, tall):
    found, _ = chunks()
    group = lax.broadcasted_iota(jnp.int32, (TALL, LATS), 1) // 8
    for plane in range(PLANES):
        for wide in range(WIDE):
            ref = (low, own, high)[wide // LONS]
            tall[plane, wide, :SHELLS, :] = ref[plane, wide % LONS]
            tall[plane, wide, SHELLS:, :] = jnp.zeros((TALL - SHELLS, LATS), F32)
        for wide, start, count in found:
            tall[plane, wide, SHELLS : SHELLS + count, :] = above[plane, start : start + count, :]
            tall[plane, wide, TALL - count :, :] = below[plane, start : start + count, :]
    for plane in range(PLANES):
        packed = jnp.zeros((TALL, LATS), F32)
        for wide in range(1, WIDE - 1):
            turned = pltpu.roll(tall[plane, wide], 8 * wide + 4, axis=1)
            packed = jnp.where(group == wide, turned, packed)
        edges[plane] = packed


def halo_lanes(edges, wide):
    lane = lax.broadcasted_iota(jnp.int32, edges.shape, 1)
    turned = pltpu.roll(edges, (LATS - 8 * wide - 4) % LATS, axis=1)
    return jnp.where((lane < 4) | (lane >= LATS - 4), turned, 0.0)


def weights(speeds, resist):
    out = []
    total = None
    for speed in speeds:
        lower = COURANT * jnp.maximum(speed, 0.0) + resist
        upper = resist - COURANT * jnp.minimum(speed, 0.0)
        out += [lower, upper]
        total = lower + upper if total is None else total + lower + upper
    return [1.0 - total] + out


def blend(w, centre, shell_lo, shell_hi, lon_lo, lon_hi, lat_lo, lat_hi):
    return (
        w[0] * centre
        + (w[1] * shell_lo + w[2] * shell_hi)
        + (w[3] * lon_lo + w[4] * lon_hi)
        + (w[5] * lat_lo + w[6] * lat_hi)
    )


def raw_chunks():
    found = []
    at = 0
    for plane in (5, 6, 8, 9, 10, 11):
        reach = PHASES + 1 if plane < FIELDS else PHASES
        for wide in range(WIDE):
            count = reach - max(LONS - wide, wide - 2 * LONS + 1, 0)
            if count > 0:
                found.append((plane, wide, at, count))
                at += count
    return found


def raw_body(low, own, high, out):
    for plane, wide, at, count in raw_chunks():
        ref = (low, own, high)[wide // LONS]
        out[at : at + count, :] = ref[plane, wide % LONS, :count, :]


def inner_body(raw, out, cells):
    span = 4 * LATS
    lane = lax.broadcasted_iota(jnp.int32, (8, span), 1)
    bottom = lax.broadcasted_iota(jnp.int32, (8, span), 0) == 0
    first, last = lane == 0, lane == span - 1
    cells[...] = jnp.zeros(cells.shape, F32)
    order = (5, 6, 8, 9, 10, 11)
    for plane, wide, at, count in raw_chunks():
        for rad in range(4):
            cells[order.index(plane), wide, :count, rad * LATS : (rad + 1) * LATS] = raw[
                rad * RAW + at : rad * RAW + at + count, :
            ]
    w = [None] + [
        weights([cells[2 + d, wide] for d in range(3)], cells[5, wide])
        for wide in range(1, WIDE - 1)
    ]
    made = []
    for part in range(2):
        now = [cells[part, wide] for wide in range(WIDE)]
        for phase in range(PHASES):
            fresh = list(now)
            for wide in range(phase + 1, WIDE - 1 - phase):
                c = now[wide]
                fresh[wide] = blend(
                    w[wide],
                    c,
                    jnp.where(bottom, 0.0, pltpu.roll(c, 1, axis=0)),
                    pltpu.roll(c, 7, axis=0),
                    now[wide - 1],
                    now[wide + 1],
                    jnp.where(first, 0.0, pltpu.roll(c, 1, axis=1)),
                    jnp.where(last, 0.0, pltpu.roll(c, span - 1, axis=1)),
                )
            now = fresh
        made.append(now[LONS : 2 * LONS])
    blon, blat = made
    for lon in range(LONS):
        c = blon[lon]
        source = jnp.where(first, 0.0, pltpu.roll(c, 1, axis=1)) - jnp.where(
            last, 0.0, pltpu.roll(c, span - 1, axis=1)
        )
        if lon < LONS - 1:
            source = source + blat[lon + 1]
        if lon > 0:
            source = source - blat[lon - 1]
        for rad in range(4):
            part = slice(rad * LATS, (rad + 1) * LATS)
            at = rad // 2 * 12 + rad % 2 * 4 + lon
            out[at : at + 1, :] = source[0:1, part]
            at = rad // 2 * 12 + 8 + rad % 2
            if lon == 0:
                out[at : at + 1, :] = blat[0][0:1, part]
            if lon == LONS - 1:
                out[at + 2 : at + 3, :] = blat[LONS - 1][0:1, part]


def base_body(spot, sent, out, cond):
    step = LATE - 16
    odd = spot[0] % 2 == 1
    for lon in range(LONS):
        at = 160 + lon
        lines = [sent[rad * SENT + at : rad * SENT + at + 1, :] for rad in range(4)]
        cond[lon : lon + 1, :] = jnp.where(odd, lines[2], lines[0])
        line = jnp.where(odd, lines[3], lines[1])
        out[pl.ds(lon, 32, stride=step), :] = jnp.broadcast_to(line, (32, LATS))
    for rad in range(4):
        for row in range(5):
            at = rad * SENT + row * 32
            out[pl.ds(4 + rad * 5 + row, 32, stride=step), :] = sent[at : at + 32, :]


def join_body(spot, one, two, cond, base, out, head, copies, sems):
    rest = pltpu.make_async_copy(base, out.at[:, pl.ds(16, LATE - 16), :], sems.at[0])
    rest.start()
    source = one[...] + two[...]
    head[:12, :] = jnp.where(spot[0] % 2 == 1, source[12:], source[:12])
    head[12:, :] = cond[...]
    mine = head[...]
    for owner in range(32):
        copies[owner] = mine
    move = pltpu.make_async_copy(copies, out.at[:, pl.ds(0, 16), :], sems.at[1])
    move.start()
    move.wait()
    rest.wait()


def join(spot, one, two, cond, base):
    vmem = pl.BlockSpec(memory_space=pltpu.VMEM)
    plain = pl.BlockSpec(memory_space=pl.ANY)
    return pl.pallas_call(
        join_body,
        out_shape=arr(32, LATE, LATS),
        in_specs=[pl.BlockSpec(memory_space=pltpu.SMEM), vmem, vmem, vmem, plain],
        out_specs=plain,
        scratch_shapes=[
            pltpu.VMEM((16, LATS), F32),
            pltpu.VMEM((32, 16, LATS), F32),
            pltpu.SemaphoreType.DMA((2,)),
        ],
        compiler_params=pltpu.CompilerParams(vmem_limit_bytes=4 * 2**20),
        cost_estimate=pl.CostEstimate(flops=10**5, bytes_accessed=10**6, transcendentals=0),
    )(spot, one, two, cond, base)


def half_body(late, out):
    for owner in range(32):
        out[owner] = late[owner, :HALF, :]


def chunks():
    found = []
    at = 0
    for wide in range(1, WIDE - 1):
        far = max(LONS - wide, wide - 2 * LONS + 1, 0)
        count = PHASES - far
        found.append((wide, at, count))
        at += count
    return found, at


def pack_body(low, own, high, up, down):
    found, rows = chunks()
    for plane in range(PLANES):
        for wide, start, count in found:
            ref = (low, own, high)[wide // LONS]
            up[plane, start : start + count, :] = ref[plane, wide % LONS, SHELLS - count :, :]
            down[plane, start : start + count, :] = ref[plane, wide % LONS, :count, :]
        up[plane, rows:, :] = jnp.zeros((32 - rows, LATS), F32)
        down[plane, rows:, :] = jnp.zeros((32 - rows, LATS), F32)


def main_body(low, own, high, above, below, from_low, from_high, out, cells, w, speeds):
    found, _ = chunks()
    lane = lax.broadcasted_iota(jnp.int32, (TALL, LATS), 1)

    def fill(plane, target):
        strip = jnp.where(lane % 8 < 4, from_low[plane], from_high[plane])
        for wide in range(WIDE):
            ref = (low, own, high)[wide // LONS]
            target[wide, :SHELLS, :LATS] = ref[plane, wide % LONS]
            target[wide, SHELLS:, :LATS] = jnp.zeros((TALL - SHELLS, LATS), F32)
            if 0 < wide < WIDE - 1:
                target[wide, :, LATS:] = halo_lanes(strip, wide)
            else:
                target[wide, :, LATS:] = jnp.zeros((TALL, LATS), F32)
        for wide, start, count in found:
            target[wide, SHELLS : SHELLS + count, :LATS] = above[plane, start : start + count, :]
            target[wide, TALL - count :, :LATS] = below[plane, start : start + count, :]

    for d in range(4):
        fill(FIELDS + d, speeds.at[d])
    for wide in range(1, WIDE - 1):
        made = weights([speeds[d, wide] for d in range(3)], speeds[3, wide])
        for i in range(7):
            w[i, wide] = made[i]

    def one(field, carry):
        fill(field, cells.at[0])
        for phase in range(PHASES):
            old = cells.at[phase % 2]
            new = cells.at[(phase + 1) % 2]
            for wide in range(phase + 1, WIDE - 1 - phase):
                c = old[wide]
                made = blend(
                    [w[i, wide] for i in range(7)],
                    c,
                    pltpu.roll(c, 1, axis=0),
                    pltpu.roll(c, TALL - 1, axis=0),
                    old[wide - 1],
                    old[wide + 1],
                    pltpu.roll(c, 1, axis=1),
                    pltpu.roll(c, 2 * LATS - 1, axis=1),
                )
                if phase == PHASES - 1:
                    out[field, pl.ds(wide - LONS, SHELLS, stride=LONS), :] = made[:SHELLS, :LATS]
                else:
                    new[wide] = made
        return carry

    lax.fori_loop(0, FIELDS, one, 0)


def slot_body(owners, rows, maps, conductance, out):
    count = owners.shape[1]
    here = lax.broadcasted_iota(jnp.int32, (count, count), 0)
    there = lax.broadcasted_iota(jnp.int32, (count, count), 1)
    aimed = (here % 32) * 4 + here // 32 == owners[...]
    earlier = jnp.dot(
        aimed.astype(jnp.bfloat16), (here < there).astype(jnp.bfloat16), preferred_element_type=F32
    )
    cell = maps[...]
    small = (cell & 127).astype(F32).astype(jnp.bfloat16)
    large = (cell >> 7).astype(F32).astype(jnp.bfloat16)
    row = (rows[...] + 1).astype(F32)
    marks = []
    lines = []
    for slot in range(2):
        chosen = jnp.where(aimed & (earlier == float(slot)), 1.0, 0.0)
        marks.append(jnp.sum(chosen * row, axis=1, keepdims=True) - 1.0)
        pick = chosen.astype(jnp.bfloat16)
        made = jnp.dot(pick, small, preferred_element_type=F32) + 128.0 * jnp.dot(
            pick, large, preferred_element_type=F32
        )
        lines += [made[:, :128], made[:, 128:]]
    lines.append(jnp.where(there < 64, marks[0], marks[1]))
    for rad in range(4):
        for j in range(5):
            at = rad * SENT + j * 32
            out[at : at + 32, :] = lines[j][rad * 32 : rad * 32 + 32]
        at = rad * SENT + 160
        out[at : at + 4, :] = conductance[...]
        out[at + 4 : at + 8, :] = jnp.zeros((4, LATS), F32)


def final_body(spot, late, other, pot, foot, phi, east_w, west_w, north_w, south_w, start, picked, hot):
    devs, rads = 32, 4
    wide = rads * LATS
    lane = lax.broadcasted_iota(jnp.int32, (devs, wide), 1)

    odd = spot[0] % 2

    def gather(at, step):
        found = []
        for rad in range(rads):
            row = at + rad % 2 * step
            mine = late[pl.ds(row, devs, stride=LATE), :]
            theirs = other[pl.ds(row, devs, stride=HALF), :]
            found.append(jnp.where(odd == rad // 2, mine, theirs))
        return jnp.concatenate(found, axis=1)

    def lon_up(values, lon):
        return values[lon + 1] if lon < LONS - 1 else pltpu.roll(values[0], devs - 1, axis=0)

    def lon_down(values, lon):
        return values[lon - 1] if lon > 0 else pltpu.roll(values[LONS - 1], 1, axis=0)

    def lat_up(value):
        return pltpu.roll(value, wide - 1, axis=1)

    def lat_down(value):
        return pltpu.roll(value, 1, axis=1)

    cond = [gather(12 + lon, 4) for lon in range(LONS)]
    sources = [gather(lon, 4) for lon in range(LONS)]
    sources[LONS - 1] += pltpu.roll(gather(8, 1), devs - 1, axis=0)
    sources[0] -= pltpu.roll(gather(10, 1), 1, axis=0)
    last, first = lane == wide - 1, lane == 0
    for lon in range(LONS):
        source = sources[lon]
        c = cond[lon]
        east = 0.5 * (c + lon_up(cond, lon))
        west = 0.5 * (c + lon_down(cond, lon))
        north = 0.5 * (c + jnp.where(last, 0.0, lat_up(c)))
        south = 0.5 * (c + jnp.where(first, 0.0, lat_down(c)))
        scale = RELAX / (DAMPING * c + east + west + north + south)
        east_w[lon] = east * scale
        west_w[lon] = west * scale
        north_w[lon] = jnp.where(last, 0.0, north * scale)
        south_w[lon] = jnp.where(first, 0.0, south * scale)
        start[lon] = source * scale
        phi[0, lon] = source * scale

    def sweep(old, new):
        values = [phi[old, lon] for lon in range(LONS)]
        for lon in range(LONS):
            c = values[lon]
            phi[new, lon] = (
                (1.0 - RELAX) * c
                + start[lon]
                + (east_w[lon] * lon_up(values, lon) + west_w[lon] * lon_down(values, lon))
                + (north_w[lon] * lat_up(c) + south_w[lon] * lat_down(c))
            )

    for turn in range(SWEEPS - 1):
        sweep(turn % 2, (turn + 1) % 2)
    done = (SWEEPS - 1) % 2
    at_lon = lax.broadcasted_iota(jnp.int32, (devs, LATS), 0) == spot[2]
    for rad in range(rads):

        @pl.when(spot[1] == rad)
        def _():
            for lon in range(LONS):
                block = phi[done, lon, :, rad * LATS : (rad + 1) * LATS]
                pot[lon : lon + 1, :] = jnp.sum(
                    jnp.where(at_lon, block, 0.0), axis=0, keepdims=True
                )

    slot_lane = lax.broadcasted_iota(jnp.int32, (devs, LATS), 1).astype(F32)
    for rad in range(rads):
        table = [phi[done, lon, :, rad * LATS : (rad + 1) * LATS] for lon in range(LONS)]
        marks = late[pl.ds(20 + rad * 5 + 4, devs, stride=LATE), :]
        for slot in range(2):
            at = (slot * rads + rad) * devs
            row = marks if slot == 0 else pltpu.roll(marks, 64, axis=1)
            hot[at : at + devs, :] = jnp.where(row == slot_lane, 1.0, 0.0)
            for half in range(2):
                cell = late[pl.ds(20 + rad * 5 + 2 * slot + half, devs, stride=LATE), :].astype(jnp.int32)
                place, lon_at = cell & 127, cell >> 7
                value = jnp.zeros((devs, LATS), F32)
                for lon in range(LONS):
                    found = jnp.take_along_axis(
                        table[lon], place, axis=1, mode="promise_in_bounds"
                    )
                    value = jnp.where(lon_at == lon, found, value)
                picked[at : at + devs, 128 * half : 128 * half + 128] = value
    summed = lax.dot_general(
        hot[...],
        picked[...],
        (((0,), (0,)), ((), ())),
        precision=lax.Precision.HIGHEST,
        preferred_element_type=F32,
    )
    foot[...] = summed[:ROWS_OWN]


def shards(plasma_fields, velocity, resistivity, conductance, foot_map, foot_owner, foot_row):
    spot = jnp.stack([lax.axis_index("sec"), lax.axis_index("rad"), lax.axis_index("lon")])
    speeds = (
        jnp.concatenate([velocity, resistivity[None]], axis=0)
        .astype(F32)
        .reshape(4, SHELLS * LONS, LATS)
    )
    own = call(
        stage_body,
        arr(PLANES, LONS, SHELLS, LATS),
        (plasma_fields.reshape(FIELDS, SHELLS * LONS, LATS), speeds),
    )
    low = lax.ppermute(own, "lon", shift("lon", 1, True))
    high = lax.ppermute(own, "lon", shift("lon", -1, True))

    slots = call(
        slot_body,
        arr(4 * SENT, LATS),
        (foot_owner.reshape(1, -1), foot_row.reshape(1, -1), foot_map, conductance),
    )
    sent = lax.all_to_all(
        slots.reshape(4, SENT, LATS), "rad", split_axis=0, concat_axis=0, tiled=True
    )

    low, high, sent = lax.optimization_barrier((low, high, sent))
    up, down = call(pack_body, (arr(PLANES, 32, LATS), arr(PLANES, 32, LATS)), (low, own, high))
    below = lax.ppermute(up, "sec", shift("sec", 1, False))
    above = lax.ppermute(down, "sec", shift("sec", -1, False))
    raw = call(raw_body, arr(RAW, LATS), (low, own, high))
    raw = lax.all_gather(raw, "rad")
    raw, above, below = lax.optimization_barrier((raw, above, below))
    inner = call(
        inner_body,
        arr(24, LATS),
        (raw.reshape(4 * RAW, LATS),),
        scratch=(pltpu.VMEM((6, WIDE, 8, 4 * LATS), F32),),
    )
    far = lax.ppermute(inner, "sec", [(0, 3)])
    far = jnp.where(lax.axis_index("sec") == 0, inner, far)
    near = lax.ppermute(far, "sec", [(0, 1), (3, 2)])
    base, cond = call(
        base_body,
        (arr(32 * (LATE - 16), LATS), arr(LONS, LATS)),
        (spot, sent.reshape(4 * SENT, LATS)),
        smem=(0,),
    )
    late = join(spot, far, near, cond, base.reshape(32, LATE - 16, LATS))
    late, low, high = lax.optimization_barrier((late, low, high))

    blocks = (low, own, high, above, below)
    edges = call(
        edge_body,
        arr(PLANES, TALL, LATS),
        blocks,
        scratch=(pltpu.VMEM((PLANES, WIDE, TALL, LATS), F32),),
    )
    from_low = lax.ppermute(edges, "rad", shift("rad", 1, False))
    from_high = lax.ppermute(edges, "rad", shift("rad", -1, False))
    late = lax.all_to_all(
        late, "lon", split_axis=0, concat_axis=0, tiled=True
    )

    advanced = call(
        main_body,
        arr(FIELDS, SHELLS * LONS, LATS),
        blocks + (from_low, from_high),
        scratch=(
            pltpu.VMEM((2, WIDE, TALL, 2 * LATS), F32),
            pltpu.VMEM((7, WIDE, TALL, 2 * LATS), F32),
            pltpu.VMEM((4, WIDE, TALL, 2 * LATS), F32),
        ),
    ).reshape(FIELDS, SHELLS, LONS, LATS)

    late, advanced = lax.optimization_barrier((late, advanced))
    other = lax.ppermute(
        call(half_body, arr(32, HALF, LATS), (late,)), "sec", [(0, 1), (1, 0), (2, 3), (3, 2)]
    )
    plane = pltpu.VMEM((LONS, 32, 4 * LATS), F32)
    potential, foot_table = call(
        final_body,
        (arr(LONS, LATS), arr(ROWS_OWN, 256)),
        (spot, late.reshape(32 * LATE, LATS), other.reshape(32 * HALF, LATS)),
        scratch=(
            pltpu.VMEM((2, LONS, 32, 4 * LATS), F32),
            plane,
            plane,
            plane,
            plane,
            plane,
            pltpu.VMEM((256, 256), F32),
            pltpu.VMEM((256, 128), F32),
        ),
        smem=(0,),
    )
    return (advanced, potential, foot_table)


def solution(mesh):
    in_specs = (
        P(None, "sec", "lon", "rad"),
        P(None, "sec", "lon", "rad"),
        P("sec", "lon", "rad"),
        P("lon", "rad"),
        P(("lon", "sec", "rad"), None),
        P(("lon", "sec", "rad"), None),
        P(("lon", "sec", "rad")),
    )
    out_specs = (P(None, "sec", "lon", "rad"), P("lon", "rad"), P(("lon", "sec", "rad"), None))
    return jax.shard_map(shards, mesh=mesh, in_specs=in_specs, out_specs=out_specs, check_vma=False)
```

```python
import jax
import jax.numpy as jnp
from jax import lax
from jax.experimental import pallas as pl
from jax.experimental.pallas import tpu as pltpu
from jax.sharding import PartitionSpec as P

PHASES = 4
SWEEPS = 8
ROWS_OWN = 32
COURANT = 0.25
DAMPING = 0.05
RELAX = 0.8

FIELDS = 8
PLANES = FIELDS + 4
SHELLS = 16
LONS = 4
LATS = 128
WIDE = 3 * LONS
LATE = 40
HALF = 24
RAW = 192
SENT = 136
TALL = SHELLS + 2 * PHASES
F32 = jnp.float32


def call(body, out_shape, args, scratch=(), smem=(), flops=10**6, traffic=10**6):
    specs = [
        pl.BlockSpec(memory_space=pltpu.SMEM if i in smem else pltpu.VMEM)
        for i in range(len(args))
    ]
    many = isinstance(out_shape, (tuple, list))
    vmem = pl.BlockSpec(memory_space=pltpu.VMEM)
    return pl.pallas_call(
        body,
        out_shape=out_shape,
        in_specs=specs,
        out_specs=[vmem] * len(out_shape) if many else vmem,
        scratch_shapes=list(scratch),
        compiler_params=pltpu.CompilerParams(vmem_limit_bytes=16 * 2**20),
        cost_estimate=pl.CostEstimate(flops=flops, bytes_accessed=traffic, transcendentals=0),
    )(*args)


def arr(*shape):
    return jax.ShapeDtypeStruct(shape, F32)


def shift(axis, step, closed):
    count = lax.axis_size(axis)
    return [
        (i, (i + step) % count) for i in range(count) if closed or 0 <= i + step < count
    ]


def first_body(*refs):
    sources, (own, slots, plain), held, sems = refs[:7], refs[7:10], refs[10:17], refs[17]
    moves = [
        pltpu.make_async_copy(source, target, sems.at[i])
        for i, (source, target) in enumerate(zip(sources, held))
    ]
    for move in moves:
        move.start()
    fields, speeds, resist, owners, rows, maps, conductance = held
    for move in moves[1:3]:
        move.wait()
    for plane in range(4):
        for shell in range(SHELLS):
            found = speeds[plane, shell] if plane < 3 else resist[shell]
            plain[plane, shell * LONS : shell * LONS + LONS, :] = found.astype(F32)
    moves[0].wait()
    for plane in range(PLANES):
        for lon in range(LONS):
            at = pl.ds(lon, SHELLS, stride=LONS)
            if plane < FIELDS:
                own[plane, lon] = fields[plane, at, :]
            else:
                own[plane, lon] = plain[plane - FIELDS, at, :]
    for move in moves[3:]:
        move.wait()
    slot_body(owners, rows, maps, conductance, slots)


def first(*args):
    vmem = pl.BlockSpec(memory_space=pltpu.VMEM)
    return pl.pallas_call(
        first_body,
        out_shape=(arr(PLANES, LONS, SHELLS, LATS), arr(4 * SENT, LATS)),
        in_specs=[pl.BlockSpec(memory_space=pltpu.HBM)] * len(args),
        out_specs=[vmem, vmem],
        scratch_shapes=[pltpu.VMEM((4, SHELLS * LONS, LATS), F32)]
        + [pltpu.VMEM(arg.shape, arg.dtype) for arg in args]
        + [pltpu.SemaphoreType.DMA((len(args),))],
        compiler_params=pltpu.CompilerParams(vmem_limit_bytes=60 * 2**20),
        cost_estimate=pl.CostEstimate(flops=10**6, bytes_accessed=10**6, transcendentals=0),
    )(*args)


def edge_body(low, own, high, above, below, edges, tall):
    found, _ = chunks()
    group = lax.broadcasted_iota(jnp.int32, (TALL, LATS), 1) // 8
    for plane in range(PLANES):
        for wide in range(WIDE):
            ref = (low, own, high)[wide // LONS]
            tall[plane, wide, :SHELLS, :] = ref[plane, wide % LONS]
            tall[plane, wide, SHELLS:, :] = jnp.zeros((TALL - SHELLS, LATS), F32)
        for wide, start, count in found:
            tall[plane, wide, SHELLS : SHELLS + count, :] = above[plane, start : start + count, :]
            tall[plane, wide, TALL - count :, :] = below[plane, start : start + count, :]
    for plane in range(PLANES):
        packed = jnp.zeros((TALL, LATS), F32)
        for wide in range(1, WIDE - 1):
            turned = pltpu.roll(tall[plane, wide], 8 * wide + 4, axis=1)
            packed = jnp.where(group == wide, turned, packed)
        edges[plane] = packed


def halo_lanes(edges, wide):
    lane = lax.broadcasted_iota(jnp.int32, edges.shape, 1)
    turned = pltpu.roll(edges, (LATS - 8 * wide - 4) % LATS, axis=1)
    return jnp.where((lane < 4) | (lane >= LATS - 4), turned, 0.0)


def weights(speeds, resist):
    out = []
    total = None
    for speed in speeds:
        lower = COURANT * jnp.maximum(speed, 0.0) + resist
        upper = resist - COURANT * jnp.minimum(speed, 0.0)
        out += [lower, upper]
        total = lower + upper if total is None else total + lower + upper
    return [1.0 - total] + out


def blend(w, centre, shell_lo, shell_hi, lon_lo, lon_hi, lat_lo, lat_hi):
    return (
        w[0] * centre
        + (w[1] * shell_lo + w[2] * shell_hi)
        + (w[3] * lon_lo + w[4] * lon_hi)
        + (w[5] * lat_lo + w[6] * lat_hi)
    )


def raw_chunks():
    found = []
    at = 0
    for plane in (5, 6, 8, 9, 10, 11):
        reach = PHASES + 1 if plane < FIELDS else PHASES
        for wide in range(WIDE):
            count = reach - max(LONS - wide, wide - 2 * LONS + 1, 0)
            if count > 0:
                found.append((plane, wide, at, count))
                at += count
    return found


def raw_body(low, own, high, out):
    for plane, wide, at, count in raw_chunks():
        ref = (low, own, high)[wide // LONS]
        out[at : at + count, :] = ref[plane, wide % LONS, :count, :]


def inner_body(raw, out, cells):
    span = 4 * LATS
    lane = lax.broadcasted_iota(jnp.int32, (8, span), 1)
    bottom = lax.broadcasted_iota(jnp.int32, (8, span), 0) == 0
    first, last = lane == 0, lane == span - 1
    cells[...] = jnp.zeros(cells.shape, F32)
    order = (5, 6, 8, 9, 10, 11)
    for plane, wide, at, count in raw_chunks():
        for rad in range(4):
            cells[order.index(plane), wide, :count, rad * LATS : (rad + 1) * LATS] = raw[
                rad * RAW + at : rad * RAW + at + count, :
            ]
    w = [None] + [
        weights([cells[2 + d, wide] for d in range(3)], cells[5, wide])
        for wide in range(1, WIDE - 1)
    ]
    made = []
    for part in range(2):
        now = [cells[part, wide] for wide in range(WIDE)]
        for phase in range(PHASES):
            fresh = list(now)
            for wide in range(phase + 1, WIDE - 1 - phase):
                c = now[wide]
                fresh[wide] = blend(
                    w[wide],
                    c,
                    jnp.where(bottom, 0.0, pltpu.roll(c, 1, axis=0)),
                    pltpu.roll(c, 7, axis=0),
                    now[wide - 1],
                    now[wide + 1],
                    jnp.where(first, 0.0, pltpu.roll(c, 1, axis=1)),
                    jnp.where(last, 0.0, pltpu.roll(c, span - 1, axis=1)),
                )
            now = fresh
        made.append(now[LONS : 2 * LONS])
    blon, blat = made
    for lon in range(LONS):
        c = blon[lon]
        source = jnp.where(first, 0.0, pltpu.roll(c, 1, axis=1)) - jnp.where(
            last, 0.0, pltpu.roll(c, span - 1, axis=1)
        )
        if lon < LONS - 1:
            source = source + blat[lon + 1]
        if lon > 0:
            source = source - blat[lon - 1]
        for rad in range(4):
            part = slice(rad * LATS, (rad + 1) * LATS)
            at = rad // 2 * 12 + rad % 2 * 4 + lon
            out[at : at + 1, :] = source[0:1, part]
            at = rad // 2 * 12 + 8 + rad % 2
            if lon == 0:
                out[at : at + 1, :] = blat[0][0:1, part]
            if lon == LONS - 1:
                out[at + 2 : at + 3, :] = blat[LONS - 1][0:1, part]


def base_body(spot, sent, out, cond):
    step = LATE - 16
    odd = spot[0] % 2 == 1
    for lon in range(LONS):
        at = 130 + lon
        lines = [sent[rad * SENT + at : rad * SENT + at + 1, :] for rad in range(4)]
        cond[lon : lon + 1, :] = jnp.where(odd, lines[2], lines[0])
        line = jnp.where(odd, lines[3], lines[1])
        out[pl.ds(lon, 32, stride=step), :] = jnp.broadcast_to(line, (32, LATS))
    lane = lax.broadcasted_iota(jnp.int32, (32, LATS), 1)
    owner = lax.broadcasted_iota(jnp.int32, (32, LATS), 0)
    for rad in range(4):
        for row in range(4):
            at = rad * SENT + row * 32
            out[pl.ds(4 + rad * 5 + row, 32, stride=step), :] = sent[at : at + 32, :]
        marks = []
        for slot in range(2):
            at = rad * SENT + 128 + slot
            line = jnp.broadcast_to(sent[at : at + 1, :], (32, LATS))
            marks.append(
                jnp.sum(jnp.where(lane == owner + spot[1] * 32, line, 0.0), axis=1, keepdims=True)
            )
        out[pl.ds(8 + rad * 5, 32, stride=step), :] = jnp.where(lane < 64, marks[0], marks[1])


def join_body(spot, one, two, cond, base, out, head, copies, sems):
    rest = pltpu.make_async_copy(base, out.at[:, pl.ds(16, LATE - 16), :], sems.at[0])
    rest.start()
    source = one[...] + two[...]
    head[:12, :] = jnp.where(spot[0] % 2 == 1, source[12:], source[:12])
    head[12:, :] = cond[...]
    mine = head[...]
    for owner in range(32):
        copies[owner] = mine
    move = pltpu.make_async_copy(copies, out.at[:, pl.ds(0, 16), :], sems.at[1])
    move.start()
    move.wait()
    rest.wait()


def join(spot, one, two, cond, base):
    vmem = pl.BlockSpec(memory_space=pltpu.VMEM)
    plain = pl.BlockSpec(memory_space=pl.ANY)
    return pl.pallas_call(
        join_body,
        out_shape=arr(32, LATE, LATS),
        in_specs=[pl.BlockSpec(memory_space=pltpu.SMEM), vmem, vmem, vmem, plain],
        out_specs=plain,
        scratch_shapes=[
            pltpu.VMEM((16, LATS), F32),
            pltpu.VMEM((32, 16, LATS), F32),
            pltpu.SemaphoreType.DMA((2,)),
        ],
        compiler_params=pltpu.CompilerParams(vmem_limit_bytes=4 * 2**20),
        cost_estimate=pl.CostEstimate(flops=10**5, bytes_accessed=10**6, transcendentals=0),
    )(spot, one, two, cond, base)


def half_body(late, out):
    for owner in range(32):
        out[owner] = late[owner, :HALF, :]


def chunks():
    found = []
    at = 0
    for wide in range(1, WIDE - 1):
        far = max(LONS - wide, wide - 2 * LONS + 1, 0)
        count = PHASES - far
        found.append((wide, at, count))
        at += count
    return found, at


def pack_body(low, own, high, up, down):
    found, rows = chunks()
    for plane in range(PLANES):
        for wide, start, count in found:
            ref = (low, own, high)[wide // LONS]
            up[plane, start : start + count, :] = ref[plane, wide % LONS, SHELLS - count :, :]
            down[plane, start : start + count, :] = ref[plane, wide % LONS, :count, :]
        up[plane, rows:, :] = jnp.zeros((32 - rows, LATS), F32)
        down[plane, rows:, :] = jnp.zeros((32 - rows, LATS), F32)


def main_body(low, own, high, above, below, from_low, from_high, out, cells, w, speeds):
    found, _ = chunks()
    lane = lax.broadcasted_iota(jnp.int32, (TALL, LATS), 1)

    def fill(plane, target):
        strip = jnp.where(lane % 8 < 4, from_low[plane], from_high[plane])
        for wide in range(WIDE):
            ref = (low, own, high)[wide // LONS]
            target[wide, :SHELLS, :LATS] = ref[plane, wide % LONS]
            target[wide, SHELLS:, :LATS] = jnp.zeros((TALL - SHELLS, LATS), F32)
            if 0 < wide < WIDE - 1:
                target[wide, :, LATS:] = halo_lanes(strip, wide)
            else:
                target[wide, :, LATS:] = jnp.zeros((TALL, LATS), F32)
        for wide, start, count in found:
            target[wide, SHELLS : SHELLS + count, :LATS] = above[plane, start : start + count, :]
            target[wide, TALL - count :, :LATS] = below[plane, start : start + count, :]

    for d in range(4):
        fill(FIELDS + d, speeds.at[d])
    for wide in range(1, WIDE - 1):
        made = weights([speeds[d, wide] for d in range(3)], speeds[3, wide])
        for i in range(7):
            w[i, wide] = made[i]

    def one(field, carry):
        fill(field, cells.at[0])
        for phase in range(PHASES):
            old = cells.at[phase % 2]
            new = cells.at[(phase + 1) % 2]
            for wide in range(phase + 1, WIDE - 1 - phase):
                c = old[wide]
                made = blend(
                    [w[i, wide] for i in range(7)],
                    c,
                    pltpu.roll(c, 1, axis=0),
                    pltpu.roll(c, TALL - 1, axis=0),
                    old[wide - 1],
                    old[wide + 1],
                    pltpu.roll(c, 1, axis=1),
                    pltpu.roll(c, 2 * LATS - 1, axis=1),
                )
                if phase == PHASES - 1:
                    out[field, pl.ds(wide - LONS, SHELLS, stride=LONS), :] = made[:SHELLS, :LATS]
                else:
                    new[wide] = made
        return carry

    lax.fori_loop(0, FIELDS, one, 0)


def slot_body(owners, rows, maps, conductance, out):
    count = owners.shape[1]
    here = lax.broadcasted_iota(jnp.int32, (count, count), 0)
    there = lax.broadcasted_iota(jnp.int32, (count, count), 1)
    aimed = (here % 32) * 4 + here // 32 == owners[...]
    earlier = jnp.dot(
        aimed.astype(jnp.bfloat16), (here < there).astype(jnp.bfloat16), preferred_element_type=F32
    )
    cell = maps[...]
    small = (cell & 127).astype(F32).astype(jnp.bfloat16)
    large = (cell >> 7).astype(F32).astype(jnp.bfloat16)
    row = jnp.broadcast_to((rows[...] + 1).astype(F32), (8, count)).astype(jnp.bfloat16)
    marks = []
    lines = []
    for slot in range(2):
        pick = jnp.where(aimed & (earlier == float(slot)), 1.0, 0.0).astype(jnp.bfloat16)
        marks.append(
            lax.dot_general(row, pick, (((1,), (1,)), ((), ())), preferred_element_type=F32) - 1.0
        )
        made = jnp.dot(pick, small, preferred_element_type=F32) + 128.0 * jnp.dot(
            pick, large, preferred_element_type=F32
        )
        lines += [made[:, :128], made[:, 128:]]
    for rad in range(4):
        for j in range(4):
            at = rad * SENT + j * 32
            out[at : at + 32, :] = lines[j][rad * 32 : rad * 32 + 32]
        at = rad * SENT + 128
        out[at : at + 1, :] = marks[0][:1]
        out[at + 1 : at + 2, :] = marks[1][:1]
        out[at + 2 : at + 6, :] = conductance[...]
        out[at + 6 : at + 8, :] = jnp.zeros((2, LATS), F32)


def final_body(spot, late, other, pot, foot, phi, east_w, west_w, north_w, south_w, start, picked, hot):
    devs, rads = 32, 4
    wide = rads * LATS
    lane = lax.broadcasted_iota(jnp.int32, (devs, wide), 1)

    odd = spot[0] % 2

    def gather(at, step):
        found = []
        for rad in range(rads):
            row = at + rad % 2 * step
            mine = late[pl.ds(row, devs, stride=LATE), :]
            theirs = other[pl.ds(row, devs, stride=HALF), :]
            found.append(jnp.where(odd == rad // 2, mine, theirs))
        return jnp.concatenate(found, axis=1)

    def lon_up(values, lon):
        return values[lon + 1] if lon < LONS - 1 else pltpu.roll(values[0], devs - 1, axis=0)

    def lon_down(values, lon):
        return values[lon - 1] if lon > 0 else pltpu.roll(values[LONS - 1], 1, axis=0)

    def lat_up(value):
        return pltpu.roll(value, wide - 1, axis=1)

    def lat_down(value):
        return pltpu.roll(value, 1, axis=1)

    cond = [gather(12 + lon, 4) for lon in range(LONS)]
    sources = [gather(lon, 4) for lon in range(LONS)]
    sources[LONS - 1] += pltpu.roll(gather(8, 1), devs - 1, axis=0)
    sources[0] -= pltpu.roll(gather(10, 1), 1, axis=0)
    last, first = lane == wide - 1, lane == 0
    for lon in range(LONS):
        source = sources[lon]
        c = cond[lon]
        east = 0.5 * (c + lon_up(cond, lon))
        west = 0.5 * (c + lon_down(cond, lon))
        north = 0.5 * (c + jnp.where(last, 0.0, lat_up(c)))
        south = 0.5 * (c + jnp.where(first, 0.0, lat_down(c)))
        scale = RELAX / (DAMPING * c + east + west + north + south)
        east_w[lon] = east * scale
        west_w[lon] = west * scale
        north_w[lon] = jnp.where(last, 0.0, north * scale)
        south_w[lon] = jnp.where(first, 0.0, south * scale)
        start[lon] = source * scale
        phi[0, lon] = source * scale

    def sweep(old, new):
        values = [phi[old, lon] for lon in range(LONS)]
        for lon in range(LONS):
            c = values[lon]
            phi[new, lon] = (
                (1.0 - RELAX) * c
                + start[lon]
                + (east_w[lon] * lon_up(values, lon) + west_w[lon] * lon_down(values, lon))
                + (north_w[lon] * lat_up(c) + south_w[lon] * lat_down(c))
            )

    for turn in range(SWEEPS - 1):
        sweep(turn % 2, (turn + 1) % 2)
    done = (SWEEPS - 1) % 2
    at_lon = lax.broadcasted_iota(jnp.int32, (devs, LATS), 0) == spot[2]
    for rad in range(rads):

        @pl.when(spot[1] == rad)
        def _():
            for lon in range(LONS):
                block = phi[done, lon, :, rad * LATS : (rad + 1) * LATS]
                pot[lon : lon + 1, :] = jnp.sum(
                    jnp.where(at_lon, block, 0.0), axis=0, keepdims=True
                )

    slot_lane = lax.broadcasted_iota(jnp.int32, (devs, LATS), 1).astype(F32)
    for rad in range(rads):
        table = [phi[done, lon, :, rad * LATS : (rad + 1) * LATS] for lon in range(LONS)]
        marks = late[pl.ds(20 + rad * 5 + 4, devs, stride=LATE), :]
        for slot in range(2):
            at = (slot * rads + rad) * devs
            row = marks if slot == 0 else pltpu.roll(marks, 64, axis=1)
            hot[at : at + devs, :] = jnp.where(row == slot_lane, 1.0, 0.0)
            for half in range(2):
                cell = late[pl.ds(20 + rad * 5 + 2 * slot + half, devs, stride=LATE), :].astype(jnp.int32)
                place, lon_at = cell & 127, cell >> 7
                value = jnp.zeros((devs, LATS), F32)
                for lon in range(LONS):
                    found = jnp.take_along_axis(
                        table[lon], place, axis=1, mode="promise_in_bounds"
                    )
                    value = jnp.where(lon_at == lon, found, value)
                picked[at : at + devs, 128 * half : 128 * half + 128] = value
    summed = lax.dot_general(
        hot[...],
        picked[...],
        (((0,), (0,)), ((), ())),
        precision=lax.Precision.HIGHEST,
        preferred_element_type=F32,
    )
    foot[...] = summed[:ROWS_OWN]


def shards(plasma_fields, velocity, resistivity, conductance, foot_map, foot_owner, foot_row):
    spot = jnp.stack([lax.axis_index("sec"), lax.axis_index("rad"), lax.axis_index("lon")])
    own, slots = first(
        plasma_fields.reshape(FIELDS, SHELLS * LONS, LATS),
        velocity,
        resistivity,
        foot_owner.reshape(1, -1),
        foot_row.reshape(1, -1),
        foot_map,
        conductance,
    )
    low = lax.ppermute(own, "lon", shift("lon", 1, True))
    high = lax.ppermute(own, "lon", shift("lon", -1, True))

    sent = lax.all_to_all(
        slots.reshape(4, SENT, LATS), "rad", split_axis=0, concat_axis=0, tiled=True
    )

    low, high, sent = lax.optimization_barrier((low, high, sent))
    up, down = call(pack_body, (arr(PLANES, 32, LATS), arr(PLANES, 32, LATS)), (low, own, high))
    above = lax.ppermute(down, "sec", shift("sec", -1, False))
    below = lax.ppermute(up, "sec", shift("sec", 1, False))
    raw = call(raw_body, arr(RAW, LATS), (low, own, high))
    raw = lax.all_gather(raw, "rad")
    raw, below, above = lax.optimization_barrier((raw, below, above))
    inner = call(
        inner_body,
        arr(24, LATS),
        (raw.reshape(4 * RAW, LATS),),
        scratch=(pltpu.VMEM((6, WIDE, 8, 4 * LATS), F32),),
    )
    far = lax.ppermute(inner, "sec", [(0, 3)])
    far = jnp.where(lax.axis_index("sec") == 0, inner, far)
    near = lax.ppermute(far, "sec", [(0, 1), (3, 2)])
    base, cond = call(
        base_body,
        (arr(32 * (LATE - 16), LATS), arr(LONS, LATS)),
        (spot, sent.reshape(4 * SENT, LATS)),
        smem=(0,),
    )
    late = join(spot, far, near, cond, base.reshape(32, LATE - 16, LATS))
    late, low, high = lax.optimization_barrier((late, low, high))

    blocks = (low, own, high, above, below)
    edges = call(
        edge_body,
        arr(PLANES, TALL, LATS),
        blocks,
        scratch=(pltpu.VMEM((PLANES, WIDE, TALL, LATS), F32),),
    )
    from_low = lax.ppermute(edges, "rad", shift("rad", 1, False))
    from_high = lax.ppermute(edges, "rad", shift("rad", -1, False))
    late = lax.all_to_all(
        late, "lon", split_axis=0, concat_axis=0, tiled=True
    )

    advanced = call(
        main_body,
        arr(FIELDS, SHELLS * LONS, LATS),
        blocks + (from_low, from_high),
        scratch=(
            pltpu.VMEM((2, WIDE, TALL, 2 * LATS), F32),
            pltpu.VMEM((7, WIDE, TALL, 2 * LATS), F32),
            pltpu.VMEM((4, WIDE, TALL, 2 * LATS), F32),
        ),
    ).reshape(FIELDS, SHELLS, LONS, LATS)

    late, advanced = lax.optimization_barrier((late, advanced))
    other = lax.ppermute(
        call(half_body, arr(32, HALF, LATS), (late,)), "sec", [(0, 1), (1, 0), (2, 3), (3, 2)]
    )
    plane = pltpu.VMEM((LONS, 32, 4 * LATS), F32)
    potential, foot_table = call(
        final_body,
        (arr(LONS, LATS), arr(ROWS_OWN, 256)),
        (spot, late.reshape(32 * LATE, LATS), other.reshape(32 * HALF, LATS)),
        scratch=(
            pltpu.VMEM((2, LONS, 32, 4 * LATS), F32),
            plane,
            plane,
            plane,
            plane,
            plane,
            pltpu.VMEM((256, 256), F32),
            pltpu.VMEM((256, 128), F32),
        ),
        smem=(0,),
    )
    return (advanced, potential, foot_table)


def solution(mesh):
    in_specs = (
        P(None, "sec", "lon", "rad"),
        P(None, "sec", "lon", "rad"),
        P("sec", "lon", "rad"),
        P("lon", "rad"),
        P(("lon", "sec", "rad"), None),
        P(("lon", "sec", "rad"), None),
        P(("lon", "sec", "rad")),
    )
    out_specs = (P(None, "sec", "lon", "rad"), P("lon", "rad"), P(("lon", "sec", "rad"), None))
    return jax.shard_map(shards, mesh=mesh, in_specs=in_specs, out_specs=out_specs, check_vma=False)
```

```python
import jax
import jax.numpy as jnp
from jax import lax
from jax.experimental import pallas as pl
from jax.experimental.pallas import tpu as pltpu
from jax.sharding import PartitionSpec as P

PHASES = 4
SWEEPS = 8
ROWS_OWN = 32
COURANT = 0.25
DAMPING = 0.05
RELAX = 0.8

FIELDS = 8
PLANES = FIELDS + 4
SHELLS = 16
LONS = 4
LATS = 128
WIDE = 3 * LONS
LATE = 40
HALF = 24
RAW = 192
SENT = 136
TALL = SHELLS + 2 * PHASES
F32 = jnp.float32


def call(body, out_shape, args, scratch=(), smem=(), flops=10**6, traffic=10**6):
    specs = [
        pl.BlockSpec(memory_space=pltpu.SMEM if i in smem else pltpu.VMEM)
        for i in range(len(args))
    ]
    many = isinstance(out_shape, (tuple, list))
    vmem = pl.BlockSpec(memory_space=pltpu.VMEM)
    return pl.pallas_call(
        body,
        out_shape=out_shape,
        in_specs=specs,
        out_specs=[vmem] * len(out_shape) if many else vmem,
        scratch_shapes=list(scratch),
        compiler_params=pltpu.CompilerParams(vmem_limit_bytes=16 * 2**20),
        cost_estimate=pl.CostEstimate(flops=flops, bytes_accessed=traffic, transcendentals=0),
    )(*args)


def arr(*shape):
    return jax.ShapeDtypeStruct(shape, F32)


def shift(axis, step, closed):
    count = lax.axis_size(axis)
    return [
        (i, (i + step) % count) for i in range(count) if closed or 0 <= i + step < count
    ]


def first_body(*refs):
    sources, (own, slots, plain), held, sems = refs[:7], refs[7:10], refs[10:17], refs[17]
    moves = [
        pltpu.make_async_copy(source, target, sems.at[i])
        for i, (source, target) in enumerate(zip(sources, held))
    ]
    for move in moves:
        move.start()
    fields, speeds, resist, owners, rows, maps, conductance = held
    for move in moves[1:3]:
        move.wait()
    for plane in range(4):
        for shell in range(SHELLS):
            found = speeds[plane, shell] if plane < 3 else resist[shell]
            plain[plane, shell * LONS : shell * LONS + LONS, :] = found.astype(F32)
    moves[0].wait()
    for plane in range(PLANES):
        for lon in range(LONS):
            at = pl.ds(lon, SHELLS, stride=LONS)
            if plane < FIELDS:
                own[plane, lon] = fields[plane, at, :]
            else:
                own[plane, lon] = plain[plane - FIELDS, at, :]
    for move in moves[3:]:
        move.wait()
    slot_body(owners, rows, maps, conductance, slots)


def first(*args):
    vmem = pl.BlockSpec(memory_space=pltpu.VMEM)
    return pl.pallas_call(
        first_body,
        out_shape=(arr(PLANES, LONS, SHELLS, LATS), arr(4 * SENT, LATS)),
        in_specs=[pl.BlockSpec(memory_space=pltpu.HBM)] * len(args),
        out_specs=[vmem, vmem],
        scratch_shapes=[pltpu.VMEM((4, SHELLS * LONS, LATS), F32)]
        + [pltpu.VMEM(arg.shape, arg.dtype) for arg in args]
        + [pltpu.SemaphoreType.DMA((len(args),))],
        compiler_params=pltpu.CompilerParams(vmem_limit_bytes=60 * 2**20),
        cost_estimate=pl.CostEstimate(flops=10**6, bytes_accessed=10**6, transcendentals=0),
    )(*args)


def edge_body(low, own, high, above, below, edges, tall):
    found, _ = chunks()
    group = lax.broadcasted_iota(jnp.int32, (TALL, LATS), 1) // 8
    for plane in range(PLANES):
        for wide in range(WIDE):
            ref = (low, own, high)[wide // LONS]
            tall[plane, wide, :SHELLS, :] = ref[plane, wide % LONS]
            tall[plane, wide, SHELLS:, :] = jnp.zeros((TALL - SHELLS, LATS), F32)
        for wide, start, count in found:
            tall[plane, wide, SHELLS : SHELLS + count, :] = above[plane, start : start + count, :]
            tall[plane, wide, TALL - count :, :] = below[plane, start : start + count, :]
    for plane in range(PLANES):
        packed = jnp.zeros((TALL, LATS), F32)
        for wide in range(1, WIDE - 1):
            turned = pltpu.roll(tall[plane, wide], 8 * wide + 4, axis=1)
            packed = jnp.where(group == wide, turned, packed)
        edges[plane] = packed


def halo_lanes(edges, wide):
    lane = lax.broadcasted_iota(jnp.int32, edges.shape, 1)
    turned = pltpu.roll(edges, (LATS - 8 * wide - 4) % LATS, axis=1)
    return jnp.where((lane < 4) | (lane >= LATS - 4), turned, 0.0)


def weights(speeds, resist):
    out = []
    total = None
    for speed in speeds:
        lower = COURANT * jnp.maximum(speed, 0.0) + resist
        upper = resist - COURANT * jnp.minimum(speed, 0.0)
        out += [lower, upper]
        total = lower + upper if total is None else total + lower + upper
    return [1.0 - total] + out


def blend(w, centre, shell_lo, shell_hi, lon_lo, lon_hi, lat_lo, lat_hi):
    return (
        w[0] * centre
        + (w[1] * shell_lo + w[2] * shell_hi)
        + (w[3] * lon_lo + w[4] * lon_hi)
        + (w[5] * lat_lo + w[6] * lat_hi)
    )


def raw_chunks():
    found = []
    at = 0
    for plane in (5, 6, 8, 9, 10, 11):
        reach = PHASES + 1 if plane < FIELDS else PHASES
        for wide in range(WIDE):
            count = reach - max(LONS - wide, wide - 2 * LONS + 1, 0)
            if count > 0:
                found.append((plane, wide, at, count))
                at += count
    return found


def raw_body(low, own, high, out):
    for plane, wide, at, count in raw_chunks():
        ref = (low, own, high)[wide // LONS]
        out[at : at + count, :] = ref[plane, wide % LONS, :count, :]


def inner_body(raw, out, cells):
    span = 4 * LATS
    lane = lax.broadcasted_iota(jnp.int32, (8, span), 1)
    bottom = lax.broadcasted_iota(jnp.int32, (8, span), 0) == 0
    first, last = lane == 0, lane == span - 1
    cells[...] = jnp.zeros(cells.shape, F32)
    order = (5, 6, 8, 9, 10, 11)
    for plane, wide, at, count in raw_chunks():
        for rad in range(4):
            cells[order.index(plane), wide, :count, rad * LATS : (rad + 1) * LATS] = raw[
                rad * RAW + at : rad * RAW + at + count, :
            ]
    w = [None] + [
        weights([cells[2 + d, wide] for d in range(3)], cells[5, wide])
        for wide in range(1, WIDE - 1)
    ]
    made = []
    for part in range(2):
        now = [cells[part, wide] for wide in range(WIDE)]
        for phase in range(PHASES):
            fresh = list(now)
            for wide in range(phase + 1, WIDE - 1 - phase):
                c = now[wide]
                fresh[wide] = blend(
                    w[wide],
                    c,
                    jnp.where(bottom, 0.0, pltpu.roll(c, 1, axis=0)),
                    pltpu.roll(c, 7, axis=0),
                    now[wide - 1],
                    now[wide + 1],
                    jnp.where(first, 0.0, pltpu.roll(c, 1, axis=1)),
                    jnp.where(last, 0.0, pltpu.roll(c, span - 1, axis=1)),
                )
            now = fresh
        made.append(now[LONS : 2 * LONS])
    blon, blat = made
    for lon in range(LONS):
        c = blon[lon]
        source = jnp.where(first, 0.0, pltpu.roll(c, 1, axis=1)) - jnp.where(
            last, 0.0, pltpu.roll(c, span - 1, axis=1)
        )
        if lon < LONS - 1:
            source = source + blat[lon + 1]
        if lon > 0:
            source = source - blat[lon - 1]
        for rad in range(4):
            part = slice(rad * LATS, (rad + 1) * LATS)
            at = rad // 2 * 12 + rad % 2 * 4 + lon
            out[at : at + 1, :] = source[0:1, part]
            at = rad // 2 * 12 + 8 + rad % 2
            if lon == 0:
                out[at : at + 1, :] = blat[0][0:1, part]
            if lon == LONS - 1:
                out[at + 2 : at + 3, :] = blat[LONS - 1][0:1, part]


def base_body(spot, sent, out, cond):
    step = LATE - 16
    odd = spot[0] % 2 == 1
    for lon in range(LONS):
        at = 130 + lon
        lines = [sent[rad * SENT + at : rad * SENT + at + 1, :] for rad in range(4)]
        cond[lon : lon + 1, :] = jnp.where(odd, lines[2], lines[0])
        line = jnp.where(odd, lines[3], lines[1])
        out[pl.ds(lon, 32, stride=step), :] = jnp.broadcast_to(line, (32, LATS))
    lane = lax.broadcasted_iota(jnp.int32, (32, LATS), 1)
    owner = lax.broadcasted_iota(jnp.int32, (32, LATS), 0)
    for rad in range(4):
        for row in range(4):
            at = rad * SENT + row * 32
            out[pl.ds(4 + rad * 5 + row, 32, stride=step), :] = sent[at : at + 32, :]
        marks = []
        for slot in range(2):
            at = rad * SENT + 128 + slot
            line = jnp.broadcast_to(sent[at : at + 1, :], (32, LATS))
            marks.append(
                jnp.sum(jnp.where(lane == owner + spot[1] * 32, line, 0.0), axis=1, keepdims=True)
            )
        out[pl.ds(8 + rad * 5, 32, stride=step), :] = jnp.where(lane < 64, marks[0], marks[1])


def join_body(spot, one, two, cond, base, out, head, copies, sems):
    rest = pltpu.make_async_copy(base, out.at[:, pl.ds(16, LATE - 16), :], sems.at[0])
    rest.start()
    source = one[...] + two[...]
    head[:12, :] = jnp.where(spot[0] % 2 == 1, source[12:], source[:12])
    head[12:, :] = cond[...]
    mine = head[...]
    for owner in range(32):
        copies[owner] = mine
    move = pltpu.make_async_copy(copies, out.at[:, pl.ds(0, 16), :], sems.at[1])
    move.start()
    move.wait()
    rest.wait()


def join(spot, one, two, cond, base):
    vmem = pl.BlockSpec(memory_space=pltpu.VMEM)
    plain = pl.BlockSpec(memory_space=pl.ANY)
    return pl.pallas_call(
        join_body,
        out_shape=arr(32, LATE, LATS),
        in_specs=[pl.BlockSpec(memory_space=pltpu.SMEM), vmem, vmem, vmem, plain],
        out_specs=plain,
        scratch_shapes=[
            pltpu.VMEM((16, LATS), F32),
            pltpu.VMEM((32, 16, LATS), F32),
            pltpu.SemaphoreType.DMA((2,)),
        ],
        compiler_params=pltpu.CompilerParams(vmem_limit_bytes=4 * 2**20),
        cost_estimate=pl.CostEstimate(flops=10**5, bytes_accessed=10**6, transcendentals=0),
    )(spot, one, two, cond, base)


def half_body(late, out):
    for owner in range(32):
        out[owner] = late[owner, :HALF, :]


def chunks():
    found = []
    at = 0
    for wide in range(1, WIDE - 1):
        far = max(LONS - wide, wide - 2 * LONS + 1, 0)
        count = PHASES - far
        found.append((wide, at, count))
        at += count
    return found, at


def pack_body(low, own, high, up, down):
    found, rows = chunks()
    for plane in range(PLANES):
        for wide, start, count in found:
            ref = (low, own, high)[wide // LONS]
            up[plane, start : start + count, :] = ref[plane, wide % LONS, SHELLS - count :, :]
            down[plane, start : start + count, :] = ref[plane, wide % LONS, :count, :]
        up[plane, rows:, :] = jnp.zeros((32 - rows, LATS), F32)
        down[plane, rows:, :] = jnp.zeros((32 - rows, LATS), F32)


def main_body(low, own, high, above, below, from_low, from_high, out, cells, w, speeds):
    found, _ = chunks()
    lane = lax.broadcasted_iota(jnp.int32, (TALL, LATS), 1)

    def fill(plane, target):
        strip = jnp.where(lane % 8 < 4, from_low[plane], from_high[plane])
        for wide in range(WIDE):
            ref = (low, own, high)[wide // LONS]
            target[wide, :SHELLS, :LATS] = ref[plane, wide % LONS]
            target[wide, SHELLS:, :LATS] = jnp.zeros((TALL - SHELLS, LATS), F32)
            if 0 < wide < WIDE - 1:
                target[wide, :, LATS:] = halo_lanes(strip, wide)
            else:
                target[wide, :, LATS:] = jnp.zeros((TALL, LATS), F32)
        for wide, start, count in found:
            target[wide, SHELLS : SHELLS + count, :LATS] = above[plane, start : start + count, :]
            target[wide, TALL - count :, :LATS] = below[plane, start : start + count, :]

    for d in range(4):
        fill(FIELDS + d, speeds.at[d])
    for wide in range(1, WIDE - 1):
        made = weights([speeds[d, wide] for d in range(3)], speeds[3, wide])
        for i in range(7):
            w[i, wide] = made[i]

    def one(field, carry):
        fill(field, cells.at[0])
        for phase in range(PHASES):
            old = cells.at[phase % 2]
            new = cells.at[(phase + 1) % 2]
            for wide in range(phase + 1, WIDE - 1 - phase):
                c = old[wide]
                made = blend(
                    [w[i, wide] for i in range(7)],
                    c,
                    pltpu.roll(c, 1, axis=0),
                    pltpu.roll(c, TALL - 1, axis=0),
                    old[wide - 1],
                    old[wide + 1],
                    pltpu.roll(c, 1, axis=1),
                    pltpu.roll(c, 2 * LATS - 1, axis=1),
                )
                if phase == PHASES - 1:
                    out[field, pl.ds(wide - LONS, SHELLS, stride=LONS), :] = made[:SHELLS, :LATS]
                else:
                    new[wide] = made
        return carry

    lax.fori_loop(0, FIELDS, one, 0)


def slot_body(owners, rows, maps, conductance, out):
    count = owners.shape[1]
    here = lax.broadcasted_iota(jnp.int32, (count, count), 0)
    there = lax.broadcasted_iota(jnp.int32, (count, count), 1)
    aimed = (here % 32) * 4 + here // 32 == owners[...]
    earlier = jnp.dot(
        aimed.astype(jnp.bfloat16), (here < there).astype(jnp.bfloat16), preferred_element_type=F32
    )
    cell = maps[...]
    small = (cell & 127).astype(F32).astype(jnp.bfloat16)
    large = (cell >> 7).astype(F32).astype(jnp.bfloat16)
    row = jnp.broadcast_to((rows[...] + 1).astype(F32), (8, count)).astype(jnp.bfloat16)
    marks = []
    lines = []
    for slot in range(2):
        pick = jnp.where(aimed & (earlier == float(slot)), 1.0, 0.0).astype(jnp.bfloat16)
        marks.append(
            lax.dot_general(row, pick, (((1,), (1,)), ((), ())), preferred_element_type=F32) - 1.0
        )
        made = jnp.dot(pick, small, preferred_element_type=F32) + 128.0 * jnp.dot(
            pick, large, preferred_element_type=F32
        )
        lines += [made[:, :128], made[:, 128:]]
    for rad in range(4):
        for j in range(4):
            at = rad * SENT + j * 32
            out[at : at + 32, :] = lines[j][rad * 32 : rad * 32 + 32]
        at = rad * SENT + 128
        out[at : at + 1, :] = marks[0][:1]
        out[at + 1 : at + 2, :] = marks[1][:1]
        out[at + 2 : at + 6, :] = conductance[...]
        out[at + 6 : at + 8, :] = jnp.zeros((2, LATS), F32)


def final_body(spot, late, other, pot, foot, phi, east_w, west_w, north_w, south_w, start, picked, hot):
    devs, rads = 32, 4
    wide = rads * LATS
    lane = lax.broadcasted_iota(jnp.int32, (devs, wide), 1)

    odd = spot[0] % 2

    def gather(at, step):
        found = []
        for rad in range(rads):
            row = at + rad % 2 * step
            mine = late[pl.ds(row, devs, stride=LATE), :]
            theirs = other[pl.ds(row, devs, stride=HALF), :]
            found.append(jnp.where(odd == rad // 2, mine, theirs))
        return jnp.concatenate(found, axis=1)

    def lon_up(values, lon):
        return values[lon + 1] if lon < LONS - 1 else pltpu.roll(values[0], devs - 1, axis=0)

    def lon_down(values, lon):
        return values[lon - 1] if lon > 0 else pltpu.roll(values[LONS - 1], 1, axis=0)

    def lat_up(value):
        return pltpu.roll(value, wide - 1, axis=1)

    def lat_down(value):
        return pltpu.roll(value, 1, axis=1)

    cond = [gather(12 + lon, 4) for lon in range(LONS)]
    sources = [gather(lon, 4) for lon in range(LONS)]
    sources[LONS - 1] += pltpu.roll(gather(8, 1), devs - 1, axis=0)
    sources[0] -= pltpu.roll(gather(10, 1), 1, axis=0)
    last, first = lane == wide - 1, lane == 0
    for lon in range(LONS):
        source = sources[lon]
        c = cond[lon]
        east = 0.5 * (c + lon_up(cond, lon))
        west = 0.5 * (c + lon_down(cond, lon))
        north = 0.5 * (c + jnp.where(last, 0.0, lat_up(c)))
        south = 0.5 * (c + jnp.where(first, 0.0, lat_down(c)))
        scale = RELAX / (DAMPING * c + east + west + north + south)
        east_w[lon] = east * scale
        west_w[lon] = west * scale
        north_w[lon] = jnp.where(last, 0.0, north * scale)
        south_w[lon] = jnp.where(first, 0.0, south * scale)
        start[lon] = source * scale
        phi[0, lon] = source * scale

    def sweep(old, new):
        values = [phi[old, lon] for lon in range(LONS)]
        for lon in range(LONS):
            c = values[lon]
            phi[new, lon] = (
                (1.0 - RELAX) * c
                + start[lon]
                + (east_w[lon] * lon_up(values, lon) + west_w[lon] * lon_down(values, lon))
                + (north_w[lon] * lat_up(c) + south_w[lon] * lat_down(c))
            )

    for turn in range(SWEEPS - 1):
        sweep(turn % 2, (turn + 1) % 2)
    done = (SWEEPS - 1) % 2
    at_lon = lax.broadcasted_iota(jnp.int32, (devs, LATS), 0) == spot[2]
    for rad in range(rads):

        @pl.when(spot[1] == rad)
        def _():
            for lon in range(LONS):
                block = phi[done, lon, :, rad * LATS : (rad + 1) * LATS]
                pot[lon : lon + 1, :] = jnp.sum(
                    jnp.where(at_lon, block, 0.0), axis=0, keepdims=True
                )

    slot_lane = lax.broadcasted_iota(jnp.int32, (devs, LATS), 1).astype(F32)
    for rad in range(rads):
        table = [phi[done, lon, :, rad * LATS : (rad + 1) * LATS] for lon in range(LONS)]
        marks = late[pl.ds(20 + rad * 5 + 4, devs, stride=LATE), :]
        for slot in range(2):
            at = (slot * rads + rad) * devs
            row = marks if slot == 0 else pltpu.roll(marks, 64, axis=1)
            hot[at : at + devs, :] = jnp.where(row == slot_lane, 1.0, 0.0)
            for half in range(2):
                cell = late[pl.ds(20 + rad * 5 + 2 * slot + half, devs, stride=LATE), :].astype(jnp.int32)
                place, lon_at = cell & 127, cell >> 7
                value = jnp.zeros((devs, LATS), F32)
                for lon in range(LONS):
                    found = jnp.take_along_axis(
                        table[lon], place, axis=1, mode="promise_in_bounds"
                    )
                    value = jnp.where(lon_at == lon, found, value)
                picked[at : at + devs, 128 * half : 128 * half + 128] = value
    summed = lax.dot_general(
        hot[...],
        picked[...],
        (((0,), (0,)), ((), ())),
        precision=lax.Precision.HIGHEST,
        preferred_element_type=F32,
    )
    foot[...] = summed[:ROWS_OWN]


def shards(plasma_fields, velocity, resistivity, conductance, foot_map, foot_owner, foot_row):
    spot = jnp.stack([lax.axis_index("sec"), lax.axis_index("rad"), lax.axis_index("lon")])
    own, slots = first(
        plasma_fields.reshape(FIELDS, SHELLS * LONS, LATS),
        velocity,
        resistivity,
        foot_owner.reshape(1, -1),
        foot_row.reshape(1, -1),
        foot_map,
        conductance,
    )
    low = lax.ppermute(own, "lon", shift("lon", 1, True))
    high = lax.ppermute(own, "lon", shift("lon", -1, True))

    sent = lax.all_to_all(
        slots.reshape(4, SENT, LATS), "rad", split_axis=0, concat_axis=0, tiled=True
    )

    low, high, sent = lax.optimization_barrier((low, high, sent))
    up, down = call(pack_body, (arr(PLANES, 32, LATS), arr(PLANES, 32, LATS)), (low, own, high))
    above = lax.ppermute(down, "sec", shift("sec", -1, False))
    below = lax.ppermute(up, "sec", shift("sec", 1, False))
    raw = call(raw_body, arr(RAW, LATS), (low, own, high))
    owner = lax.axis_index("sec") == 0

    def advance_inner(rows):
        gathered = lax.all_gather(rows, "rad")
        return call(
            inner_body,
            arr(24, LATS),
            (gathered.reshape(4 * RAW, LATS),),
            scratch=(pltpu.VMEM((6, WIDE, 8, 4 * LATS), F32),),
        )

    inner = lax.cond(owner, advance_inner, lambda rows: jnp.zeros((24, LATS), F32), raw)
    inner, below, above = lax.optimization_barrier((inner, below, above))
    far = lax.ppermute(inner, "sec", [(0, 3)])
    far = inner + far
    near = lax.ppermute(far, "sec", [(0, 1), (3, 2)])
    base, cond = call(
        base_body,
        (arr(32 * (LATE - 16), LATS), arr(LONS, LATS)),
        (spot, sent.reshape(4 * SENT, LATS)),
        smem=(0,),
    )
    late = join(spot, far, near, cond, base.reshape(32, LATE - 16, LATS))
    late, low, high = lax.optimization_barrier((late, low, high))

    blocks = (low, own, high, above, below)
    edges = call(
        edge_body,
        arr(PLANES, TALL, LATS),
        blocks,
        scratch=(pltpu.VMEM((PLANES, WIDE, TALL, LATS), F32),),
    )
    from_low = lax.ppermute(edges, "rad", shift("rad", 1, False))
    from_high = lax.ppermute(edges, "rad", shift("rad", -1, False))
    late = lax.all_to_all(
        late, "lon", split_axis=0, concat_axis=0, tiled=True
    )

    advanced = call(
        main_body,
        arr(FIELDS, SHELLS * LONS, LATS),
        blocks + (from_low, from_high),
        scratch=(
            pltpu.VMEM((2, WIDE, TALL, 2 * LATS), F32),
            pltpu.VMEM((7, WIDE, TALL, 2 * LATS), F32),
            pltpu.VMEM((4, WIDE, TALL, 2 * LATS), F32),
        ),
    ).reshape(FIELDS, SHELLS, LONS, LATS)

    late, advanced = lax.optimization_barrier((late, advanced))
    other = lax.ppermute(
        call(half_body, arr(32, HALF, LATS), (late,)), "sec", [(0, 1), (1, 0), (2, 3), (3, 2)]
    )
    plane = pltpu.VMEM((LONS, 32, 4 * LATS), F32)
    potential, foot_table = call(
        final_body,
        (arr(LONS, LATS), arr(ROWS_OWN, 256)),
        (spot, late.reshape(32 * LATE, LATS), other.reshape(32 * HALF, LATS)),
        scratch=(
            pltpu.VMEM((2, LONS, 32, 4 * LATS), F32),
            plane,
            plane,
            plane,
            plane,
            plane,
            pltpu.VMEM((256, 256), F32),
            pltpu.VMEM((256, 128), F32),
        ),
        smem=(0,),
    )
    return (advanced, potential, foot_table)


def solution(mesh):
    in_specs = (
        P(None, "sec", "lon", "rad"),
        P(None, "sec", "lon", "rad"),
        P("sec", "lon", "rad"),
        P("lon", "rad"),
        P(("lon", "sec", "rad"), None),
        P(("lon", "sec", "rad"), None),
        P(("lon", "sec", "rad")),
    )
    out_specs = (P(None, "sec", "lon", "rad"), P("lon", "rad"), P(("lon", "sec", "rad"), None))
    return jax.shard_map(shards, mesh=mesh, in_specs=in_specs, out_specs=out_specs, check_vma=False)
```

```python
import jax
import jax.numpy as jnp
from jax import lax
from jax.experimental import pallas as pl
from jax.experimental.pallas import tpu as pltpu
from jax.sharding import PartitionSpec as P

PHASES = 4
SWEEPS = 8
ROWS_OWN = 32
COURANT = 0.25
DAMPING = 0.05
RELAX = 0.8

FIELDS = 8
PLANES = FIELDS + 4
SHELLS = 16
LONS = 4
LATS = 128
WIDE = 3 * LONS
LATE = 40
HALF = 20
RAW = 192
SENT = 136
TALL = SHELLS + 2 * PHASES
F32 = jnp.float32


def call(body, out_shape, args, scratch=(), smem=(), flops=10**6, traffic=10**6):
    specs = [
        pl.BlockSpec(memory_space=pltpu.SMEM if i in smem else pltpu.VMEM)
        for i in range(len(args))
    ]
    many = isinstance(out_shape, (tuple, list))
    vmem = pl.BlockSpec(memory_space=pltpu.VMEM)
    return pl.pallas_call(
        body,
        out_shape=out_shape,
        in_specs=specs,
        out_specs=[vmem] * len(out_shape) if many else vmem,
        scratch_shapes=list(scratch),
        compiler_params=pltpu.CompilerParams(vmem_limit_bytes=16 * 2**20),
        cost_estimate=pl.CostEstimate(flops=flops, bytes_accessed=traffic, transcendentals=0),
    )(*args)


def arr(*shape):
    return jax.ShapeDtypeStruct(shape, F32)


def shift(axis, step, closed):
    count = lax.axis_size(axis)
    return [
        (i, (i + step) % count) for i in range(count) if closed or 0 <= i + step < count
    ]


def first_body(*refs):
    sources, (own, slots, plain), held, sems = refs[:7], refs[7:10], refs[10:17], refs[17]
    moves = [
        pltpu.make_async_copy(source, target, sems.at[i])
        for i, (source, target) in enumerate(zip(sources, held))
    ]
    for move in moves:
        move.start()
    fields, speeds, resist, owners, rows, maps, conductance = held
    for move in moves[1:3]:
        move.wait()
    for plane in range(4):
        for shell in range(SHELLS):
            found = speeds[plane, shell] if plane < 3 else resist[shell]
            plain[plane, shell * LONS : shell * LONS + LONS, :] = found.astype(F32)
    moves[0].wait()
    for plane in range(PLANES):
        for lon in range(LONS):
            at = pl.ds(lon, SHELLS, stride=LONS)
            if plane < FIELDS:
                own[plane, lon] = fields[plane, at, :]
            else:
                own[plane, lon] = plain[plane - FIELDS, at, :]
    for move in moves[3:]:
        move.wait()
    slot_body(owners, rows, maps, conductance, slots)


def first(*args):
    vmem = pl.BlockSpec(memory_space=pltpu.VMEM)
    return pl.pallas_call(
        first_body,
        out_shape=(arr(PLANES, LONS, SHELLS, LATS), arr(4 * SENT, LATS)),
        in_specs=[pl.BlockSpec(memory_space=pltpu.HBM)] * len(args),
        out_specs=[vmem, vmem],
        scratch_shapes=[pltpu.VMEM((4, SHELLS * LONS, LATS), F32)]
        + [pltpu.VMEM(arg.shape, arg.dtype) for arg in args]
        + [pltpu.SemaphoreType.DMA((len(args),))],
        compiler_params=pltpu.CompilerParams(vmem_limit_bytes=60 * 2**20),
        cost_estimate=pl.CostEstimate(flops=10**6, bytes_accessed=10**6, transcendentals=0),
    )(*args)


def edge_body(low, own, high, above, below, edges, tall):
    found, _ = chunks()
    group = lax.broadcasted_iota(jnp.int32, (TALL, LATS), 1) // 8
    for plane in range(PLANES):
        for wide in range(WIDE):
            ref = (low, own, high)[wide // LONS]
            tall[plane, wide, :SHELLS, :] = ref[plane, wide % LONS]
            tall[plane, wide, SHELLS:, :] = jnp.zeros((TALL - SHELLS, LATS), F32)
        for wide, start, count in found:
            tall[plane, wide, SHELLS : SHELLS + count, :] = above[plane, start : start + count, :]
            tall[plane, wide, TALL - count :, :] = below[plane, start : start + count, :]
    for plane in range(PLANES):
        packed = jnp.zeros((TALL, LATS), F32)
        for wide in range(1, WIDE - 1):
            turned = pltpu.roll(tall[plane, wide], 8 * wide + 4, axis=1)
            packed = jnp.where(group == wide, turned, packed)
        edges[plane] = packed


def halo_lanes(edges, wide):
    lane = lax.broadcasted_iota(jnp.int32, edges.shape, 1)
    turned = pltpu.roll(edges, (LATS - 8 * wide - 4) % LATS, axis=1)
    return jnp.where((lane < 4) | (lane >= LATS - 4), turned, 0.0)


def weights(speeds, resist):
    out = []
    total = None
    for speed in speeds:
        lower = COURANT * jnp.maximum(speed, 0.0) + resist
        upper = resist - COURANT * jnp.minimum(speed, 0.0)
        out += [lower, upper]
        total = lower + upper if total is None else total + lower + upper
    return [1.0 - total] + out


def blend(w, centre, shell_lo, shell_hi, lon_lo, lon_hi, lat_lo, lat_hi):
    return (
        w[0] * centre
        + (w[1] * shell_lo + w[2] * shell_hi)
        + (w[3] * lon_lo + w[4] * lon_hi)
        + (w[5] * lat_lo + w[6] * lat_hi)
    )


def raw_chunks():
    found = []
    at = 0
    for plane in (5, 6, 8, 9, 10, 11):
        reach = PHASES + 1 if plane < FIELDS else PHASES
        for wide in range(WIDE):
            count = reach - max(LONS - wide, wide - 2 * LONS + 1, 0)
            if count > 0:
                found.append((plane, wide, at, count))
                at += count
    return found


def raw_body(low, own, high, out):
    for plane, wide, at, count in raw_chunks():
        ref = (low, own, high)[wide // LONS]
        out[at : at + count, :] = ref[plane, wide % LONS, :count, :]


def inner_body(raw, out, cells):
    span = 4 * LATS
    lane = lax.broadcasted_iota(jnp.int32, (8, span), 1)
    bottom = lax.broadcasted_iota(jnp.int32, (8, span), 0) == 0
    first, last = lane == 0, lane == span - 1
    cells[...] = jnp.zeros(cells.shape, F32)
    order = (5, 6, 8, 9, 10, 11)
    for plane, wide, at, count in raw_chunks():
        for rad in range(4):
            cells[order.index(plane), wide, :count, rad * LATS : (rad + 1) * LATS] = raw[
                rad * RAW + at : rad * RAW + at + count, :
            ]
    w = [None] + [
        weights([cells[2 + d, wide] for d in range(3)], cells[5, wide])
        for wide in range(1, WIDE - 1)
    ]
    made = []
    for part in range(2):
        now = [cells[part, wide] for wide in range(WIDE)]
        for phase in range(PHASES):
            fresh = list(now)
            for wide in range(phase + 1, WIDE - 1 - phase):
                c = now[wide]
                fresh[wide] = blend(
                    w[wide],
                    c,
                    jnp.where(bottom, 0.0, pltpu.roll(c, 1, axis=0)),
                    pltpu.roll(c, 7, axis=0),
                    now[wide - 1],
                    now[wide + 1],
                    jnp.where(first, 0.0, pltpu.roll(c, 1, axis=1)),
                    jnp.where(last, 0.0, pltpu.roll(c, span - 1, axis=1)),
                )
            now = fresh
        made.append(now[LONS : 2 * LONS])
    blon, blat = made
    for lon in range(LONS):
        c = blon[lon]
        source = jnp.where(first, 0.0, pltpu.roll(c, 1, axis=1)) - jnp.where(
            last, 0.0, pltpu.roll(c, span - 1, axis=1)
        )
        if lon < LONS - 1:
            source = source + blat[lon + 1]
        if lon > 0:
            source = source - blat[lon - 1]
        for rad in range(4):
            part = slice(rad * LATS, (rad + 1) * LATS)
            at = rad // 2 * 12 + rad % 2 * 4 + lon
            out[at : at + 1, :] = source[0:1, part]
            at = rad // 2 * 12 + 8 + rad % 2
            if lon == 0:
                out[at : at + 1, :] = blat[0][0:1, part]
            if lon == LONS - 1:
                out[at + 2 : at + 3, :] = blat[LONS - 1][0:1, part]


def base_body(spot, sent, out, cond):
    step = LATE - 16
    odd = spot[0] % 2 == 1
    for lon in range(LONS):
        at = 130 + lon
        lines = [sent[rad * SENT + at : rad * SENT + at + 1, :] for rad in range(4)]
        cond[lon : lon + 1, :] = jnp.where(odd, lines[2], lines[0])
        line = jnp.where(odd, lines[3], lines[1])
        out[pl.ds(lon, 32, stride=step), :] = jnp.broadcast_to(line, (32, LATS))
    lane = lax.broadcasted_iota(jnp.int32, (32, LATS), 1)
    owner = lax.broadcasted_iota(jnp.int32, (32, LATS), 0)
    for rad in range(4):
        for row in range(4):
            at = rad * SENT + row * 32
            out[pl.ds(4 + rad * 5 + row, 32, stride=step), :] = sent[at : at + 32, :]
        marks = []
        for slot in range(2):
            at = rad * SENT + 128 + slot
            line = jnp.broadcast_to(sent[at : at + 1, :], (32, LATS))
            marks.append(
                jnp.sum(jnp.where(lane == owner + spot[1] * 32, line, 0.0), axis=1, keepdims=True)
            )
        out[pl.ds(8 + rad * 5, 32, stride=step), :] = jnp.where(lane < 64, marks[0], marks[1])


def join_body(spot, one, two, cond, base, out, head, copies, sems):
    rest = pltpu.make_async_copy(base, out.at[:, pl.ds(16, LATE - 16), :], sems.at[0])
    rest.start()
    source = one[...] + two[...]
    head[:12, :] = jnp.where(spot[0] % 2 == 1, source[12:], source[:12])
    head[12:, :] = cond[...]
    mine = head[...]
    for owner in range(32):
        copies[owner] = mine
    move = pltpu.make_async_copy(copies, out.at[:, pl.ds(0, 16), :], sems.at[1])
    move.start()
    move.wait()
    rest.wait()


def join(spot, one, two, cond, base):
    vmem = pl.BlockSpec(memory_space=pltpu.VMEM)
    plain = pl.BlockSpec(memory_space=pl.ANY)
    return pl.pallas_call(
        join_body,
        out_shape=arr(32, LATE, LATS),
        in_specs=[pl.BlockSpec(memory_space=pltpu.SMEM), vmem, vmem, vmem, plain],
        out_specs=plain,
        scratch_shapes=[
            pltpu.VMEM((16, LATS), F32),
            pltpu.VMEM((32, 16, LATS), F32),
            pltpu.SemaphoreType.DMA((2,)),
        ],
        compiler_params=pltpu.CompilerParams(vmem_limit_bytes=4 * 2**20),
        cost_estimate=pl.CostEstimate(flops=10**5, bytes_accessed=10**6, transcendentals=0),
    )(spot, one, two, cond, base)


def half_body(late, out):
    for row in range(HALF):
        out[row] = late[pl.ds(row, 32, stride=LATE), :]


def mark_body(late, cells, hot):
    lane = lax.broadcasted_iota(jnp.int32, (32, LATS), 1).astype(F32)
    for rad in range(4):
        marks = late[pl.ds(HALF + rad * 5 + 4, 32, stride=LATE), :]
        for slot in range(2):
            row = marks if slot == 0 else pltpu.roll(marks, 64, axis=1)
            at = (slot * 4 + rad) * 32
            hot[at : at + 32, :] = jnp.where(row == lane, 1.0, 0.0)
            for half in range(2):
                cells[(rad * 2 + slot) * 2 + half] = late[
                    pl.ds(HALF + rad * 5 + 2 * slot + half, 32, stride=LATE), :
                ].astype(jnp.int32)


def chunks():
    found = []
    at = 0
    for wide in range(1, WIDE - 1):
        far = max(LONS - wide, wide - 2 * LONS + 1, 0)
        count = PHASES - far
        found.append((wide, at, count))
        at += count
    return found, at


def pack_body(low, own, high, up, down):
    found, rows = chunks()
    for plane in range(PLANES):
        for wide, start, count in found:
            ref = (low, own, high)[wide // LONS]
            up[plane, start : start + count, :] = ref[plane, wide % LONS, SHELLS - count :, :]
            down[plane, start : start + count, :] = ref[plane, wide % LONS, :count, :]
        up[plane, rows:, :] = jnp.zeros((32 - rows, LATS), F32)
        down[plane, rows:, :] = jnp.zeros((32 - rows, LATS), F32)


def main_body(low, own, high, above, below, from_low, from_high, out, cells, w, speeds):
    found, _ = chunks()
    lane = lax.broadcasted_iota(jnp.int32, (TALL, LATS), 1)

    def fill(plane, target):
        strip = jnp.where(lane % 8 < 4, from_low[plane], from_high[plane])
        for wide in range(WIDE):
            ref = (low, own, high)[wide // LONS]
            target[wide, :SHELLS, :LATS] = ref[plane, wide % LONS]
            target[wide, SHELLS:, :LATS] = jnp.zeros((TALL - SHELLS, LATS), F32)
            if 0 < wide < WIDE - 1:
                target[wide, :, LATS:] = halo_lanes(strip, wide)
            else:
                target[wide, :, LATS:] = jnp.zeros((TALL, LATS), F32)
        for wide, start, count in found:
            target[wide, SHELLS : SHELLS + count, :LATS] = above[plane, start : start + count, :]
            target[wide, TALL - count :, :LATS] = below[plane, start : start + count, :]

    for d in range(4):
        fill(FIELDS + d, speeds.at[d])
    for wide in range(1, WIDE - 1):
        made = weights([speeds[d, wide] for d in range(3)], speeds[3, wide])
        for i in range(7):
            w[i, wide] = made[i]

    def one(field, carry):
        fill(field, cells.at[0])
        for phase in range(PHASES):
            old = cells.at[phase % 2]
            new = cells.at[(phase + 1) % 2]
            for wide in range(phase + 1, WIDE - 1 - phase):
                c = old[wide]
                made = blend(
                    [w[i, wide] for i in range(7)],
                    c,
                    pltpu.roll(c, 1, axis=0),
                    pltpu.roll(c, TALL - 1, axis=0),
                    old[wide - 1],
                    old[wide + 1],
                    pltpu.roll(c, 1, axis=1),
                    pltpu.roll(c, 2 * LATS - 1, axis=1),
                )
                if phase == PHASES - 1:
                    out[field, pl.ds(wide - LONS, SHELLS, stride=LONS), :] = made[:SHELLS, :LATS]
                else:
                    new[wide] = made
        return carry

    lax.fori_loop(0, FIELDS, one, 0)


def slot_body(owners, rows, maps, conductance, out):
    count = owners.shape[1]
    here = lax.broadcasted_iota(jnp.int32, (count, count), 0)
    there = lax.broadcasted_iota(jnp.int32, (count, count), 1)
    aimed = (here % 32) * 4 + here // 32 == owners[...]
    earlier = jnp.dot(
        aimed.astype(jnp.bfloat16), (here < there).astype(jnp.bfloat16), preferred_element_type=F32
    )
    cell = maps[...]
    small = (cell & 127).astype(F32).astype(jnp.bfloat16)
    large = (cell >> 7).astype(F32).astype(jnp.bfloat16)
    row = jnp.broadcast_to((rows[...] + 1).astype(F32), (8, count)).astype(jnp.bfloat16)
    marks = []
    lines = []
    for slot in range(2):
        pick = jnp.where(aimed & (earlier == float(slot)), 1.0, 0.0).astype(jnp.bfloat16)
        marks.append(
            lax.dot_general(row, pick, (((1,), (1,)), ((), ())), preferred_element_type=F32) - 1.0
        )
        made = jnp.dot(pick, small, preferred_element_type=F32) + 128.0 * jnp.dot(
            pick, large, preferred_element_type=F32
        )
        lines += [made[:, :128], made[:, 128:]]
    for rad in range(4):
        for j in range(4):
            at = rad * SENT + j * 32
            out[at : at + 32, :] = lines[j][rad * 32 : rad * 32 + 32]
        at = rad * SENT + 128
        out[at : at + 1, :] = marks[0][:1]
        out[at + 1 : at + 2, :] = marks[1][:1]
        out[at + 2 : at + 6, :] = conductance[...]
        out[at + 6 : at + 8, :] = jnp.zeros((2, LATS), F32)


def final_body(
    spot, mine, other, cells, hot, pot, foot, phi, east_w, west_w, north_w, south_w, start, picked
):
    devs, rads = 32, 4
    wide = rads * LATS
    lane = lax.broadcasted_iota(jnp.int32, (devs, wide), 1)

    odd = spot[0] % 2

    def gather(at, step):
        found = []
        for rad in range(rads):
            row = at + rad % 2 * step
            found.append(jnp.where(odd == rad // 2, mine[row], other[row]))
        return jnp.concatenate(found, axis=1)

    def lon_up(values, lon):
        return values[lon + 1] if lon < LONS - 1 else pltpu.roll(values[0], devs - 1, axis=0)

    def lon_down(values, lon):
        return values[lon - 1] if lon > 0 else pltpu.roll(values[LONS - 1], 1, axis=0)

    def lat_up(value):
        return pltpu.roll(value, wide - 1, axis=1)

    def lat_down(value):
        return pltpu.roll(value, 1, axis=1)

    cond = [gather(12 + lon, 4) for lon in range(LONS)]
    sources = [gather(lon, 4) for lon in range(LONS)]
    sources[LONS - 1] += pltpu.roll(gather(8, 1), devs - 1, axis=0)
    sources[0] -= pltpu.roll(gather(10, 1), 1, axis=0)
    last, first = lane == wide - 1, lane == 0
    for lon in range(LONS):
        source = sources[lon]
        c = cond[lon]
        east = 0.5 * (c + lon_up(cond, lon))
        west = 0.5 * (c + lon_down(cond, lon))
        north = 0.5 * (c + jnp.where(last, 0.0, lat_up(c)))
        south = 0.5 * (c + jnp.where(first, 0.0, lat_down(c)))
        scale = RELAX / (DAMPING * c + east + west + north + south)
        east_w[lon] = east * scale
        west_w[lon] = west * scale
        north_w[lon] = jnp.where(last, 0.0, north * scale)
        south_w[lon] = jnp.where(first, 0.0, south * scale)
        start[lon] = source * scale
        phi[0, lon] = source * scale

    def sweep(old, new):
        values = [phi[old, lon] for lon in range(LONS)]
        for lon in range(LONS):
            c = values[lon]
            phi[new, lon] = (
                (1.0 - RELAX) * c
                + start[lon]
                + (east_w[lon] * lon_up(values, lon) + west_w[lon] * lon_down(values, lon))
                + (north_w[lon] * lat_up(c) + south_w[lon] * lat_down(c))
            )

    for turn in range(SWEEPS - 1):
        sweep(turn % 2, (turn + 1) % 2)
    done = (SWEEPS - 1) % 2
    at_lon = lax.broadcasted_iota(jnp.int32, (devs, LATS), 0) == spot[2]
    for rad in range(rads):

        @pl.when(spot[1] == rad)
        def _():
            for lon in range(LONS):
                block = phi[done, lon, :, rad * LATS : (rad + 1) * LATS]
                pot[lon : lon + 1, :] = jnp.sum(
                    jnp.where(at_lon, block, 0.0), axis=0, keepdims=True
                )

    for rad in range(rads):
        table = [phi[done, lon, :, rad * LATS : (rad + 1) * LATS] for lon in range(LONS)]
        for slot in range(2):
            at = (slot * rads + rad) * devs
            for half in range(2):
                cell = cells[(rad * 2 + slot) * 2 + half]
                place, lon_at = cell & 127, cell >> 7
                value = jnp.zeros((devs, LATS), F32)
                for lon in range(LONS):
                    found = jnp.take_along_axis(
                        table[lon], place, axis=1, mode="promise_in_bounds"
                    )
                    value = jnp.where(lon_at == lon, found, value)
                picked[at : at + devs, 128 * half : 128 * half + 128] = value
    rest = picked[...]
    rows = hot[...].astype(jnp.bfloat16)
    summed = jnp.zeros((LATS, 2 * LATS), F32)
    for part in range(3):
        piece = rest.astype(jnp.bfloat16)
        rest = rest - piece.astype(F32)
        summed = summed + lax.dot_general(
            rows, piece, (((0,), (0,)), ((), ())), preferred_element_type=F32
        )
    foot[...] = summed[:ROWS_OWN]


def shards(plasma_fields, velocity, resistivity, conductance, foot_map, foot_owner, foot_row):
    spot = jnp.stack([lax.axis_index("sec"), lax.axis_index("rad"), lax.axis_index("lon")])
    own, slots = first(
        plasma_fields.reshape(FIELDS, SHELLS * LONS, LATS),
        velocity,
        resistivity,
        foot_owner.reshape(1, -1),
        foot_row.reshape(1, -1),
        foot_map,
        conductance,
    )
    low = lax.ppermute(own, "lon", shift("lon", 1, True))
    high = lax.ppermute(own, "lon", shift("lon", -1, True))

    sent = lax.all_to_all(
        slots.reshape(4, SENT, LATS), "rad", split_axis=0, concat_axis=0, tiled=True
    )

    low, high, sent = lax.optimization_barrier((low, high, sent))
    up, down = call(pack_body, (arr(PLANES, 32, LATS), arr(PLANES, 32, LATS)), (low, own, high))
    above = lax.ppermute(down, "sec", shift("sec", -1, False))
    below = lax.ppermute(up, "sec", shift("sec", 1, False))
    raw = call(raw_body, arr(RAW, LATS), (low, own, high))
    owner = lax.axis_index("sec") == 0

    def advance_inner(rows):
        gathered = lax.all_gather(rows, "rad")
        return call(
            inner_body,
            arr(24, LATS),
            (gathered.reshape(4 * RAW, LATS),),
            scratch=(pltpu.VMEM((6, WIDE, 8, 4 * LATS), F32),),
        )

    inner = lax.cond(owner, advance_inner, lambda rows: jnp.zeros((24, LATS), F32), raw)
    inner, below, above = lax.optimization_barrier((inner, below, above))
    far = lax.ppermute(inner, "sec", [(0, 3)])
    far = inner + far
    near = lax.ppermute(far, "sec", [(0, 1), (3, 2)])
    base, cond = call(
        base_body,
        (arr(32 * (LATE - 16), LATS), arr(LONS, LATS)),
        (spot, sent.reshape(4 * SENT, LATS)),
        smem=(0,),
    )
    late = join(spot, far, near, cond, base.reshape(32, LATE - 16, LATS))
    late, low, high = lax.optimization_barrier((late, low, high))

    blocks = (low, own, high, above, below)
    edges = call(
        edge_body,
        arr(PLANES, TALL, LATS),
        blocks,
        scratch=(pltpu.VMEM((PLANES, WIDE, TALL, LATS), F32),),
    )
    from_low = lax.ppermute(edges, "rad", shift("rad", 1, False))
    from_high = lax.ppermute(edges, "rad", shift("rad", -1, False))
    late = lax.all_to_all(
        late, "lon", split_axis=0, concat_axis=0, tiled=True
    )

    advanced = call(
        main_body,
        arr(FIELDS, SHELLS * LONS, LATS),
        blocks + (from_low, from_high),
        scratch=(
            pltpu.VMEM((2, WIDE, TALL, 2 * LATS), F32),
            pltpu.VMEM((7, WIDE, TALL, 2 * LATS), F32),
            pltpu.VMEM((4, WIDE, TALL, 2 * LATS), F32),
        ),
    ).reshape(FIELDS, SHELLS, LONS, LATS)

    late, advanced = lax.optimization_barrier((late, advanced))
    late = late.reshape(32 * LATE, LATS)
    mine = call(half_body, arr(HALF, 32, LATS), (late,))
    other = lax.ppermute(mine, "sec", [(0, 1), (1, 0), (2, 3), (3, 2)])
    cells, hot = call(
        mark_body,
        (jax.ShapeDtypeStruct((16, 32, LATS), jnp.int32), arr(256, LATS)),
        (late,),
    )
    plane = pltpu.VMEM((LONS, 32, 4 * LATS), F32)
    potential, foot_table = call(
        final_body,
        (arr(LONS, LATS), arr(ROWS_OWN, 256)),
        (spot, mine, other, cells, hot),
        scratch=(
            pltpu.VMEM((2, LONS, 32, 4 * LATS), F32),
            plane,
            plane,
            plane,
            plane,
            plane,
            pltpu.VMEM((256, 256), F32),
        ),
        smem=(0,),
    )
    return (advanced, potential, foot_table)


def solution(mesh):
    in_specs = (
        P(None, "sec", "lon", "rad"),
        P(None, "sec", "lon", "rad"),
        P("sec", "lon", "rad"),
        P("lon", "rad"),
        P(("lon", "sec", "rad"), None),
        P(("lon", "sec", "rad"), None),
        P(("lon", "sec", "rad")),
    )
    out_specs = (P(None, "sec", "lon", "rad"), P("lon", "rad"), P(("lon", "sec", "rad"), None))
    return jax.shard_map(shards, mesh=mesh, in_specs=in_specs, out_specs=out_specs, check_vma=False)
```

```python
import jax
import jax.numpy as jnp
from jax import lax
from jax.experimental import pallas as pl
from jax.experimental.pallas import tpu as pltpu
from jax.sharding import PartitionSpec as P

PHASES = 4
SWEEPS = 8
ROWS_OWN = 32
COURANT = 0.25
DAMPING = 0.05
RELAX = 0.8

FIELDS = 8
PLANES = FIELDS + 4
SHELLS = 16
LONS = 4
LATS = 128
WIDE = 3 * LONS
LATE = 40
HALF = 20
RAW = 192
SENT = 136
TALL = SHELLS + 2 * PHASES
F32 = jnp.float32


def call(body, out_shape, args, scratch=(), smem=(), flops=10**6, traffic=10**6):
    specs = [
        pl.BlockSpec(memory_space=pltpu.SMEM if i in smem else pltpu.VMEM)
        for i in range(len(args))
    ]
    many = isinstance(out_shape, (tuple, list))
    vmem = pl.BlockSpec(memory_space=pltpu.VMEM)
    return pl.pallas_call(
        body,
        out_shape=out_shape,
        in_specs=specs,
        out_specs=[vmem] * len(out_shape) if many else vmem,
        scratch_shapes=list(scratch),
        compiler_params=pltpu.CompilerParams(vmem_limit_bytes=16 * 2**20),
        cost_estimate=pl.CostEstimate(flops=flops, bytes_accessed=traffic, transcendentals=0),
    )(*args)


def arr(*shape):
    return jax.ShapeDtypeStruct(shape, F32)


def shift(axis, step, closed):
    count = lax.axis_size(axis)
    return [
        (i, (i + step) % count) for i in range(count) if closed or 0 <= i + step < count
    ]


def first_body(*refs):
    sources, (staged, slots, plain, own), held, sems = refs[:7], refs[7:11], refs[11:18], refs[18]
    moves = [
        pltpu.make_async_copy(source, target, sems.at[i])
        for i, (source, target) in enumerate(zip(sources, held))
    ]
    for move in moves:
        move.start()
    fields, speeds, resist, owners, rows, maps, conductance = held
    for move in moves[1:3]:
        move.wait()
    for plane in range(4):
        for shell in range(SHELLS):
            found = speeds[plane, shell] if plane < 3 else resist[shell]
            plain[plane, shell * LONS : shell * LONS + LONS, :] = found.astype(F32)
    moves[0].wait()
    for plane in range(PLANES):
        for lon in range(LONS):
            at = pl.ds(lon, SHELLS, stride=LONS)
            if plane < FIELDS:
                own[plane, lon] = fields[plane, at, :]
            else:
                own[plane, lon] = plain[plane - FIELDS, at, :]
    leave = pltpu.make_async_copy(own, staged, sems.at[7])
    leave.start()
    for move in moves[3:]:
        move.wait()
    slot_body(owners, rows, maps, conductance, slots)
    leave.wait()


def first(*args):
    vmem = pl.BlockSpec(memory_space=pltpu.VMEM)
    return pl.pallas_call(
        first_body,
        out_shape=(arr(PLANES, LONS, SHELLS, LATS), arr(4 * SENT, LATS)),
        in_specs=[pl.BlockSpec(memory_space=pltpu.HBM)] * len(args),
        out_specs=[pl.BlockSpec(memory_space=pl.ANY), vmem],
        scratch_shapes=[
            pltpu.VMEM((4, SHELLS * LONS, LATS), F32),
            pltpu.VMEM((PLANES, LONS, SHELLS, LATS), F32),
        ]
        + [pltpu.VMEM(arg.shape, arg.dtype) for arg in args]
        + [pltpu.SemaphoreType.DMA((len(args) + 1,))],
        compiler_params=pltpu.CompilerParams(vmem_limit_bytes=60 * 2**20),
        cost_estimate=pl.CostEstimate(flops=10**6, bytes_accessed=10**6, transcendentals=0),
    )(*args)


def edge_body(low, own, high, above, below, edges, tall):
    found, _ = chunks()
    group = lax.broadcasted_iota(jnp.int32, (TALL, LATS), 1) // 8
    for plane in range(PLANES):
        for wide in range(WIDE):
            ref = (low, own, high)[wide // LONS]
            tall[plane, wide, :SHELLS, :] = ref[plane, wide % LONS]
            tall[plane, wide, SHELLS:, :] = jnp.zeros((TALL - SHELLS, LATS), F32)
        for wide, start, count in found:
            tall[plane, wide, SHELLS : SHELLS + count, :] = above[plane, start : start + count, :]
            tall[plane, wide, TALL - count :, :] = below[plane, start : start + count, :]
    for plane in range(PLANES):
        packed = jnp.zeros((TALL, LATS), F32)
        for wide in range(1, WIDE - 1):
            turned = pltpu.roll(tall[plane, wide], 8 * wide + 4, axis=1)
            packed = jnp.where(group == wide, turned, packed)
        edges[plane] = packed


def halo_lanes(edges, wide):
    lane = lax.broadcasted_iota(jnp.int32, edges.shape, 1)
    turned = pltpu.roll(edges, (LATS - 8 * wide - 4) % LATS, axis=1)
    return jnp.where((lane < 4) | (lane >= LATS - 4), turned, 0.0)


def weights(speeds, resist):
    out = []
    total = None
    for speed in speeds:
        lower = COURANT * jnp.maximum(speed, 0.0) + resist
        upper = resist - COURANT * jnp.minimum(speed, 0.0)
        out += [lower, upper]
        total = lower + upper if total is None else total + lower + upper
    return [1.0 - total] + out


def blend(w, centre, shell_lo, shell_hi, lon_lo, lon_hi, lat_lo, lat_hi):
    return (
        w[0] * centre
        + (w[1] * shell_lo + w[2] * shell_hi)
        + (w[3] * lon_lo + w[4] * lon_hi)
        + (w[5] * lat_lo + w[6] * lat_hi)
    )


def raw_chunks():
    found = []
    at = 0
    for plane in (5, 6, 8, 9, 10, 11):
        reach = PHASES + 1 if plane < FIELDS else PHASES
        for wide in range(WIDE):
            count = reach - max(LONS - wide, wide - 2 * LONS + 1, 0)
            if count > 0:
                found.append((plane, wide, at, count))
                at += count
    return found


def raw_body(low, own, high, out):
    for plane, wide, at, count in raw_chunks():
        ref = (low, own, high)[wide // LONS]
        out[at : at + count, :] = ref[plane, wide % LONS, :count, :]


def inner_body(raw, out, cells):
    span = 4 * LATS
    lane = lax.broadcasted_iota(jnp.int32, (8, span), 1)
    bottom = lax.broadcasted_iota(jnp.int32, (8, span), 0) == 0
    first, last = lane == 0, lane == span - 1
    cells[...] = jnp.zeros(cells.shape, F32)
    order = (5, 6, 8, 9, 10, 11)
    for plane, wide, at, count in raw_chunks():
        for rad in range(4):
            cells[order.index(plane), wide, :count, rad * LATS : (rad + 1) * LATS] = raw[
                rad * RAW + at : rad * RAW + at + count, :
            ]
    w = [None] + [
        weights([cells[2 + d, wide] for d in range(3)], cells[5, wide])
        for wide in range(1, WIDE - 1)
    ]
    made = []
    for part in range(2):
        now = [cells[part, wide] for wide in range(WIDE)]
        for phase in range(PHASES):
            fresh = list(now)
            for wide in range(phase + 1, WIDE - 1 - phase):
                c = now[wide]
                fresh[wide] = blend(
                    w[wide],
                    c,
                    jnp.where(bottom, 0.0, pltpu.roll(c, 1, axis=0)),
                    pltpu.roll(c, 7, axis=0),
                    now[wide - 1],
                    now[wide + 1],
                    jnp.where(first, 0.0, pltpu.roll(c, 1, axis=1)),
                    jnp.where(last, 0.0, pltpu.roll(c, span - 1, axis=1)),
                )
            now = fresh
        made.append(now[LONS : 2 * LONS])
    blon, blat = made
    for lon in range(LONS):
        c = blon[lon]
        source = jnp.where(first, 0.0, pltpu.roll(c, 1, axis=1)) - jnp.where(
            last, 0.0, pltpu.roll(c, span - 1, axis=1)
        )
        if lon < LONS - 1:
            source = source + blat[lon + 1]
        if lon > 0:
            source = source - blat[lon - 1]
        for rad in range(4):
            part = slice(rad * LATS, (rad + 1) * LATS)
            at = rad // 2 * 12 + rad % 2 * 4 + lon
            out[at : at + 1, :] = source[0:1, part]
            at = rad // 2 * 12 + 8 + rad % 2
            if lon == 0:
                out[at : at + 1, :] = blat[0][0:1, part]
            if lon == LONS - 1:
                out[at + 2 : at + 3, :] = blat[LONS - 1][0:1, part]


def base_body(spot, sent, out, cond):
    odd = spot[0] % 2 == 1
    for row in range(16):
        out[pl.ds(row, 32, stride=LATE), :] = jnp.zeros((32, LATS), F32)
    for lon in range(LONS):
        at = 130 + lon
        lines = [sent[rad * SENT + at : rad * SENT + at + 1, :] for rad in range(4)]
        cond[lon : lon + 1, :] = jnp.where(odd, lines[2], lines[0])
        line = jnp.where(odd, lines[3], lines[1])
        out[pl.ds(16 + lon, 32, stride=LATE), :] = jnp.broadcast_to(line, (32, LATS))
    lane = lax.broadcasted_iota(jnp.int32, (32, LATS), 1)
    owner = lax.broadcasted_iota(jnp.int32, (32, LATS), 0)
    for rad in range(4):
        for row in range(4):
            at = rad * SENT + row * 32
            out[pl.ds(20 + rad * 5 + row, 32, stride=LATE), :] = sent[at : at + 32, :]
        marks = []
        for slot in range(2):
            at = rad * SENT + 128 + slot
            line = jnp.broadcast_to(sent[at : at + 1, :], (32, LATS))
            marks.append(
                jnp.sum(jnp.where(lane == owner + spot[1] * 32, line, 0.0), axis=1, keepdims=True)
            )
        out[pl.ds(24 + rad * 5, 32, stride=LATE), :] = jnp.where(lane < 64, marks[0], marks[1])


def join_body(spot, one, two, cond, base, out, head, copies, sem):
    source = one[...] + two[...]
    head[:12, :] = jnp.where(spot[0] % 2 == 1, source[12:], source[:12])
    head[12:, :] = cond[...]
    mine = head[...]
    for owner in range(32):
        copies[owner] = mine
    move = pltpu.make_async_copy(copies, out.at[:, pl.ds(0, 16), :], sem)
    move.start()
    move.wait()


def join(spot, one, two, cond, base):
    vmem = pl.BlockSpec(memory_space=pltpu.VMEM)
    plain = pl.BlockSpec(memory_space=pl.ANY)
    return pl.pallas_call(
        join_body,
        out_shape=arr(32, LATE, LATS),
        in_specs=[pl.BlockSpec(memory_space=pltpu.SMEM), vmem, vmem, vmem, plain],
        out_specs=plain,
        scratch_shapes=[
            pltpu.VMEM((16, LATS), F32),
            pltpu.VMEM((32, 16, LATS), F32),
            pltpu.SemaphoreType.DMA,
        ],
        input_output_aliases={4: 0},
        compiler_params=pltpu.CompilerParams(vmem_limit_bytes=4 * 2**20),
        cost_estimate=pl.CostEstimate(flops=10**5, bytes_accessed=10**6, transcendentals=0),
    )(spot, one, two, cond, base)


def half_body(late, out):
    for row in range(HALF):
        out[row] = late[pl.ds(row, 32, stride=LATE), :]


def mark_body(late, cells, hot, tall):
    lane = lax.broadcasted_iota(jnp.int32, (32, LATS), 1).astype(F32)
    for rad in range(4):
        marks = late[pl.ds(HALF + rad * 5 + 4, 32, stride=LATE), :]
        for slot in range(2):
            row = marks if slot == 0 else pltpu.roll(marks, 64, axis=1)
            tall[slot, rad * 32 : rad * 32 + 32, :] = jnp.where(row == lane, 1.0, 0.0)
            for half in range(2):
                cells[(rad * 2 + slot) * 2 + half] = late[
                    pl.ds(HALF + rad * 5 + 2 * slot + half, 32, stride=LATE), :
                ].astype(jnp.int32)
    for slot in range(2):
        hot[:, slot * LATS : (slot + 1) * LATS] = jnp.transpose(tall[slot])[:ROWS_OWN]


def chunks():
    found = []
    at = 0
    for wide in range(1, WIDE - 1):
        far = max(LONS - wide, wide - 2 * LONS + 1, 0)
        count = PHASES - far
        found.append((wide, at, count))
        at += count
    return found, at


def pack_body(low, own, high, up, down):
    found, rows = chunks()
    for plane in range(PLANES):
        for wide, start, count in found:
            ref = (low, own, high)[wide // LONS]
            up[plane, start : start + count, :] = ref[plane, wide % LONS, SHELLS - count :, :]
            down[plane, start : start + count, :] = ref[plane, wide % LONS, :count, :]
        up[plane, rows:, :] = jnp.zeros((32 - rows, LATS), F32)
        down[plane, rows:, :] = jnp.zeros((32 - rows, LATS), F32)


def main_body(low, own, high, above, below, from_low, from_high, out, cells, w, speeds):
    found, _ = chunks()
    lane = lax.broadcasted_iota(jnp.int32, (TALL, LATS), 1)

    def fill(plane, target):
        strip = jnp.where(lane % 8 < 4, from_low[plane], from_high[plane])
        for wide in range(WIDE):
            ref = (low, own, high)[wide // LONS]
            target[wide, :SHELLS, :LATS] = ref[plane, wide % LONS]
            target[wide, SHELLS:, :LATS] = jnp.zeros((TALL - SHELLS, LATS), F32)
            if 0 < wide < WIDE - 1:
                target[wide, :, LATS:] = halo_lanes(strip, wide)
            else:
                target[wide, :, LATS:] = jnp.zeros((TALL, LATS), F32)
        for wide, start, count in found:
            target[wide, SHELLS : SHELLS + count, :LATS] = above[plane, start : start + count, :]
            target[wide, TALL - count :, :LATS] = below[plane, start : start + count, :]

    for d in range(4):
        fill(FIELDS + d, speeds.at[d])
    for wide in range(1, WIDE - 1):
        made = weights([speeds[d, wide] for d in range(3)], speeds[3, wide])
        for i in range(7):
            w[i, wide] = made[i]

    def one(field, carry):
        fill(field, cells.at[0])
        for phase in range(PHASES):
            old = cells.at[phase % 2]
            new = cells.at[(phase + 1) % 2]
            for wide in range(phase + 1, WIDE - 1 - phase):
                c = old[wide]
                made = blend(
                    [w[i, wide] for i in range(7)],
                    c,
                    pltpu.roll(c, 1, axis=0),
                    pltpu.roll(c, TALL - 1, axis=0),
                    old[wide - 1],
                    old[wide + 1],
                    pltpu.roll(c, 1, axis=1),
                    pltpu.roll(c, 2 * LATS - 1, axis=1),
                )
                if phase == PHASES - 1:
                    out[field, pl.ds(wide - LONS, SHELLS, stride=LONS), :] = made[:SHELLS, :LATS]
                else:
                    new[wide] = made
        return carry

    lax.fori_loop(0, FIELDS, one, 0)


def slot_body(owners, rows, maps, conductance, out):
    count = owners.shape[1]
    here = lax.broadcasted_iota(jnp.int32, (count, count), 0)
    there = lax.broadcasted_iota(jnp.int32, (count, count), 1)
    aimed = (here % 32) * 4 + here // 32 == owners[...]
    earlier = jnp.dot(
        aimed.astype(jnp.bfloat16), (here < there).astype(jnp.bfloat16), preferred_element_type=F32
    )
    cell = maps[...]
    small = (cell & 127).astype(F32).astype(jnp.bfloat16)
    large = (cell >> 7).astype(F32).astype(jnp.bfloat16)
    row = jnp.broadcast_to((rows[...] + 1).astype(F32), (8, count)).astype(jnp.bfloat16)
    marks = []
    lines = []
    for slot in range(2):
        pick = jnp.where(aimed & (earlier == float(slot)), 1.0, 0.0).astype(jnp.bfloat16)
        marks.append(
            lax.dot_general(row, pick, (((1,), (1,)), ((), ())), preferred_element_type=F32) - 1.0
        )
        made = jnp.dot(pick, small, preferred_element_type=F32) + 128.0 * jnp.dot(
            pick, large, preferred_element_type=F32
        )
        lines += [made[:, :128], made[:, 128:]]
    for rad in range(4):
        for j in range(4):
            at = rad * SENT + j * 32
            out[at : at + 32, :] = lines[j][rad * 32 : rad * 32 + 32]
        at = rad * SENT + 128
        out[at : at + 1, :] = marks[0][:1]
        out[at + 1 : at + 2, :] = marks[1][:1]
        out[at + 2 : at + 6, :] = conductance[...]
        out[at + 6 : at + 8, :] = jnp.zeros((2, LATS), F32)


def final_body(
    spot, mine, other, cells, hot, pot, foot, phi, east_w, west_w, north_w, south_w, start, picked
):
    devs, rads = 32, 4
    wide = rads * LATS
    lane = lax.broadcasted_iota(jnp.int32, (devs, wide), 1)

    odd = spot[0] % 2

    def gather(at, step):
        found = []
        for rad in range(rads):
            row = at + rad % 2 * step
            found.append(jnp.where(odd == rad // 2, mine[row], other[row]))
        return jnp.concatenate(found, axis=1)

    def lon_up(values, lon):
        return values[lon + 1] if lon < LONS - 1 else pltpu.roll(values[0], devs - 1, axis=0)

    def lon_down(values, lon):
        return values[lon - 1] if lon > 0 else pltpu.roll(values[LONS - 1], 1, axis=0)

    def lat_up(value):
        return pltpu.roll(value, wide - 1, axis=1)

    def lat_down(value):
        return pltpu.roll(value, 1, axis=1)

    cond = [gather(12 + lon, 4) for lon in range(LONS)]
    sources = [gather(lon, 4) for lon in range(LONS)]
    sources[LONS - 1] += pltpu.roll(gather(8, 1), devs - 1, axis=0)
    sources[0] -= pltpu.roll(gather(10, 1), 1, axis=0)
    last, first = lane == wide - 1, lane == 0
    for lon in range(LONS):
        source = sources[lon]
        c = cond[lon]
        east = 0.5 * (c + lon_up(cond, lon))
        west = 0.5 * (c + lon_down(cond, lon))
        north = 0.5 * (c + jnp.where(last, 0.0, lat_up(c)))
        south = 0.5 * (c + jnp.where(first, 0.0, lat_down(c)))
        scale = RELAX / (DAMPING * c + east + west + north + south)
        east_w[lon] = east * scale
        west_w[lon] = west * scale
        north_w[lon] = jnp.where(last, 0.0, north * scale)
        south_w[lon] = jnp.where(first, 0.0, south * scale)
        start[lon] = source * scale
        phi[0, lon] = source * scale

    def sweep(old, new):
        values = [phi[old, lon] for lon in range(LONS)]
        for lon in range(LONS):
            c = values[lon]
            phi[new, lon] = (
                (1.0 - RELAX) * c
                + start[lon]
                + (east_w[lon] * lon_up(values, lon) + west_w[lon] * lon_down(values, lon))
                + (north_w[lon] * lat_up(c) + south_w[lon] * lat_down(c))
            )

    for turn in range(SWEEPS - 1):
        sweep(turn % 2, (turn + 1) % 2)
    done = (SWEEPS - 1) % 2
    at_lon = lax.broadcasted_iota(jnp.int32, (devs, LATS), 0) == spot[2]
    for rad in range(rads):

        @pl.when(spot[1] == rad)
        def _():
            for lon in range(LONS):
                block = phi[done, lon, :, rad * LATS : (rad + 1) * LATS]
                pot[lon : lon + 1, :] = jnp.sum(
                    jnp.where(at_lon, block, 0.0), axis=0, keepdims=True
                )

    for rad in range(rads):
        table = [phi[done, lon, :, rad * LATS : (rad + 1) * LATS] for lon in range(LONS)]
        for slot in range(2):
            at = (slot * rads + rad) * devs
            for half in range(2):
                cell = cells[(rad * 2 + slot) * 2 + half]
                place, lon_at = cell & 127, cell >> 7
                value = jnp.zeros((devs, LATS), F32)
                for lon in range(LONS):
                    found = jnp.take_along_axis(
                        table[lon], place, axis=1, mode="promise_in_bounds"
                    )
                    value = jnp.where(lon_at == lon, found, value)
                picked[at : at + devs, 128 * half : 128 * half + 128] = value
    records = picked[...]
    rows = hot[...].astype(jnp.bfloat16)
    large = records.astype(jnp.bfloat16)
    small = (records - large.astype(F32)).astype(jnp.bfloat16)
    foot[...] = jnp.dot(rows, large, preferred_element_type=F32) + jnp.dot(
        rows, small, preferred_element_type=F32
    )


def shards(plasma_fields, velocity, resistivity, conductance, foot_map, foot_owner, foot_row):
    spot = jnp.stack([lax.axis_index("sec"), lax.axis_index("rad"), lax.axis_index("lon")])
    own, slots = first(
        plasma_fields.reshape(FIELDS, SHELLS * LONS, LATS),
        velocity,
        resistivity,
        foot_owner.reshape(1, -1),
        foot_row.reshape(1, -1),
        foot_map,
        conductance,
    )
    low = lax.ppermute(own, "lon", shift("lon", 1, True))
    high = lax.ppermute(own, "lon", shift("lon", -1, True))

    sent = lax.all_to_all(
        slots.reshape(4, SENT, LATS), "rad", split_axis=0, concat_axis=0, tiled=True
    )

    low, high, sent = lax.optimization_barrier((low, high, sent))
    up, down = call(pack_body, (arr(PLANES, 32, LATS), arr(PLANES, 32, LATS)), (low, own, high))
    above = lax.ppermute(down, "sec", shift("sec", -1, False))
    below = lax.ppermute(up, "sec", shift("sec", 1, False))
    raw = call(raw_body, arr(RAW, LATS), (low, own, high))
    owner = lax.axis_index("sec") == 0

    def advance_inner(rows):
        gathered = lax.all_gather(rows, "rad")
        return call(
            inner_body,
            arr(24, LATS),
            (gathered.reshape(4 * RAW, LATS),),
            scratch=(pltpu.VMEM((6, WIDE, 8, 4 * LATS), F32),),
        )

    inner = lax.cond(owner, advance_inner, lambda rows: jnp.zeros((24, LATS), F32), raw)
    inner, below, above = lax.optimization_barrier((inner, below, above))
    far = lax.ppermute(inner, "sec", [(0, 3)])
    far = inner + far
    near = lax.ppermute(far, "sec", [(0, 1), (3, 2)])
    base, cond = call(
        base_body,
        (arr(32 * LATE, LATS), arr(LONS, LATS)),
        (spot, sent.reshape(4 * SENT, LATS)),
        smem=(0,),
    )
    late = join(spot, far, near, cond, base.reshape(32, LATE, LATS))
    late, low, high = lax.optimization_barrier((late, low, high))

    blocks = (low, own, high, above, below)
    edges = call(
        edge_body,
        arr(PLANES, TALL, LATS),
        blocks,
        scratch=(pltpu.VMEM((PLANES, WIDE, TALL, LATS), F32),),
    )
    from_low = lax.ppermute(edges, "rad", shift("rad", 1, False))
    from_high = lax.ppermute(edges, "rad", shift("rad", -1, False))
    late = lax.all_to_all(
        late, "lon", split_axis=0, concat_axis=0, tiled=True
    )

    advanced = call(
        main_body,
        arr(FIELDS, SHELLS * LONS, LATS),
        blocks + (from_low, from_high),
        scratch=(
            pltpu.VMEM((2, WIDE, TALL, 2 * LATS), F32),
            pltpu.VMEM((7, WIDE, TALL, 2 * LATS), F32),
            pltpu.VMEM((4, WIDE, TALL, 2 * LATS), F32),
        ),
    ).reshape(FIELDS, SHELLS, LONS, LATS)

    late, advanced = lax.optimization_barrier((late, advanced))
    late = late.reshape(32 * LATE, LATS)
    mine = call(half_body, arr(HALF, 32, LATS), (late,))
    other = lax.ppermute(mine, "sec", [(0, 1), (1, 0), (2, 3), (3, 2)])
    cells, hot = call(
        mark_body,
        (jax.ShapeDtypeStruct((16, 32, LATS), jnp.int32), arr(ROWS_OWN, 2 * LATS)),
        (late,),
        scratch=(pltpu.VMEM((2, LATS, LATS), F32),),
    )
    plane = pltpu.VMEM((LONS, 32, 4 * LATS), F32)
    potential, foot_table = call(
        final_body,
        (arr(LONS, LATS), arr(ROWS_OWN, 256)),
        (spot, mine, other, cells, hot),
        scratch=(
            pltpu.VMEM((2, LONS, 32, 4 * LATS), F32),
            plane,
            plane,
            plane,
            plane,
            plane,
            pltpu.VMEM((256, 256), F32),
        ),
        smem=(0,),
    )
    return (advanced, potential, foot_table)


def solution(mesh):
    in_specs = (
        P(None, "sec", "lon", "rad"),
        P(None, "sec", "lon", "rad"),
        P("sec", "lon", "rad"),
        P("lon", "rad"),
        P(("lon", "sec", "rad"), None),
        P(("lon", "sec", "rad"), None),
        P(("lon", "sec", "rad")),
    )
    out_specs = (P(None, "sec", "lon", "rad"), P("lon", "rad"), P(("lon", "sec", "rad"), None))
    return jax.shard_map(shards, mesh=mesh, in_specs=in_specs, out_specs=out_specs, check_vma=False)
```

```python
import jax
import jax.numpy as jnp
from jax import lax
from jax.experimental import pallas as pl
from jax.experimental.pallas import tpu as pltpu
from jax.sharding import PartitionSpec as P

PHASES = 4
SWEEPS = 8
ROWS_OWN = 32
COURANT = 0.25
DAMPING = 0.05
RELAX = 0.8

FIELDS = 8
PLANES = FIELDS + 4
SHELLS = 16
LONS = 4
LATS = 128
WIDE = 3 * LONS
LATE = 40
HALF = 20
RAW = 192
SENT = 136
TALL = SHELLS + 2 * PHASES
F32 = jnp.float32


def call(body, out_shape, args, scratch=(), smem=(), flops=10**6, traffic=10**6):
    specs = [
        pl.BlockSpec(memory_space=pltpu.SMEM if i in smem else pltpu.VMEM)
        for i in range(len(args))
    ]
    many = isinstance(out_shape, (tuple, list))
    vmem = pl.BlockSpec(memory_space=pltpu.VMEM)
    return pl.pallas_call(
        body,
        out_shape=out_shape,
        in_specs=specs,
        out_specs=[vmem] * len(out_shape) if many else vmem,
        scratch_shapes=list(scratch),
        compiler_params=pltpu.CompilerParams(vmem_limit_bytes=16 * 2**20),
        cost_estimate=pl.CostEstimate(flops=flops, bytes_accessed=traffic, transcendentals=0),
    )(*args)


def arr(*shape):
    return jax.ShapeDtypeStruct(shape, F32)


def shift(axis, step, closed):
    count = lax.axis_size(axis)
    return [
        (i, (i + step) % count) for i in range(count) if closed or 0 <= i + step < count
    ]


def first_body(*refs):
    sources, (own, slots, plain), held, sems = refs[:7], refs[7:10], refs[10:17], refs[17]
    moves = [
        pltpu.make_async_copy(source, target, sems.at[i])
        for i, (source, target) in enumerate(zip(sources, held))
    ]
    for move in moves:
        move.start()
    fields, speeds, resist, owners, rows, maps, conductance = held
    for move in moves[1:3]:
        move.wait()
    for plane in range(4):
        for shell in range(SHELLS):
            found = speeds[plane, shell] if plane < 3 else resist[shell]
            plain[plane, shell * LONS : shell * LONS + LONS, :] = found.astype(F32)
    moves[0].wait()
    for plane in range(PLANES):
        for lon in range(LONS):
            at = pl.ds(lon, SHELLS, stride=LONS)
            if plane < FIELDS:
                own[plane, lon] = fields[plane, at, :]
            else:
                own[plane, lon] = plain[plane - FIELDS, at, :]
    for move in moves[3:]:
        move.wait()
    slot_body(owners, rows, maps, conductance, slots)


def first(*args):
    vmem = pl.BlockSpec(memory_space=pltpu.VMEM)
    return pl.pallas_call(
        first_body,
        out_shape=(arr(PLANES, LONS, SHELLS, LATS), arr(4 * SENT, LATS)),
        in_specs=[pl.BlockSpec(memory_space=pltpu.HBM)] * len(args),
        out_specs=[vmem, vmem],
        scratch_shapes=[pltpu.VMEM((4, SHELLS * LONS, LATS), F32)]
        + [pltpu.VMEM(arg.shape, arg.dtype) for arg in args]
        + [pltpu.SemaphoreType.DMA((len(args),))],
        compiler_params=pltpu.CompilerParams(vmem_limit_bytes=60 * 2**20),
        cost_estimate=pl.CostEstimate(flops=10**6, bytes_accessed=10**6, transcendentals=0),
    )(*args)


def edge_body(low, own, high, above, below, edges, tall):
    found, _ = chunks()
    group = lax.broadcasted_iota(jnp.int32, (TALL, LATS), 1) // 8
    for plane in range(PLANES):
        for wide in range(WIDE):
            ref = (low, own, high)[wide // LONS]
            tall[plane, wide, :SHELLS, :] = ref[plane, wide % LONS]
            tall[plane, wide, SHELLS:, :] = jnp.zeros((TALL - SHELLS, LATS), F32)
        for wide, start, count in found:
            tall[plane, wide, SHELLS : SHELLS + count, :] = above[plane, start : start + count, :]
            tall[plane, wide, TALL - count :, :] = below[plane, start : start + count, :]
    for plane in range(PLANES):
        packed = jnp.zeros((TALL, LATS), F32)
        for wide in range(1, WIDE - 1):
            turned = pltpu.roll(tall[plane, wide], 8 * wide + 4, axis=1)
            packed = jnp.where(group == wide, turned, packed)
        edges[plane] = packed


def halo_lanes(edges, wide):
    lane = lax.broadcasted_iota(jnp.int32, edges.shape, 1)
    turned = pltpu.roll(edges, (LATS - 8 * wide - 4) % LATS, axis=1)
    return jnp.where((lane < 4) | (lane >= LATS - 4), turned, 0.0)


def weights(speeds, resist):
    out = []
    total = None
    for speed in speeds:
        lower = COURANT * jnp.maximum(speed, 0.0) + resist
        upper = resist - COURANT * jnp.minimum(speed, 0.0)
        out += [lower, upper]
        total = lower + upper if total is None else total + lower + upper
    return [1.0 - total] + out


def blend(w, centre, shell_lo, shell_hi, lon_lo, lon_hi, lat_lo, lat_hi):
    return (
        w[0] * centre
        + (w[1] * shell_lo + w[2] * shell_hi)
        + (w[3] * lon_lo + w[4] * lon_hi)
        + (w[5] * lat_lo + w[6] * lat_hi)
    )


def raw_chunks():
    found = []
    at = 0
    for plane in (5, 6, 8, 9, 10, 11):
        reach = PHASES + 1 if plane < FIELDS else PHASES
        for wide in range(WIDE):
            count = reach - max(LONS - wide, wide - 2 * LONS + 1, 0)
            if count > 0:
                found.append((plane, wide, at, count))
                at += count
    return found


def raw_body(low, own, high, out):
    for plane, wide, at, count in raw_chunks():
        ref = (low, own, high)[wide // LONS]
        for block in range(4):
            row = block * RAW + at
            out[row : row + count, :] = ref[plane, wide % LONS, :count, :]


def inner_body(raw, out, cells):
    span = 4 * LATS
    lane = lax.broadcasted_iota(jnp.int32, (8, span), 1)
    bottom = lax.broadcasted_iota(jnp.int32, (8, span), 0) == 0
    first, last = lane == 0, lane == span - 1
    cells[...] = jnp.zeros(cells.shape, F32)
    order = (5, 6, 8, 9, 10, 11)
    for plane, wide, at, count in raw_chunks():
        for rad in range(4):
            cells[order.index(plane), wide, :count, rad * LATS : (rad + 1) * LATS] = raw[
                rad * RAW + at : rad * RAW + at + count, :
            ]
    w = [None] + [
        weights([cells[2 + d, wide] for d in range(3)], cells[5, wide])
        for wide in range(1, WIDE - 1)
    ]
    made = []
    for part in range(2):
        now = [cells[part, wide] for wide in range(WIDE)]
        for phase in range(PHASES):
            fresh = list(now)
            for wide in range(phase + 1, WIDE - 1 - phase):
                c = now[wide]
                fresh[wide] = blend(
                    w[wide],
                    c,
                    jnp.where(bottom, 0.0, pltpu.roll(c, 1, axis=0)),
                    pltpu.roll(c, 7, axis=0),
                    now[wide - 1],
                    now[wide + 1],
                    jnp.where(first, 0.0, pltpu.roll(c, 1, axis=1)),
                    jnp.where(last, 0.0, pltpu.roll(c, span - 1, axis=1)),
                )
            now = fresh
        made.append(now[LONS : 2 * LONS])
    blon, blat = made
    for lon in range(LONS):
        c = blon[lon]
        source = jnp.where(first, 0.0, pltpu.roll(c, 1, axis=1)) - jnp.where(
            last, 0.0, pltpu.roll(c, span - 1, axis=1)
        )
        if lon < LONS - 1:
            source = source + blat[lon + 1]
        if lon > 0:
            source = source - blat[lon - 1]
        for rad in range(4):
            part = slice(rad * LATS, (rad + 1) * LATS)
            at = rad // 2 * 12 + rad % 2 * 4 + lon
            out[at : at + 1, :] = source[0:1, part]
            at = rad // 2 * 12 + 8 + rad % 2
            if lon == 0:
                out[at : at + 1, :] = blat[0][0:1, part]
            if lon == LONS - 1:
                out[at + 2 : at + 3, :] = blat[LONS - 1][0:1, part]


def base_body(spot, sent, out, cond):
    step = LATE - 16
    odd = spot[0] % 2 == 1
    for lon in range(LONS):
        at = 130 + lon
        lines = [sent[rad * SENT + at : rad * SENT + at + 1, :] for rad in range(4)]
        cond[lon : lon + 1, :] = jnp.where(odd, lines[2], lines[0])
        line = jnp.where(odd, lines[3], lines[1])
        out[pl.ds(lon, 32, stride=step), :] = jnp.broadcast_to(line, (32, LATS))
    lane = lax.broadcasted_iota(jnp.int32, (32, LATS), 1)
    owner = lax.broadcasted_iota(jnp.int32, (32, LATS), 0)
    for rad in range(4):
        for row in range(4):
            at = rad * SENT + row * 32
            out[pl.ds(4 + rad * 5 + row, 32, stride=step), :] = sent[at : at + 32, :]
        marks = []
        for slot in range(2):
            at = rad * SENT + 128 + slot
            line = jnp.broadcast_to(sent[at : at + 1, :], (32, LATS))
            marks.append(
                jnp.sum(jnp.where(lane == owner + spot[1] * 32, line, 0.0), axis=1, keepdims=True)
            )
        out[pl.ds(8 + rad * 5, 32, stride=step), :] = jnp.where(lane < 64, marks[0], marks[1])


def join_body(spot, one, two, cond, base, out, head, copies, sems):
    rest = pltpu.make_async_copy(base, out.at[:, pl.ds(16, LATE - 16), :], sems.at[0])
    rest.start()
    source = one[...] + two[...]
    head[:12, :] = jnp.where(spot[0] % 2 == 1, source[12:], source[:12])
    head[12:, :] = cond[...]
    mine = head[...]
    for owner in range(32):
        copies[owner] = mine
    move = pltpu.make_async_copy(copies, out.at[:, pl.ds(0, 16), :], sems.at[1])
    move.start()
    move.wait()
    rest.wait()


def join(spot, one, two, cond, base):
    vmem = pl.BlockSpec(memory_space=pltpu.VMEM)
    plain = pl.BlockSpec(memory_space=pl.ANY)
    return pl.pallas_call(
        join_body,
        out_shape=arr(32, LATE, LATS),
        in_specs=[pl.BlockSpec(memory_space=pltpu.SMEM), vmem, vmem, vmem, plain],
        out_specs=plain,
        scratch_shapes=[
            pltpu.VMEM((16, LATS), F32),
            pltpu.VMEM((32, 16, LATS), F32),
            pltpu.SemaphoreType.DMA((2,)),
        ],
        compiler_params=pltpu.CompilerParams(vmem_limit_bytes=4 * 2**20),
        cost_estimate=pl.CostEstimate(flops=10**5, bytes_accessed=10**6, transcendentals=0),
    )(spot, one, two, cond, base)


def half_body(late, out):
    for row in range(HALF):
        out[row] = late[pl.ds(row, 32, stride=LATE), :]


def mark_body(late, cells, hot, tall):
    lane = lax.broadcasted_iota(jnp.int32, (32, LATS), 1).astype(F32)
    for rad in range(4):
        marks = late[pl.ds(HALF + rad * 5 + 4, 32, stride=LATE), :]
        for slot in range(2):
            row = marks if slot == 0 else pltpu.roll(marks, 64, axis=1)
            tall[slot, rad * 32 : rad * 32 + 32, :] = jnp.where(row == lane, 1.0, 0.0)
            for half in range(2):
                cells[(rad * 2 + slot) * 2 + half] = late[
                    pl.ds(HALF + rad * 5 + 2 * slot + half, 32, stride=LATE), :
                ].astype(jnp.int32)
    for slot in range(2):
        hot[:, slot * LATS : (slot + 1) * LATS] = jnp.transpose(tall[slot])[:ROWS_OWN]


def chunks():
    found = []
    at = 0
    for wide in range(1, WIDE - 1):
        far = max(LONS - wide, wide - 2 * LONS + 1, 0)
        count = PHASES - far
        found.append((wide, at, count))
        at += count
    return found, at


def pack_body(low, own, high, up, down):
    found, rows = chunks()
    for plane in range(PLANES):
        for wide, start, count in found:
            ref = (low, own, high)[wide // LONS]
            up[plane, start : start + count, :] = ref[plane, wide % LONS, SHELLS - count :, :]
            down[plane, start : start + count, :] = ref[plane, wide % LONS, :count, :]
        up[plane, rows:, :] = jnp.zeros((32 - rows, LATS), F32)
        down[plane, rows:, :] = jnp.zeros((32 - rows, LATS), F32)


def main_body(low, own, high, above, below, from_low, from_high, out, cells, w, speeds):
    found, _ = chunks()
    lane = lax.broadcasted_iota(jnp.int32, (TALL, LATS), 1)

    def fill(plane, target):
        strip = jnp.where(lane % 8 < 4, from_low[plane], from_high[plane])
        for wide in range(WIDE):
            ref = (low, own, high)[wide // LONS]
            target[wide, :SHELLS, :LATS] = ref[plane, wide % LONS]
            target[wide, SHELLS:, :LATS] = jnp.zeros((TALL - SHELLS, LATS), F32)
            if 0 < wide < WIDE - 1:
                target[wide, :, LATS:] = halo_lanes(strip, wide)
            else:
                target[wide, :, LATS:] = jnp.zeros((TALL, LATS), F32)
        for wide, start, count in found:
            target[wide, SHELLS : SHELLS + count, :LATS] = above[plane, start : start + count, :]
            target[wide, TALL - count :, :LATS] = below[plane, start : start + count, :]

    for d in range(4):
        fill(FIELDS + d, speeds.at[d])
    for wide in range(1, WIDE - 1):
        made = weights([speeds[d, wide] for d in range(3)], speeds[3, wide])
        for i in range(7):
            w[i, wide] = made[i]

    def one(field, carry):
        fill(field, cells.at[0])
        for phase in range(PHASES):
            old = cells.at[phase % 2]
            new = cells.at[(phase + 1) % 2]
            for wide in range(phase + 1, WIDE - 1 - phase):
                c = old[wide]
                made = blend(
                    [w[i, wide] for i in range(7)],
                    c,
                    pltpu.roll(c, 1, axis=0),
                    pltpu.roll(c, TALL - 1, axis=0),
                    old[wide - 1],
                    old[wide + 1],
                    pltpu.roll(c, 1, axis=1),
                    pltpu.roll(c, 2 * LATS - 1, axis=1),
                )
                if phase == PHASES - 1:
                    out[field, pl.ds(wide - LONS, SHELLS, stride=LONS), :] = made[:SHELLS, :LATS]
                else:
                    new[wide] = made
        return carry

    lax.fori_loop(0, FIELDS, one, 0)


def slot_body(owners, rows, maps, conductance, out):
    count = owners.shape[1]
    here = lax.broadcasted_iota(jnp.int32, (count, count), 0)
    there = lax.broadcasted_iota(jnp.int32, (count, count), 1)
    aimed = (here % 32) * 4 + here // 32 == owners[...]
    earlier = jnp.dot(
        aimed.astype(jnp.bfloat16), (here < there).astype(jnp.bfloat16), preferred_element_type=F32
    )
    cell = maps[...]
    small = (cell & 127).astype(F32).astype(jnp.bfloat16)
    large = (cell >> 7).astype(F32).astype(jnp.bfloat16)
    row = jnp.broadcast_to((rows[...] + 1).astype(F32), (8, count)).astype(jnp.bfloat16)
    marks = []
    lines = []
    for slot in range(2):
        pick = jnp.where(aimed & (earlier == float(slot)), 1.0, 0.0).astype(jnp.bfloat16)
        marks.append(
            lax.dot_general(row, pick, (((1,), (1,)), ((), ())), preferred_element_type=F32) - 1.0
        )
        made = jnp.dot(pick, small, preferred_element_type=F32) + 128.0 * jnp.dot(
            pick, large, preferred_element_type=F32
        )
        lines += [made[:, :128], made[:, 128:]]
    for rad in range(4):
        for j in range(4):
            at = rad * SENT + j * 32
            out[at : at + 32, :] = lines[j][rad * 32 : rad * 32 + 32]
        at = rad * SENT + 128
        out[at : at + 1, :] = marks[0][:1]
        out[at + 1 : at + 2, :] = marks[1][:1]
        out[at + 2 : at + 6, :] = conductance[...]
        out[at + 6 : at + 8, :] = jnp.zeros((2, LATS), F32)


def final_body(
    spot, mine, other, cells, hot, pot, foot, phi, east_w, west_w, north_w, south_w, start, picked
):
    devs, rads = 32, 4
    wide = rads * LATS
    lane = lax.broadcasted_iota(jnp.int32, (devs, wide), 1)

    odd = spot[0] % 2

    def gather(at, step):
        found = []
        for rad in range(rads):
            row = at + rad % 2 * step
            found.append(jnp.where(odd == rad // 2, mine[row], other[row]))
        return jnp.concatenate(found, axis=1)

    def lon_up(values, lon):
        return values[lon + 1] if lon < LONS - 1 else pltpu.roll(values[0], devs - 1, axis=0)

    def lon_down(values, lon):
        return values[lon - 1] if lon > 0 else pltpu.roll(values[LONS - 1], 1, axis=0)

    def lat_up(value):
        return pltpu.roll(value, wide - 1, axis=1)

    def lat_down(value):
        return pltpu.roll(value, 1, axis=1)

    cond = [gather(12 + lon, 4) for lon in range(LONS)]
    sources = [gather(lon, 4) for lon in range(LONS)]
    sources[LONS - 1] += pltpu.roll(gather(8, 1), devs - 1, axis=0)
    sources[0] -= pltpu.roll(gather(10, 1), 1, axis=0)
    last, first = lane == wide - 1, lane == 0
    for lon in range(LONS):
        source = sources[lon]
        c = cond[lon]
        east = 0.5 * (c + lon_up(cond, lon))
        west = 0.5 * (c + lon_down(cond, lon))
        north = 0.5 * (c + jnp.where(last, 0.0, lat_up(c)))
        south = 0.5 * (c + jnp.where(first, 0.0, lat_down(c)))
        scale = RELAX / (DAMPING * c + east + west + north + south)
        east_w[lon] = east * scale
        west_w[lon] = west * scale
        north_w[lon] = jnp.where(last, 0.0, north * scale)
        south_w[lon] = jnp.where(first, 0.0, south * scale)
        start[lon] = source * scale
        phi[0, lon] = source * scale

    def sweep(old, new):
        values = [phi[old, lon] for lon in range(LONS)]
        for lon in range(LONS):
            c = values[lon]
            phi[new, lon] = (
                (1.0 - RELAX) * c
                + start[lon]
                + (east_w[lon] * lon_up(values, lon) + west_w[lon] * lon_down(values, lon))
                + (north_w[lon] * lat_up(c) + south_w[lon] * lat_down(c))
            )

    for turn in range(SWEEPS - 1):
        sweep(turn % 2, (turn + 1) % 2)
    done = (SWEEPS - 1) % 2
    at_lon = lax.broadcasted_iota(jnp.int32, (devs, LATS), 0) == spot[2]
    for rad in range(rads):

        @pl.when(spot[1] == rad)
        def _():
            for lon in range(LONS):
                block = phi[done, lon, :, rad * LATS : (rad + 1) * LATS]
                pot[lon : lon + 1, :] = jnp.sum(
                    jnp.where(at_lon, block, 0.0), axis=0, keepdims=True
                )

    for rad in range(rads):
        table = [phi[done, lon, :, rad * LATS : (rad + 1) * LATS] for lon in range(LONS)]
        for slot in range(2):
            at = (slot * rads + rad) * devs
            for half in range(2):
                cell = cells[(rad * 2 + slot) * 2 + half]
                place, lon_at = cell & 127, cell >> 7
                value = jnp.zeros((devs, LATS), F32)
                for lon in range(LONS):
                    found = jnp.take_along_axis(
                        table[lon], place, axis=1, mode="promise_in_bounds"
                    )
                    value = jnp.where(lon_at == lon, found, value)
                picked[at : at + devs, 128 * half : 128 * half + 128] = value
    records = picked[...]
    rows = hot[...].astype(jnp.bfloat16)
    large = records.astype(jnp.bfloat16)
    small = (records - large.astype(F32)).astype(jnp.bfloat16)
    foot[...] = jnp.dot(rows, large, preferred_element_type=F32) + jnp.dot(
        rows, small, preferred_element_type=F32
    )


def shards(plasma_fields, velocity, resistivity, conductance, foot_map, foot_owner, foot_row):
    spot = jnp.stack([lax.axis_index("sec"), lax.axis_index("rad"), lax.axis_index("lon")])
    own, slots = first(
        plasma_fields.reshape(FIELDS, SHELLS * LONS, LATS),
        velocity,
        resistivity,
        foot_owner.reshape(1, -1),
        foot_row.reshape(1, -1),
        foot_map,
        conductance,
    )
    low = lax.ppermute(own, "lon", shift("lon", 1, True))
    high = lax.ppermute(own, "lon", shift("lon", -1, True))

    sent = lax.all_to_all(
        slots.reshape(4, SENT, LATS), "rad", split_axis=0, concat_axis=0, tiled=True
    )

    low, high, sent = lax.optimization_barrier((low, high, sent))
    up, down = call(pack_body, (arr(PLANES, 32, LATS), arr(PLANES, 32, LATS)), (low, own, high))
    above = lax.ppermute(down, "sec", shift("sec", -1, False))
    below = lax.ppermute(up, "sec", shift("sec", 1, False))
    raw = call(raw_body, arr(4 * RAW, LATS), (low, own, high))
    owner = lax.axis_index("sec") == 0

    def advance_inner(rows):
        gathered = lax.all_to_all(
            rows.reshape(4, RAW, LATS), "rad", split_axis=0, concat_axis=0, tiled=True
        )
        return call(
            inner_body,
            arr(24, LATS),
            (gathered.reshape(4 * RAW, LATS),),
            scratch=(pltpu.VMEM((6, WIDE, 8, 4 * LATS), F32),),
        )

    inner = lax.cond(owner, advance_inner, lambda rows: jnp.zeros((24, LATS), F32), raw)
    inner, below, above = lax.optimization_barrier((inner, below, above))
    far = lax.ppermute(inner, "sec", [(0, 3)])
    far = inner + far
    near = lax.ppermute(far, "sec", [(0, 1), (3, 2)])
    base, cond = call(
        base_body,
        (arr(32 * (LATE - 16), LATS), arr(LONS, LATS)),
        (spot, sent.reshape(4 * SENT, LATS)),
        smem=(0,),
    )
    late = join(spot, far, near, cond, base.reshape(32, LATE - 16, LATS))
    late, low, high = lax.optimization_barrier((late, low, high))

    blocks = (low, own, high, above, below)
    edges = call(
        edge_body,
        arr(PLANES, TALL, LATS),
        blocks,
        scratch=(pltpu.VMEM((PLANES, WIDE, TALL, LATS), F32),),
    )
    from_low = lax.ppermute(edges, "rad", shift("rad", 1, False))
    from_high = lax.ppermute(edges, "rad", shift("rad", -1, False))
    late = lax.all_to_all(
        late, "lon", split_axis=0, concat_axis=0, tiled=True
    )

    advanced = call(
        main_body,
        arr(FIELDS, SHELLS * LONS, LATS),
        blocks + (from_low, from_high),
        scratch=(
            pltpu.VMEM((2, WIDE, TALL, 2 * LATS), F32),
            pltpu.VMEM((7, WIDE, TALL, 2 * LATS), F32),
            pltpu.VMEM((4, WIDE, TALL, 2 * LATS), F32),
        ),
    ).reshape(FIELDS, SHELLS, LONS, LATS)

    late, advanced = lax.optimization_barrier((late, advanced))
    late = late.reshape(32 * LATE, LATS)
    mine = call(half_body, arr(HALF, 32, LATS), (late,))
    other = lax.ppermute(mine, "sec", [(0, 1), (1, 0), (2, 3), (3, 2)])
    cells, hot = call(
        mark_body,
        (jax.ShapeDtypeStruct((16, 32, LATS), jnp.int32), arr(ROWS_OWN, 2 * LATS)),
        (late,),
        scratch=(pltpu.VMEM((2, LATS, LATS), F32),),
    )
    plane = pltpu.VMEM((LONS, 32, 4 * LATS), F32)
    potential, foot_table = call(
        final_body,
        (arr(LONS, LATS), arr(ROWS_OWN, 256)),
        (spot, mine, other, cells, hot),
        scratch=(
            pltpu.VMEM((2, LONS, 32, 4 * LATS), F32),
            plane,
            plane,
            plane,
            plane,
            plane,
            pltpu.VMEM((256, 256), F32),
        ),
        smem=(0,),
    )
    return (advanced, potential, foot_table)


def solution(mesh):
    in_specs = (
        P(None, "sec", "lon", "rad"),
        P(None, "sec", "lon", "rad"),
        P("sec", "lon", "rad"),
        P("lon", "rad"),
        P(("lon", "sec", "rad"), None),
        P(("lon", "sec", "rad"), None),
        P(("lon", "sec", "rad")),
    )
    out_specs = (P(None, "sec", "lon", "rad"), P("lon", "rad"), P(("lon", "sec", "rad"), None))
    return jax.shard_map(shards, mesh=mesh, in_specs=in_specs, out_specs=out_specs, check_vma=False)
```

```python
import jax
import jax.numpy as jnp
from jax import lax
from jax.experimental import pallas as pl
from jax.experimental.pallas import tpu as pltpu
from jax.sharding import PartitionSpec as P

PHASES = 4
SWEEPS = 8
ROWS_OWN = 32
COURANT = 0.25
DAMPING = 0.05
RELAX = 0.8

FIELDS = 8
PLANES = FIELDS + 4
SHELLS = 16
LONS = 4
LATS = 128
WIDE = 3 * LONS
LATE = 40
HALF = 20
RAW = 192
SENT = 136
TALL = SHELLS + 2 * PHASES
F32 = jnp.float32


def call(body, out_shape, args, scratch=(), smem=(), flops=10**6, traffic=10**6):
    specs = [
        pl.BlockSpec(memory_space=pltpu.SMEM if i in smem else pltpu.VMEM)
        for i in range(len(args))
    ]
    many = isinstance(out_shape, (tuple, list))
    vmem = pl.BlockSpec(memory_space=pltpu.VMEM)
    return pl.pallas_call(
        body,
        out_shape=out_shape,
        in_specs=specs,
        out_specs=[vmem] * len(out_shape) if many else vmem,
        scratch_shapes=list(scratch),
        compiler_params=pltpu.CompilerParams(vmem_limit_bytes=16 * 2**20),
        cost_estimate=pl.CostEstimate(flops=flops, bytes_accessed=traffic, transcendentals=0),
    )(*args)


def arr(*shape):
    return jax.ShapeDtypeStruct(shape, F32)


def shift(axis, step, closed):
    count = lax.axis_size(axis)
    return [
        (i, (i + step) % count) for i in range(count) if closed or 0 <= i + step < count
    ]


def first_body(*refs):
    sources, (own, slots, plain), held, sems = refs[:7], refs[7:10], refs[10:17], refs[17]
    moves = [
        pltpu.make_async_copy(source, target, sems.at[i])
        for i, (source, target) in enumerate(zip(sources, held))
    ]
    for move in moves:
        move.start()
    fields, speeds, resist, owners, rows, maps, conductance = held
    for move in moves[1:3]:
        move.wait()
    for plane in range(4):
        for shell in range(SHELLS):
            found = speeds[plane, shell] if plane < 3 else resist[shell]
            plain[plane, shell * LONS : shell * LONS + LONS, :] = found.astype(F32)
    moves[0].wait()
    for plane in range(PLANES):
        for lon in range(LONS):
            at = pl.ds(lon, SHELLS, stride=LONS)
            if plane < FIELDS:
                own[plane, lon] = fields[plane, at, :]
            else:
                own[plane, lon] = plain[plane - FIELDS, at, :]
    for move in moves[3:]:
        move.wait()
    slot_body(owners, rows, maps, conductance, slots)


def first(*args):
    vmem = pl.BlockSpec(memory_space=pltpu.VMEM)
    return pl.pallas_call(
        first_body,
        out_shape=(arr(PLANES, LONS, SHELLS, LATS), arr(4 * SENT, LATS)),
        in_specs=[pl.BlockSpec(memory_space=pltpu.HBM)] * len(args),
        out_specs=[vmem, vmem],
        scratch_shapes=[pltpu.VMEM((4, SHELLS * LONS, LATS), F32)]
        + [pltpu.VMEM(arg.shape, arg.dtype) for arg in args]
        + [pltpu.SemaphoreType.DMA((len(args),))],
        compiler_params=pltpu.CompilerParams(vmem_limit_bytes=60 * 2**20),
        cost_estimate=pl.CostEstimate(flops=10**6, bytes_accessed=10**6, transcendentals=0),
    )(*args)


def edge_body(low, own, high, above, below, edges, tall):
    found, _ = chunks()
    group = lax.broadcasted_iota(jnp.int32, (TALL, LATS), 1) // 8
    for plane in range(PLANES):
        for wide in range(WIDE):
            ref = (low, own, high)[wide // LONS]
            tall[plane, wide, :SHELLS, :] = ref[plane, wide % LONS]
            tall[plane, wide, SHELLS:, :] = jnp.zeros((TALL - SHELLS, LATS), F32)
        for wide, start, count in found:
            tall[plane, wide, SHELLS : SHELLS + count, :] = above[plane, start : start + count, :]
            tall[plane, wide, TALL - count :, :] = below[plane, start : start + count, :]
    for plane in range(PLANES):
        packed = jnp.zeros((TALL, LATS), F32)
        for wide in range(1, WIDE - 1):
            turned = pltpu.roll(tall[plane, wide], 8 * wide + 4, axis=1)
            packed = jnp.where(group == wide, turned, packed)
        edges[plane] = packed


def halo_lanes(edges, wide):
    lane = lax.broadcasted_iota(jnp.int32, edges.shape, 1)
    turned = pltpu.roll(edges, (LATS - 8 * wide - 4) % LATS, axis=1)
    return jnp.where((lane < 4) | (lane >= LATS - 4), turned, 0.0)


def weights(speeds, resist):
    out = []
    total = None
    for speed in speeds:
        lower = COURANT * jnp.maximum(speed, 0.0) + resist
        upper = resist - COURANT * jnp.minimum(speed, 0.0)
        out += [lower, upper]
        total = lower + upper if total is None else total + lower + upper
    return [1.0 - total] + out


def blend(w, centre, shell_lo, shell_hi, lon_lo, lon_hi, lat_lo, lat_hi):
    return (
        w[0] * centre
        + (w[1] * shell_lo + w[2] * shell_hi)
        + (w[3] * lon_lo + w[4] * lon_hi)
        + (w[5] * lat_lo + w[6] * lat_hi)
    )


def raw_chunks():
    found = []
    at = 0
    for plane in (5, 6, 8, 9, 10, 11):
        reach = PHASES + 1 if plane < FIELDS else PHASES
        for wide in range(WIDE):
            count = reach - max(LONS - wide, wide - 2 * LONS + 1, 0)
            if count > 0:
                found.append((plane, wide, at, count))
                at += count
    return found


def raw_body(low, own, high, out):
    for plane, wide, at, count in raw_chunks():
        ref = (low, own, high)[wide // LONS]
        for block in range(4):
            row = block * RAW + at
            out[row : row + count, :] = ref[plane, wide % LONS, :count, :]


def inner_body(raw, out, cells):
    span = 4 * LATS
    lane = lax.broadcasted_iota(jnp.int32, (8, span), 1)
    bottom = lax.broadcasted_iota(jnp.int32, (8, span), 0) == 0
    first, last = lane == 0, lane == span - 1
    cells[...] = jnp.zeros(cells.shape, F32)
    order = (5, 6, 8, 9, 10, 11)
    for plane, wide, at, count in raw_chunks():
        for rad in range(4):
            cells[order.index(plane), wide, :count, rad * LATS : (rad + 1) * LATS] = raw[
                rad * RAW + at : rad * RAW + at + count, :
            ]
    w = [None] + [
        weights([cells[2 + d, wide] for d in range(3)], cells[5, wide])
        for wide in range(1, WIDE - 1)
    ]
    made = []
    for part in range(2):
        now = [cells[part, wide] for wide in range(WIDE)]
        for phase in range(PHASES):
            fresh = list(now)
            for wide in range(phase + 1, WIDE - 1 - phase):
                c = now[wide]
                fresh[wide] = blend(
                    w[wide],
                    c,
                    jnp.where(bottom, 0.0, pltpu.roll(c, 1, axis=0)),
                    pltpu.roll(c, 7, axis=0),
                    now[wide - 1],
                    now[wide + 1],
                    jnp.where(first, 0.0, pltpu.roll(c, 1, axis=1)),
                    jnp.where(last, 0.0, pltpu.roll(c, span - 1, axis=1)),
                )
            now = fresh
        made.append(now[LONS : 2 * LONS])
    blon, blat = made
    for lon in range(LONS):
        c = blon[lon]
        source = jnp.where(first, 0.0, pltpu.roll(c, 1, axis=1)) - jnp.where(
            last, 0.0, pltpu.roll(c, span - 1, axis=1)
        )
        if lon < LONS - 1:
            source = source + blat[lon + 1]
        if lon > 0:
            source = source - blat[lon - 1]
        for rad in range(4):
            part = slice(rad * LATS, (rad + 1) * LATS)
            at = rad // 2 * 12 + rad % 2 * 4 + lon
            out[at : at + 1, :] = source[0:1, part]
            at = rad // 2 * 12 + 8 + rad % 2
            if lon == 0:
                out[at : at + 1, :] = blat[0][0:1, part]
            if lon == LONS - 1:
                out[at + 2 : at + 3, :] = blat[LONS - 1][0:1, part]


def base_body(spot, sent, out, cond):
    step = LATE - 16
    odd = spot[0] % 2 == 1
    for lon in range(LONS):
        at = 130 + lon
        lines = [sent[rad * SENT + at : rad * SENT + at + 1, :] for rad in range(4)]
        cond[lon : lon + 1, :] = jnp.where(odd, lines[2], lines[0])
        line = jnp.where(odd, lines[3], lines[1])
        out[pl.ds(lon, 32, stride=step), :] = jnp.broadcast_to(line, (32, LATS))
    lane = lax.broadcasted_iota(jnp.int32, (32, LATS), 1)
    owner = lax.broadcasted_iota(jnp.int32, (32, LATS), 0)
    for rad in range(4):
        for row in range(4):
            at = rad * SENT + row * 32
            out[pl.ds(4 + rad * 5 + row, 32, stride=step), :] = sent[at : at + 32, :]
        marks = []
        for slot in range(2):
            at = rad * SENT + 128 + slot
            line = jnp.broadcast_to(sent[at : at + 1, :], (32, LATS))
            marks.append(
                jnp.sum(jnp.where(lane == owner + spot[1] * 32, line, 0.0), axis=1, keepdims=True)
            )
        out[pl.ds(8 + rad * 5, 32, stride=step), :] = jnp.where(lane < 64, marks[0], marks[1])


def join_body(spot, one, two, cond, base, out, head, copies, sems):
    rest = pltpu.make_async_copy(base, out.at[:, pl.ds(16, LATE - 16), :], sems.at[0])
    rest.start()
    source = one[...] + two[...]
    head[:12, :] = jnp.where(spot[0] % 2 == 1, source[12:], source[:12])
    head[12:, :] = cond[...]
    mine = head[...]
    for owner in range(32):
        copies[owner] = mine
    move = pltpu.make_async_copy(copies, out.at[:, pl.ds(0, 16), :], sems.at[1])
    move.start()
    move.wait()
    rest.wait()


def join(spot, one, two, cond, base):
    vmem = pl.BlockSpec(memory_space=pltpu.VMEM)
    plain = pl.BlockSpec(memory_space=pl.ANY)
    return pl.pallas_call(
        join_body,
        out_shape=arr(32, LATE, LATS),
        in_specs=[pl.BlockSpec(memory_space=pltpu.SMEM), vmem, vmem, vmem, plain],
        out_specs=plain,
        scratch_shapes=[
            pltpu.VMEM((16, LATS), F32),
            pltpu.VMEM((32, 16, LATS), F32),
            pltpu.SemaphoreType.DMA((2,)),
        ],
        compiler_params=pltpu.CompilerParams(vmem_limit_bytes=4 * 2**20),
        cost_estimate=pl.CostEstimate(flops=10**5, bytes_accessed=10**6, transcendentals=0),
    )(spot, one, two, cond, base)


def half_body(late, out):
    for row in range(HALF):
        out[row] = late[pl.ds(row, 32, stride=LATE), :]


def mark_body(late, cells, hot, tall):
    lane = lax.broadcasted_iota(jnp.int32, (32, LATS), 1).astype(F32)
    for rad in range(4):
        marks = late[pl.ds(HALF + rad * 5 + 4, 32, stride=LATE), :]
        for slot in range(2):
            row = marks if slot == 0 else pltpu.roll(marks, 64, axis=1)
            tall[slot, rad * 32 : rad * 32 + 32, :] = jnp.where(row == lane, 1.0, 0.0)
            for half in range(2):
                cells[(rad * 2 + slot) * 2 + half] = late[
                    pl.ds(HALF + rad * 5 + 2 * slot + half, 32, stride=LATE), :
                ].astype(jnp.int32)
    for slot in range(2):
        hot[:, slot * LATS : (slot + 1) * LATS] = jnp.transpose(tall[slot])[:ROWS_OWN]


def chunks():
    found = []
    at = 0
    for wide in range(1, WIDE - 1):
        far = max(LONS - wide, wide - 2 * LONS + 1, 0)
        count = PHASES - far
        found.append((wide, at, count))
        at += count
    return found, at


def pack_body(low, own, high, up, down):
    found, rows = chunks()
    for plane in range(PLANES):
        for wide, start, count in found:
            ref = (low, own, high)[wide // LONS]
            up[plane, start : start + count, :] = ref[plane, wide % LONS, SHELLS - count :, :]
            down[plane, start : start + count, :] = ref[plane, wide % LONS, :count, :]
        up[plane, rows:, :] = jnp.zeros((32 - rows, LATS), F32)
        down[plane, rows:, :] = jnp.zeros((32 - rows, LATS), F32)


def main_body(low, own, high, above, below, from_low, from_high, out, cells, w, speeds):
    found, _ = chunks()
    lane = lax.broadcasted_iota(jnp.int32, (TALL, LATS), 1)

    def fill(plane, target):
        strip = jnp.where(lane % 8 < 4, from_low[plane], from_high[plane])
        for wide in range(WIDE):
            ref = (low, own, high)[wide // LONS]
            target[wide, :SHELLS, :LATS] = ref[plane, wide % LONS]
            target[wide, SHELLS:, :LATS] = jnp.zeros((TALL - SHELLS, LATS), F32)
            if 0 < wide < WIDE - 1:
                target[wide, :, LATS:] = halo_lanes(strip, wide)
            else:
                target[wide, :, LATS:] = jnp.zeros((TALL, LATS), F32)
        for wide, start, count in found:
            target[wide, SHELLS : SHELLS + count, :LATS] = above[plane, start : start + count, :]
            target[wide, TALL - count :, :LATS] = below[plane, start : start + count, :]

    for d in range(4):
        fill(FIELDS + d, speeds.at[d])
    for wide in range(1, WIDE - 1):
        made = weights([speeds[d, wide] for d in range(3)], speeds[3, wide])
        for i in range(7):
            w[i, wide] = made[i]

    def one(field, carry):
        fill(field, cells.at[0])
        for phase in range(PHASES):
            old = cells.at[phase % 2]
            new = cells.at[(phase + 1) % 2]
            for wide in range(phase + 1, WIDE - 1 - phase):
                c = old[wide]
                made = blend(
                    [w[i, wide] for i in range(7)],
                    c,
                    pltpu.roll(c, 1, axis=0),
                    pltpu.roll(c, TALL - 1, axis=0),
                    old[wide - 1],
                    old[wide + 1],
                    pltpu.roll(c, 1, axis=1),
                    pltpu.roll(c, 2 * LATS - 1, axis=1),
                )
                if phase == PHASES - 1:
                    out[field, pl.ds(wide - LONS, SHELLS, stride=LONS), :] = made[:SHELLS, :LATS]
                else:
                    new[wide] = made
        return carry

    lax.fori_loop(0, FIELDS, one, 0)


def slot_body(owners, rows, maps, conductance, out):
    count = owners.shape[1]
    here = lax.broadcasted_iota(jnp.int32, (count, count), 0)
    there = lax.broadcasted_iota(jnp.int32, (count, count), 1)
    aimed = (here % 32) * 4 + here // 32 == owners[...]
    earlier = jnp.dot(
        aimed.astype(jnp.bfloat16), (here < there).astype(jnp.bfloat16), preferred_element_type=F32
    )
    cell = maps[...]
    small = (cell & 127).astype(F32).astype(jnp.bfloat16)
    large = (cell >> 7).astype(F32).astype(jnp.bfloat16)
    row = jnp.broadcast_to((rows[...] + 1).astype(F32), (8, count)).astype(jnp.bfloat16)
    marks = []
    lines = []
    for slot in range(2):
        pick = jnp.where(aimed & (earlier == float(slot)), 1.0, 0.0).astype(jnp.bfloat16)
        marks.append(
            lax.dot_general(row, pick, (((1,), (1,)), ((), ())), preferred_element_type=F32) - 1.0
        )
        made = jnp.dot(pick, small, preferred_element_type=F32) + 128.0 * jnp.dot(
            pick, large, preferred_element_type=F32
        )
        lines += [made[:, :128], made[:, 128:]]
    for rad in range(4):
        for j in range(4):
            at = rad * SENT + j * 32
            out[at : at + 32, :] = lines[j][rad * 32 : rad * 32 + 32]
        at = rad * SENT + 128
        out[at : at + 1, :] = marks[0][:1]
        out[at + 1 : at + 2, :] = marks[1][:1]
        out[at + 2 : at + 6, :] = conductance[...]
        out[at + 6 : at + 8, :] = jnp.zeros((2, LATS), F32)


def final_body(
    spot, mine, other, cells, hot, pot, foot, phi, east_w, west_w, north_w, south_w, start, picked
):
    devs, rads = 32, 4
    wide = rads * LATS
    lane = lax.broadcasted_iota(jnp.int32, (devs, wide), 1)

    odd = spot[0] % 2

    def gather(at, step):
        found = []
        for rad in range(rads):
            row = at + rad % 2 * step
            found.append(jnp.where(odd == rad // 2, mine[row], other[row]))
        return jnp.concatenate(found, axis=1)

    def lon_up(values, lon):
        return values[lon + 1] if lon < LONS - 1 else pltpu.roll(values[0], devs - 1, axis=0)

    def lon_down(values, lon):
        return values[lon - 1] if lon > 0 else pltpu.roll(values[LONS - 1], 1, axis=0)

    def lat_up(value):
        return pltpu.roll(value, wide - 1, axis=1)

    def lat_down(value):
        return pltpu.roll(value, 1, axis=1)

    cond = [gather(12 + lon, 4) for lon in range(LONS)]
    sources = [gather(lon, 4) for lon in range(LONS)]
    sources[LONS - 1] += pltpu.roll(gather(8, 1), devs - 1, axis=0)
    sources[0] -= pltpu.roll(gather(10, 1), 1, axis=0)
    last, first = lane == wide - 1, lane == 0
    for lon in range(LONS):
        source = sources[lon]
        c = cond[lon]
        east = 0.5 * (c + lon_up(cond, lon))
        west = 0.5 * (c + lon_down(cond, lon))
        north = 0.5 * (c + jnp.where(last, 0.0, lat_up(c)))
        south = 0.5 * (c + jnp.where(first, 0.0, lat_down(c)))
        scale = RELAX / (DAMPING * c + east + west + north + south)
        east_w[lon] = east * scale
        west_w[lon] = west * scale
        north_w[lon] = jnp.where(last, 0.0, north * scale)
        south_w[lon] = jnp.where(first, 0.0, south * scale)
        start[lon] = source * scale
        phi[0, lon] = source * scale

    def sweep(old, new):
        values = [phi[old, lon] for lon in range(LONS)]
        for lon in range(LONS):
            c = values[lon]
            phi[new, lon] = (
                (1.0 - RELAX) * c
                + start[lon]
                + (east_w[lon] * lon_up(values, lon) + west_w[lon] * lon_down(values, lon))
                + (north_w[lon] * lat_up(c) + south_w[lon] * lat_down(c))
            )

    for turn in range(SWEEPS - 1):
        sweep(turn % 2, (turn + 1) % 2)
    done = (SWEEPS - 1) % 2
    at_lon = lax.broadcasted_iota(jnp.int32, (devs, LATS), 0) == spot[2]
    for rad in range(rads):

        @pl.when(spot[1] == rad)
        def _():
            for lon in range(LONS):
                block = phi[done, lon, :, rad * LATS : (rad + 1) * LATS]
                pot[lon : lon + 1, :] = jnp.sum(
                    jnp.where(at_lon, block, 0.0), axis=0, keepdims=True
                )

    for rad in range(rads):
        table = [phi[done, lon, :, rad * LATS : (rad + 1) * LATS] for lon in range(LONS)]
        for slot in range(2):
            at = (slot * rads + rad) * devs
            for half in range(2):
                cell = cells[(rad * 2 + slot) * 2 + half]
                place, lon_at = cell & 127, cell >> 7
                value = jnp.zeros((devs, LATS), F32)
                for lon in range(LONS):
                    found = jnp.take_along_axis(
                        table[lon], place, axis=1, mode="promise_in_bounds"
                    )
                    value = jnp.where(lon_at == lon, found, value)
                picked[at : at + devs, 128 * half : 128 * half + 128] = value
    records = picked[...]
    rows = hot[...].astype(jnp.bfloat16)
    large = records.astype(jnp.bfloat16)
    small = (records - large.astype(F32)).astype(jnp.bfloat16)
    foot[...] = jnp.dot(rows, large, preferred_element_type=F32) + jnp.dot(
        rows, small, preferred_element_type=F32
    )


def shards(plasma_fields, velocity, resistivity, conductance, foot_map, foot_owner, foot_row):
    spot = jnp.stack([lax.axis_index("sec"), lax.axis_index("rad"), lax.axis_index("lon")])
    own, slots = first(
        plasma_fields.reshape(FIELDS, SHELLS * LONS, LATS),
        velocity,
        resistivity,
        foot_owner.reshape(1, -1),
        foot_row.reshape(1, -1),
        foot_map,
        conductance,
    )
    count = lax.axis_size("lon")
    wrap = [(i, (i + (1 if i % 2 else -1)) % count) for i in range(count)]
    first_swap = lax.ppermute(own, "lon", wrap)
    second_swap = lax.ppermute(own, "lon", [(i, i ^ 1) for i in range(count)])

    sent = lax.all_to_all(
        slots.reshape(4, SENT, LATS), "rad", split_axis=0, concat_axis=0, tiled=True
    )

    first_swap, second_swap, sent = lax.optimization_barrier((first_swap, second_swap, sent))
    odd = lax.axis_index("lon") % 2 == 1
    low = jnp.where(odd, second_swap, first_swap)
    high = jnp.where(odd, first_swap, second_swap)
    up, down = call(pack_body, (arr(PLANES, 32, LATS), arr(PLANES, 32, LATS)), (low, own, high))
    above = lax.ppermute(down, "sec", shift("sec", -1, False))
    below = lax.ppermute(up, "sec", shift("sec", 1, False))
    raw = call(raw_body, arr(4 * RAW, LATS), (low, own, high))
    owner = lax.axis_index("sec") == 0

    def advance_inner(rows):
        gathered = lax.all_to_all(
            rows.reshape(4, RAW, LATS), "rad", split_axis=0, concat_axis=0, tiled=True
        )
        return call(
            inner_body,
            arr(24, LATS),
            (gathered.reshape(4 * RAW, LATS),),
            scratch=(pltpu.VMEM((6, WIDE, 8, 4 * LATS), F32),),
        )

    inner = lax.cond(owner, advance_inner, lambda rows: jnp.zeros((24, LATS), F32), raw)
    inner, below, above = lax.optimization_barrier((inner, below, above))
    far = lax.ppermute(inner, "sec", [(0, 3)])
    far = inner + far
    near = lax.ppermute(far, "sec", [(0, 1), (3, 2)])
    base, cond = call(
        base_body,
        (arr(32 * (LATE - 16), LATS), arr(LONS, LATS)),
        (spot, sent.reshape(4 * SENT, LATS)),
        smem=(0,),
    )
    late = join(spot, far, near, cond, base.reshape(32, LATE - 16, LATS))
    late, low, high = lax.optimization_barrier((late, low, high))

    blocks = (low, own, high, above, below)
    edges = call(
        edge_body,
        arr(PLANES, TALL, LATS),
        blocks,
        scratch=(pltpu.VMEM((PLANES, WIDE, TALL, LATS), F32),),
    )
    from_low = lax.ppermute(edges, "rad", shift("rad", 1, False))
    from_high = lax.ppermute(edges, "rad", shift("rad", -1, False))
    late = lax.all_to_all(
        late, "lon", split_axis=0, concat_axis=0, tiled=True
    )

    advanced = call(
        main_body,
        arr(FIELDS, SHELLS * LONS, LATS),
        blocks + (from_low, from_high),
        scratch=(
            pltpu.VMEM((2, WIDE, TALL, 2 * LATS), F32),
            pltpu.VMEM((7, WIDE, TALL, 2 * LATS), F32),
            pltpu.VMEM((4, WIDE, TALL, 2 * LATS), F32),
        ),
    ).reshape(FIELDS, SHELLS, LONS, LATS)

    late, advanced = lax.optimization_barrier((late, advanced))
    late = late.reshape(32 * LATE, LATS)
    mine = call(half_body, arr(HALF, 32, LATS), (late,))
    other = lax.ppermute(mine, "sec", [(0, 1), (1, 0), (2, 3), (3, 2)])
    cells, hot = call(
        mark_body,
        (jax.ShapeDtypeStruct((16, 32, LATS), jnp.int32), arr(ROWS_OWN, 2 * LATS)),
        (late,),
        scratch=(pltpu.VMEM((2, LATS, LATS), F32),),
    )
    plane = pltpu.VMEM((LONS, 32, 4 * LATS), F32)
    potential, foot_table = call(
        final_body,
        (arr(LONS, LATS), arr(ROWS_OWN, 256)),
        (spot, mine, other, cells, hot),
        scratch=(
            pltpu.VMEM((2, LONS, 32, 4 * LATS), F32),
            plane,
            plane,
            plane,
            plane,
            plane,
            pltpu.VMEM((256, 256), F32),
        ),
        smem=(0,),
    )
    return (advanced, potential, foot_table)


def solution(mesh):
    in_specs = (
        P(None, "sec", "lon", "rad"),
        P(None, "sec", "lon", "rad"),
        P("sec", "lon", "rad"),
        P("lon", "rad"),
        P(("lon", "sec", "rad"), None),
        P(("lon", "sec", "rad"), None),
        P(("lon", "sec", "rad")),
    )
    out_specs = (P(None, "sec", "lon", "rad"), P("lon", "rad"), P(("lon", "sec", "rad"), None))
    return jax.shard_map(shards, mesh=mesh, in_specs=in_specs, out_specs=out_specs, check_vma=False)
```

```python
import jax
import jax.numpy as jnp
from jax import lax
from jax.experimental import pallas as pl
from jax.experimental.pallas import tpu as pltpu
from jax.sharding import PartitionSpec as P

PHASES = 4
SWEEPS = 8
ROWS_OWN = 32
COURANT = 0.25
DAMPING = 0.05
RELAX = 0.8

FIELDS = 8
PLANES = FIELDS + 4
SHELLS = 16
LONS = 4
LATS = 128
WIDE = 3 * LONS
LATE = 40
HALF = 20
RAW = 192
SENT = 136
TALL = SHELLS + 2 * PHASES
F32 = jnp.float32


def call(body, out_shape, args, scratch=(), smem=(), flops=10**6, traffic=10**6):
    specs = [
        pl.BlockSpec(memory_space=pltpu.SMEM if i in smem else pltpu.VMEM)
        for i in range(len(args))
    ]
    many = isinstance(out_shape, (tuple, list))
    vmem = pl.BlockSpec(memory_space=pltpu.VMEM)
    return pl.pallas_call(
        body,
        out_shape=out_shape,
        in_specs=specs,
        out_specs=[vmem] * len(out_shape) if many else vmem,
        scratch_shapes=list(scratch),
        compiler_params=pltpu.CompilerParams(vmem_limit_bytes=16 * 2**20),
        cost_estimate=pl.CostEstimate(flops=flops, bytes_accessed=traffic, transcendentals=0),
    )(*args)


def arr(*shape):
    return jax.ShapeDtypeStruct(shape, F32)


def shift(axis, step, closed):
    count = lax.axis_size(axis)
    return [
        (i, (i + step) % count) for i in range(count) if closed or 0 <= i + step < count
    ]


def first_body(*refs):
    sources, (own, slots, plain), held, sems = refs[:7], refs[7:10], refs[10:17], refs[17]
    moves = [
        pltpu.make_async_copy(source, target, sems.at[i])
        for i, (source, target) in enumerate(zip(sources, held))
    ]
    for move in moves:
        move.start()
    fields, speeds, resist, owners, rows, maps, conductance = held
    for move in moves[1:3]:
        move.wait()
    for plane in range(4):
        for shell in range(SHELLS):
            found = speeds[plane, shell] if plane < 3 else resist[shell]
            plain[plane, shell * LONS : shell * LONS + LONS, :] = found.astype(F32)
    moves[0].wait()
    for plane in range(PLANES):
        for lon in range(LONS):
            at = pl.ds(lon, SHELLS, stride=LONS)
            if plane < FIELDS:
                own[plane, lon] = fields[plane, at, :]
            else:
                own[plane, lon] = plain[plane - FIELDS, at, :]
    for move in moves[3:]:
        move.wait()
    slot_body(owners, rows, maps, conductance, slots)


def first(*args):
    vmem = pl.BlockSpec(memory_space=pltpu.VMEM)
    return pl.pallas_call(
        first_body,
        out_shape=(arr(PLANES, LONS, SHELLS, LATS), arr(4 * SENT, LATS)),
        in_specs=[pl.BlockSpec(memory_space=pltpu.HBM)] * len(args),
        out_specs=[vmem, vmem],
        scratch_shapes=[pltpu.VMEM((4, SHELLS * LONS, LATS), F32)]
        + [pltpu.VMEM(arg.shape, arg.dtype) for arg in args]
        + [pltpu.SemaphoreType.DMA((len(args),))],
        compiler_params=pltpu.CompilerParams(vmem_limit_bytes=60 * 2**20),
        cost_estimate=pl.CostEstimate(flops=10**6, bytes_accessed=10**6, transcendentals=0),
    )(*args)


def edge_body(low, own, high, above, below, edges, tall):
    found, _ = chunks()
    group = lax.broadcasted_iota(jnp.int32, (TALL, LATS), 1) // 8
    for plane in range(PLANES):
        for wide in range(WIDE):
            ref = (low, own, high)[wide // LONS]
            tall[plane, wide, :SHELLS, :] = ref[plane, wide % LONS]
            tall[plane, wide, SHELLS:, :] = jnp.zeros((TALL - SHELLS, LATS), F32)
        for wide, start, count in found:
            tall[plane, wide, SHELLS : SHELLS + count, :] = above[plane, start : start + count, :]
            tall[plane, wide, TALL - count :, :] = below[plane, start : start + count, :]
    for plane in range(PLANES):
        packed = jnp.zeros((TALL, LATS), F32)
        for wide in range(1, WIDE - 1):
            turned = pltpu.roll(tall[plane, wide], 8 * wide + 4, axis=1)
            packed = jnp.where(group == wide, turned, packed)
        edges[plane] = packed


def halo_lanes(edges, wide):
    lane = lax.broadcasted_iota(jnp.int32, edges.shape, 1)
    turned = pltpu.roll(edges, (LATS - 8 * wide - 4) % LATS, axis=1)
    return jnp.where((lane < 4) | (lane >= LATS - 4), turned, 0.0)


def weights(speeds, resist):
    out = []
    total = None
    for speed in speeds:
        lower = COURANT * jnp.maximum(speed, 0.0) + resist
        upper = resist - COURANT * jnp.minimum(speed, 0.0)
        out += [lower, upper]
        total = lower + upper if total is None else total + lower + upper
    return [1.0 - total] + out


def blend(w, centre, shell_lo, shell_hi, lon_lo, lon_hi, lat_lo, lat_hi):
    return (
        w[0] * centre
        + (w[1] * shell_lo + w[2] * shell_hi)
        + (w[3] * lon_lo + w[4] * lon_hi)
        + (w[5] * lat_lo + w[6] * lat_hi)
    )


def raw_chunks():
    found = []
    at = 0
    for plane in (5, 6, 8, 9, 10, 11):
        reach = PHASES + 1 if plane < FIELDS else PHASES
        for wide in range(WIDE):
            count = reach - max(LONS - wide, wide - 2 * LONS + 1, 0)
            if count > 0:
                found.append((plane, wide, at, count))
                at += count
    return found


def raw_body(low, own, high, out):
    for plane, wide, at, count in raw_chunks():
        ref = (low, own, high)[wide // LONS]
        for block in range(4):
            row = block * RAW + at
            out[row : row + count, :] = ref[plane, wide % LONS, :count, :]


def inner_body(raw, out, cells):
    span = 4 * LATS
    lane = lax.broadcasted_iota(jnp.int32, (8, span), 1)
    bottom = lax.broadcasted_iota(jnp.int32, (8, span), 0) == 0
    first, last = lane == 0, lane == span - 1
    cells[...] = jnp.zeros(cells.shape, F32)
    order = (5, 6, 8, 9, 10, 11)
    for plane, wide, at, count in raw_chunks():
        for rad in range(4):
            cells[order.index(plane), wide, :count, rad * LATS : (rad + 1) * LATS] = raw[
                rad * RAW + at : rad * RAW + at + count, :
            ]
    w = [None] + [
        weights([cells[2 + d, wide] for d in range(3)], cells[5, wide])
        for wide in range(1, WIDE - 1)
    ]
    made = []
    for part in range(2):
        now = [cells[part, wide] for wide in range(WIDE)]
        for phase in range(PHASES):
            fresh = list(now)
            for wide in range(phase + 1, WIDE - 1 - phase):
                c = now[wide]
                fresh[wide] = blend(
                    w[wide],
                    c,
                    jnp.where(bottom, 0.0, pltpu.roll(c, 1, axis=0)),
                    pltpu.roll(c, 7, axis=0),
                    now[wide - 1],
                    now[wide + 1],
                    jnp.where(first, 0.0, pltpu.roll(c, 1, axis=1)),
                    jnp.where(last, 0.0, pltpu.roll(c, span - 1, axis=1)),
                )
            now = fresh
        made.append(now[LONS : 2 * LONS])
    blon, blat = made
    for lon in range(LONS):
        c = blon[lon]
        source = jnp.where(first, 0.0, pltpu.roll(c, 1, axis=1)) - jnp.where(
            last, 0.0, pltpu.roll(c, span - 1, axis=1)
        )
        if lon < LONS - 1:
            source = source + blat[lon + 1]
        if lon > 0:
            source = source - blat[lon - 1]
        for rad in range(4):
            part = slice(rad * LATS, (rad + 1) * LATS)
            at = rad // 2 * 12 + rad % 2 * 4 + lon
            out[at : at + 1, :] = source[0:1, part]
            at = rad // 2 * 12 + 8 + rad % 2
            if lon == 0:
                out[at : at + 1, :] = blat[0][0:1, part]
            if lon == LONS - 1:
                out[at + 2 : at + 3, :] = blat[LONS - 1][0:1, part]


def base_body(spot, sent, out, cond):
    step = LATE - 16
    odd = spot[0] % 2 == 1
    for lon in range(LONS):
        at = 130 + lon
        lines = [sent[rad * SENT + at : rad * SENT + at + 1, :] for rad in range(4)]
        cond[lon : lon + 1, :] = jnp.where(odd, lines[2], lines[0])
        line = jnp.where(odd, lines[3], lines[1])
        out[pl.ds(lon, 32, stride=step), :] = jnp.broadcast_to(line, (32, LATS))
    lane = lax.broadcasted_iota(jnp.int32, (32, LATS), 1)
    owner = lax.broadcasted_iota(jnp.int32, (32, LATS), 0)
    for rad in range(4):
        for row in range(4):
            at = rad * SENT + row * 32
            out[pl.ds(4 + rad * 5 + row, 32, stride=step), :] = sent[at : at + 32, :]
        marks = []
        for slot in range(2):
            at = rad * SENT + 128 + slot
            line = jnp.broadcast_to(sent[at : at + 1, :], (32, LATS))
            marks.append(
                jnp.sum(jnp.where(lane == owner + spot[1] * 32, line, 0.0), axis=1, keepdims=True)
            )
        out[pl.ds(8 + rad * 5, 32, stride=step), :] = jnp.where(lane < 64, marks[0], marks[1])


def join_body(spot, one, two, cond, base, out, head, copies, sems):
    rest = pltpu.make_async_copy(base, out.at[:, pl.ds(16, LATE - 16), :], sems.at[0])
    rest.start()
    source = one[...] + two[...]
    head[:12, :] = jnp.where(spot[0] % 2 == 1, source[12:], source[:12])
    head[12:, :] = cond[...]
    mine = head[...]
    for owner in range(32):
        copies[owner] = mine
    move = pltpu.make_async_copy(copies, out.at[:, pl.ds(0, 16), :], sems.at[1])
    move.start()
    move.wait()
    rest.wait()


def join(spot, one, two, cond, base):
    vmem = pl.BlockSpec(memory_space=pltpu.VMEM)
    plain = pl.BlockSpec(memory_space=pl.ANY)
    return pl.pallas_call(
        join_body,
        out_shape=arr(32, LATE, LATS),
        in_specs=[pl.BlockSpec(memory_space=pltpu.SMEM), vmem, vmem, vmem, plain],
        out_specs=plain,
        scratch_shapes=[
            pltpu.VMEM((16, LATS), F32),
            pltpu.VMEM((32, 16, LATS), F32),
            pltpu.SemaphoreType.DMA((2,)),
        ],
        compiler_params=pltpu.CompilerParams(vmem_limit_bytes=4 * 2**20),
        cost_estimate=pl.CostEstimate(flops=10**5, bytes_accessed=10**6, transcendentals=0),
    )(spot, one, two, cond, base)


def half_body(late, out):
    for row in range(HALF):
        out[row] = late[pl.ds(row, 32, stride=LATE), :]


def mark_body(late, cells, hot, tall):
    lane = lax.broadcasted_iota(jnp.int32, (32, LATS), 1).astype(F32)
    for rad in range(4):
        marks = late[pl.ds(HALF + rad * 5 + 4, 32, stride=LATE), :]
        for slot in range(2):
            row = marks if slot == 0 else pltpu.roll(marks, 64, axis=1)
            tall[slot, rad * 32 : rad * 32 + 32, :] = jnp.where(row == lane, 1.0, 0.0)
            for half in range(2):
                cells[(rad * 2 + slot) * 2 + half] = late[
                    pl.ds(HALF + rad * 5 + 2 * slot + half, 32, stride=LATE), :
                ].astype(jnp.int32)
    for slot in range(2):
        hot[:, slot * LATS : (slot + 1) * LATS] = jnp.transpose(tall[slot])[:ROWS_OWN]


def chunks():
    found = []
    at = 0
    for wide in range(1, WIDE - 1):
        far = max(LONS - wide, wide - 2 * LONS + 1, 0)
        count = PHASES - far
        found.append((wide, at, count))
        at += count
    return found, at


def pack_body(spot, low, own, high, near, away):
    found, rows = chunks()
    odd = spot[0] % 2 == 1
    for plane in range(PLANES):
        for wide, start, count in found:
            ref = (low, own, high)[wide // LONS]
            up = ref[plane, wide % LONS, SHELLS - count :, :]
            down = ref[plane, wide % LONS, :count, :]
            near[plane, start : start + count, :] = jnp.where(odd, down, up)
            away[plane, start : start + count, :] = jnp.where(odd, up, down)
        near[plane, rows:, :] = jnp.zeros((32 - rows, LATS), F32)
        away[plane, rows:, :] = jnp.zeros((32 - rows, LATS), F32)


def main_body(low, own, high, above, below, from_low, from_high, out, cells, w, speeds):
    found, _ = chunks()
    lane = lax.broadcasted_iota(jnp.int32, (TALL, LATS), 1)

    def fill(plane, target):
        strip = jnp.where(lane % 8 < 4, from_low[plane], from_high[plane])
        for wide in range(WIDE):
            ref = (low, own, high)[wide // LONS]
            target[wide, :SHELLS, :LATS] = ref[plane, wide % LONS]
            target[wide, SHELLS:, :LATS] = jnp.zeros((TALL - SHELLS, LATS), F32)
            if 0 < wide < WIDE - 1:
                target[wide, :, LATS:] = halo_lanes(strip, wide)
            else:
                target[wide, :, LATS:] = jnp.zeros((TALL, LATS), F32)
        for wide, start, count in found:
            target[wide, SHELLS : SHELLS + count, :LATS] = above[plane, start : start + count, :]
            target[wide, TALL - count :, :LATS] = below[plane, start : start + count, :]

    for d in range(4):
        fill(FIELDS + d, speeds.at[d])
    for wide in range(1, WIDE - 1):
        made = weights([speeds[d, wide] for d in range(3)], speeds[3, wide])
        for i in range(7):
            w[i, wide] = made[i]

    def one(field, carry):
        fill(field, cells.at[0])
        for phase in range(PHASES):
            old = cells.at[phase % 2]
            new = cells.at[(phase + 1) % 2]
            for wide in range(phase + 1, WIDE - 1 - phase):
                c = old[wide]
                made = blend(
                    [w[i, wide] for i in range(7)],
                    c,
                    pltpu.roll(c, 1, axis=0),
                    pltpu.roll(c, TALL - 1, axis=0),
                    old[wide - 1],
                    old[wide + 1],
                    pltpu.roll(c, 1, axis=1),
                    pltpu.roll(c, 2 * LATS - 1, axis=1),
                )
                if phase == PHASES - 1:
                    out[field, pl.ds(wide - LONS, SHELLS, stride=LONS), :] = made[:SHELLS, :LATS]
                else:
                    new[wide] = made
        return carry

    lax.fori_loop(0, FIELDS, one, 0)


def slot_body(owners, rows, maps, conductance, out):
    count = owners.shape[1]
    here = lax.broadcasted_iota(jnp.int32, (count, count), 0)
    there = lax.broadcasted_iota(jnp.int32, (count, count), 1)
    aimed = (here % 32) * 4 + here // 32 == owners[...]
    earlier = jnp.dot(
        aimed.astype(jnp.bfloat16), (here < there).astype(jnp.bfloat16), preferred_element_type=F32
    )
    cell = maps[...]
    small = (cell & 127).astype(F32).astype(jnp.bfloat16)
    large = (cell >> 7).astype(F32).astype(jnp.bfloat16)
    row = jnp.broadcast_to((rows[...] + 1).astype(F32), (8, count)).astype(jnp.bfloat16)
    marks = []
    lines = []
    for slot in range(2):
        pick = jnp.where(aimed & (earlier == float(slot)), 1.0, 0.0).astype(jnp.bfloat16)
        marks.append(
            lax.dot_general(row, pick, (((1,), (1,)), ((), ())), preferred_element_type=F32) - 1.0
        )
        made = jnp.dot(pick, small, preferred_element_type=F32) + 128.0 * jnp.dot(
            pick, large, preferred_element_type=F32
        )
        lines += [made[:, :128], made[:, 128:]]
    for rad in range(4):
        for j in range(4):
            at = rad * SENT + j * 32
            out[at : at + 32, :] = lines[j][rad * 32 : rad * 32 + 32]
        at = rad * SENT + 128
        out[at : at + 1, :] = marks[0][:1]
        out[at + 1 : at + 2, :] = marks[1][:1]
        out[at + 2 : at + 6, :] = conductance[...]
        out[at + 6 : at + 8, :] = jnp.zeros((2, LATS), F32)


def final_body(
    spot, mine, other, cells, hot, pot, foot, phi, east_w, west_w, north_w, south_w, start, picked
):
    devs, rads = 32, 4
    wide = rads * LATS
    lane = lax.broadcasted_iota(jnp.int32, (devs, wide), 1)

    odd = spot[0] % 2

    def gather(at, step):
        found = []
        for rad in range(rads):
            row = at + rad % 2 * step
            found.append(jnp.where(odd == rad // 2, mine[row], other[row]))
        return jnp.concatenate(found, axis=1)

    def lon_up(values, lon):
        return values[lon + 1] if lon < LONS - 1 else pltpu.roll(values[0], devs - 1, axis=0)

    def lon_down(values, lon):
        return values[lon - 1] if lon > 0 else pltpu.roll(values[LONS - 1], 1, axis=0)

    def lat_up(value):
        return pltpu.roll(value, wide - 1, axis=1)

    def lat_down(value):
        return pltpu.roll(value, 1, axis=1)

    cond = [gather(12 + lon, 4) for lon in range(LONS)]
    sources = [gather(lon, 4) for lon in range(LONS)]
    sources[LONS - 1] += pltpu.roll(gather(8, 1), devs - 1, axis=0)
    sources[0] -= pltpu.roll(gather(10, 1), 1, axis=0)
    last, first = lane == wide - 1, lane == 0
    for lon in range(LONS):
        source = sources[lon]
        c = cond[lon]
        east = 0.5 * (c + lon_up(cond, lon))
        west = 0.5 * (c + lon_down(cond, lon))
        north = 0.5 * (c + jnp.where(last, 0.0, lat_up(c)))
        south = 0.5 * (c + jnp.where(first, 0.0, lat_down(c)))
        scale = RELAX / (DAMPING * c + east + west + north + south)
        east_w[lon] = east * scale
        west_w[lon] = west * scale
        north_w[lon] = jnp.where(last, 0.0, north * scale)
        south_w[lon] = jnp.where(first, 0.0, south * scale)
        start[lon] = source * scale
        phi[0, lon] = source * scale

    def sweep(old, new):
        values = [phi[old, lon] for lon in range(LONS)]
        for lon in range(LONS):
            c = values[lon]
            phi[new, lon] = (
                (1.0 - RELAX) * c
                + start[lon]
                + (east_w[lon] * lon_up(values, lon) + west_w[lon] * lon_down(values, lon))
                + (north_w[lon] * lat_up(c) + south_w[lon] * lat_down(c))
            )

    for turn in range(SWEEPS - 1):
        sweep(turn % 2, (turn + 1) % 2)
    done = (SWEEPS - 1) % 2
    at_lon = lax.broadcasted_iota(jnp.int32, (devs, LATS), 0) == spot[2]
    for rad in range(rads):

        @pl.when(spot[1] == rad)
        def _():
            for lon in range(LONS):
                block = phi[done, lon, :, rad * LATS : (rad + 1) * LATS]
                pot[lon : lon + 1, :] = jnp.sum(
                    jnp.where(at_lon, block, 0.0), axis=0, keepdims=True
                )

    for rad in range(rads):
        table = [phi[done, lon, :, rad * LATS : (rad + 1) * LATS] for lon in range(LONS)]
        for slot in range(2):
            at = (slot * rads + rad) * devs
            for half in range(2):
                cell = cells[(rad * 2 + slot) * 2 + half]
                place, lon_at = cell & 127, cell >> 7
                value = jnp.zeros((devs, LATS), F32)
                for lon in range(LONS):
                    found = jnp.take_along_axis(
                        table[lon], place, axis=1, mode="promise_in_bounds"
                    )
                    value = jnp.where(lon_at == lon, found, value)
                picked[at : at + devs, 128 * half : 128 * half + 128] = value
    records = picked[...]
    rows = hot[...].astype(jnp.bfloat16)
    large = records.astype(jnp.bfloat16)
    small = (records - large.astype(F32)).astype(jnp.bfloat16)
    foot[...] = jnp.dot(rows, large, preferred_element_type=F32) + jnp.dot(
        rows, small, preferred_element_type=F32
    )


def shards(plasma_fields, velocity, resistivity, conductance, foot_map, foot_owner, foot_row):
    spot = jnp.stack([lax.axis_index("sec"), lax.axis_index("rad"), lax.axis_index("lon")])
    own, slots = first(
        plasma_fields.reshape(FIELDS, SHELLS * LONS, LATS),
        velocity,
        resistivity,
        foot_owner.reshape(1, -1),
        foot_row.reshape(1, -1),
        foot_map,
        conductance,
    )
    count = lax.axis_size("lon")
    wrap = [(i, (i + (1 if i % 2 else -1)) % count) for i in range(count)]
    first_swap = lax.ppermute(own, "lon", wrap)
    second_swap = lax.ppermute(own, "lon", [(i, i ^ 1) for i in range(count)])

    sent = lax.all_to_all(
        slots.reshape(4, SENT, LATS), "rad", split_axis=0, concat_axis=0, tiled=True
    )

    first_swap, second_swap, sent = lax.optimization_barrier((first_swap, second_swap, sent))
    odd = lax.axis_index("lon") % 2 == 1
    low = jnp.where(odd, second_swap, first_swap)
    high = jnp.where(odd, first_swap, second_swap)
    near_rows, away_rows = call(
        pack_body,
        (arr(PLANES, 32, LATS), arr(PLANES, 32, LATS)),
        (spot, low, own, high),
        smem=(0,),
    )
    away_rows = lax.ppermute(away_rows, "sec", [(1, 2), (2, 1)])
    raw = call(raw_body, arr(4 * RAW, LATS), (low, own, high))
    owner = lax.axis_index("sec") == 0

    def advance_inner(rows):
        gathered = lax.all_to_all(
            rows.reshape(4, RAW, LATS), "rad", split_axis=0, concat_axis=0, tiled=True
        )
        return call(
            inner_body,
            arr(24, LATS),
            (gathered.reshape(4 * RAW, LATS),),
            scratch=(pltpu.VMEM((6, WIDE, 8, 4 * LATS), F32),),
        )

    inner = lax.cond(owner, advance_inner, lambda rows: jnp.zeros((24, LATS), F32), raw)
    away_rows, inner = lax.optimization_barrier((away_rows, inner))
    far = lax.ppermute(inner, "sec", [(0, 3)])
    far = inner + far
    near = lax.ppermute(far, "sec", [(0, 1), (3, 2)])
    base, cond = call(
        base_body,
        (arr(32 * (LATE - 16), LATS), arr(LONS, LATS)),
        (spot, sent.reshape(4 * SENT, LATS)),
        smem=(0,),
    )
    late = join(spot, far, near, cond, base.reshape(32, LATE - 16, LATS))
    late, low, high, near_rows = lax.optimization_barrier((late, low, high, near_rows))
    near_rows = lax.ppermute(near_rows, "sec", [(0, 1), (1, 0), (2, 3), (3, 2)])

    odd = lax.axis_index("sec") % 2 == 1
    above = jnp.where(odd, away_rows, near_rows)
    below = jnp.where(odd, near_rows, away_rows)
    blocks = (low, own, high, above, below)
    edges = call(
        edge_body,
        arr(PLANES, TALL, LATS),
        blocks,
        scratch=(pltpu.VMEM((PLANES, WIDE, TALL, LATS), F32),),
    )
    from_low = lax.ppermute(edges, "rad", shift("rad", 1, False))
    from_high = lax.ppermute(edges, "rad", shift("rad", -1, False))
    late = lax.all_to_all(
        late, "lon", split_axis=0, concat_axis=0, tiled=True
    )

    advanced = call(
        main_body,
        arr(FIELDS, SHELLS * LONS, LATS),
        blocks + (from_low, from_high),
        scratch=(
            pltpu.VMEM((2, WIDE, TALL, 2 * LATS), F32),
            pltpu.VMEM((7, WIDE, TALL, 2 * LATS), F32),
            pltpu.VMEM((4, WIDE, TALL, 2 * LATS), F32),
        ),
    ).reshape(FIELDS, SHELLS, LONS, LATS)

    late, advanced = lax.optimization_barrier((late, advanced))
    late = late.reshape(32 * LATE, LATS)
    mine = call(half_body, arr(HALF, 32, LATS), (late,))
    other = lax.ppermute(mine, "sec", [(0, 1), (1, 0), (2, 3), (3, 2)])
    cells, hot = call(
        mark_body,
        (jax.ShapeDtypeStruct((16, 32, LATS), jnp.int32), arr(ROWS_OWN, 2 * LATS)),
        (late,),
        scratch=(pltpu.VMEM((2, LATS, LATS), F32),),
    )
    plane = pltpu.VMEM((LONS, 32, 4 * LATS), F32)
    potential, foot_table = call(
        final_body,
        (arr(LONS, LATS), arr(ROWS_OWN, 256)),
        (spot, mine, other, cells, hot),
        scratch=(
            pltpu.VMEM((2, LONS, 32, 4 * LATS), F32),
            plane,
            plane,
            plane,
            plane,
            plane,
            pltpu.VMEM((256, 256), F32),
        ),
        smem=(0,),
    )
    return (advanced, potential, foot_table)


def solution(mesh):
    in_specs = (
        P(None, "sec", "lon", "rad"),
        P(None, "sec", "lon", "rad"),
        P("sec", "lon", "rad"),
        P("lon", "rad"),
        P(("lon", "sec", "rad"), None),
        P(("lon", "sec", "rad"), None),
        P(("lon", "sec", "rad")),
    )
    out_specs = (P(None, "sec", "lon", "rad"), P("lon", "rad"), P(("lon", "sec", "rad"), None))
    return jax.shard_map(shards, mesh=mesh, in_specs=in_specs, out_specs=out_specs, check_vma=False)
```

```python
import jax
import jax.numpy as jnp
from jax import lax
from jax.experimental import pallas as pl
from jax.experimental.pallas import tpu as pltpu
from jax.sharding import PartitionSpec as P

PHASES = 4
SWEEPS = 8
ROWS_OWN = 32
COURANT = 0.25
DAMPING = 0.05
RELAX = 0.8

FIELDS = 8
PLANES = FIELDS + 4
SHELLS = 16
LONS = 4
LATS = 128
WIDE = 3 * LONS
LATE = 40
HALF = 20
RAW = 192
SENT = 136
TALL = SHELLS + 2 * PHASES
F32 = jnp.float32


def call(body, out_shape, args, scratch=(), smem=(), flops=10**6, traffic=10**6):
    specs = [
        pl.BlockSpec(memory_space=pltpu.SMEM if i in smem else pltpu.VMEM)
        for i in range(len(args))
    ]
    many = isinstance(out_shape, (tuple, list))
    vmem = pl.BlockSpec(memory_space=pltpu.VMEM)
    return pl.pallas_call(
        body,
        out_shape=out_shape,
        in_specs=specs,
        out_specs=[vmem] * len(out_shape) if many else vmem,
        scratch_shapes=list(scratch),
        compiler_params=pltpu.CompilerParams(vmem_limit_bytes=16 * 2**20),
        cost_estimate=pl.CostEstimate(flops=flops, bytes_accessed=traffic, transcendentals=0),
    )(*args)


def arr(*shape):
    return jax.ShapeDtypeStruct(shape, F32)


def shift(axis, step, closed):
    count = lax.axis_size(axis)
    return [
        (i, (i + step) % count) for i in range(count) if closed or 0 <= i + step < count
    ]


def first_body(*refs):
    sources, (own, slots, plain), held, sems = refs[:7], refs[7:10], refs[10:17], refs[17]
    moves = [
        pltpu.make_async_copy(source, target, sems.at[i])
        for i, (source, target) in enumerate(zip(sources, held))
    ]
    for move in moves:
        move.start()
    fields, speeds, resist, owners, rows, maps, conductance = held
    for move in moves[1:3]:
        move.wait()
    for plane in range(4):
        for shell in range(SHELLS):
            found = speeds[plane, shell] if plane < 3 else resist[shell]
            plain[plane, shell * LONS : shell * LONS + LONS, :] = found.astype(F32)
    moves[0].wait()
    for plane in range(PLANES):
        for lon in range(LONS):
            at = pl.ds(lon, SHELLS, stride=LONS)
            if plane < FIELDS:
                own[plane, lon] = fields[plane, at, :]
            else:
                own[plane, lon] = plain[plane - FIELDS, at, :]
    for move in moves[3:]:
        move.wait()
    slot_body(owners, rows, maps, conductance, slots)


def first(*args):
    vmem = pl.BlockSpec(memory_space=pltpu.VMEM)
    return pl.pallas_call(
        first_body,
        out_shape=(arr(PLANES, LONS, SHELLS, LATS), arr(4 * SENT, LATS)),
        in_specs=[pl.BlockSpec(memory_space=pltpu.HBM)] * len(args),
        out_specs=[vmem, vmem],
        scratch_shapes=[pltpu.VMEM((4, SHELLS * LONS, LATS), F32)]
        + [pltpu.VMEM(arg.shape, arg.dtype) for arg in args]
        + [pltpu.SemaphoreType.DMA((len(args),))],
        compiler_params=pltpu.CompilerParams(vmem_limit_bytes=60 * 2**20),
        cost_estimate=pl.CostEstimate(flops=10**6, bytes_accessed=10**6, transcendentals=0),
    )(*args)


def edge_body(low, own, high, above, below, edges, tall):
    found, _ = chunks()
    group = lax.broadcasted_iota(jnp.int32, (TALL, LATS), 1) // 8
    for plane in range(PLANES):
        for wide in range(WIDE):
            ref = (low, own, high)[wide // LONS]
            tall[plane, wide, :SHELLS, :] = ref[plane, wide % LONS]
            tall[plane, wide, SHELLS:, :] = jnp.zeros((TALL - SHELLS, LATS), F32)
        for wide, start, count in found:
            tall[plane, wide, SHELLS : SHELLS + count, :] = above[plane, start : start + count, :]
            tall[plane, wide, TALL - count :, :] = below[plane, start : start + count, :]
    for plane in range(PLANES):
        packed = jnp.zeros((TALL, LATS), F32)
        for wide in range(1, WIDE - 1):
            turned = pltpu.roll(tall[plane, wide], 8 * wide + 4, axis=1)
            packed = jnp.where(group == wide, turned, packed)
        edges[plane] = packed


def halo_lanes(edges, wide):
    lane = lax.broadcasted_iota(jnp.int32, edges.shape, 1)
    turned = pltpu.roll(edges, (LATS - 8 * wide - 4) % LATS, axis=1)
    return jnp.where((lane < 4) | (lane >= LATS - 4), turned, 0.0)


def weights(speeds, resist):
    out = []
    total = None
    for speed in speeds:
        lower = COURANT * jnp.maximum(speed, 0.0) + resist
        upper = resist - COURANT * jnp.minimum(speed, 0.0)
        out += [lower, upper]
        total = lower + upper if total is None else total + lower + upper
    return [1.0 - total] + out


def blend(w, centre, shell_lo, shell_hi, lon_lo, lon_hi, lat_lo, lat_hi):
    return (
        w[0] * centre
        + (w[1] * shell_lo + w[2] * shell_hi)
        + (w[3] * lon_lo + w[4] * lon_hi)
        + (w[5] * lat_lo + w[6] * lat_hi)
    )


def raw_chunks():
    found = []
    at = 0
    for plane in (5, 6, 8, 9, 10, 11):
        reach = PHASES + 1 if plane < FIELDS else PHASES
        for wide in range(WIDE):
            count = reach - max(LONS - wide, wide - 2 * LONS + 1, 0)
            if count > 0:
                found.append((plane, wide, at, count))
                at += count
    return found


def raw_body(low, own, high, out):
    for plane, wide, at, count in raw_chunks():
        ref = (low, own, high)[wide // LONS]
        for block in range(4):
            row = block * RAW + at
            out[row : row + count, :] = ref[plane, wide % LONS, :count, :]


def inner_body(raw, out, cells):
    span = 4 * LATS
    lane = lax.broadcasted_iota(jnp.int32, (8, span), 1)
    bottom = lax.broadcasted_iota(jnp.int32, (8, span), 0) == 0
    first, last = lane == 0, lane == span - 1
    cells[...] = jnp.zeros(cells.shape, F32)
    order = (5, 6, 8, 9, 10, 11)
    for plane, wide, at, count in raw_chunks():
        for rad in range(4):
            cells[order.index(plane), wide, :count, rad * LATS : (rad + 1) * LATS] = raw[
                rad * RAW + at : rad * RAW + at + count, :
            ]
    w = [None] + [
        weights([cells[2 + d, wide] for d in range(3)], cells[5, wide])
        for wide in range(1, WIDE - 1)
    ]
    made = []
    for part in range(2):
        now = [cells[part, wide] for wide in range(WIDE)]
        for phase in range(PHASES):
            fresh = list(now)
            for wide in range(phase + 1, WIDE - 1 - phase):
                c = now[wide]
                fresh[wide] = blend(
                    w[wide],
                    c,
                    jnp.where(bottom, 0.0, pltpu.roll(c, 1, axis=0)),
                    pltpu.roll(c, 7, axis=0),
                    now[wide - 1],
                    now[wide + 1],
                    jnp.where(first, 0.0, pltpu.roll(c, 1, axis=1)),
                    jnp.where(last, 0.0, pltpu.roll(c, span - 1, axis=1)),
                )
            now = fresh
        made.append(now[LONS : 2 * LONS])
    blon, blat = made
    for lon in range(LONS):
        c = blon[lon]
        source = jnp.where(first, 0.0, pltpu.roll(c, 1, axis=1)) - jnp.where(
            last, 0.0, pltpu.roll(c, span - 1, axis=1)
        )
        if lon < LONS - 1:
            source = source + blat[lon + 1]
        if lon > 0:
            source = source - blat[lon - 1]
        for rad in range(4):
            part = slice(rad * LATS, (rad + 1) * LATS)
            at = rad // 2 * 12 + rad % 2 * 4 + lon
            out[at : at + 1, :] = source[0:1, part]
            at = rad // 2 * 12 + 8 + rad % 2
            if lon == 0:
                out[at : at + 1, :] = blat[0][0:1, part]
            if lon == LONS - 1:
                out[at + 2 : at + 3, :] = blat[LONS - 1][0:1, part]


def base_body(spot, sent, out, cond):
    step = LATE - 16
    odd = spot[0] % 2 == 1
    for lon in range(LONS):
        at = 130 + lon
        lines = [sent[rad * SENT + at : rad * SENT + at + 1, :] for rad in range(4)]
        cond[lon : lon + 1, :] = jnp.where(odd, lines[2], lines[0])
        line = jnp.where(odd, lines[3], lines[1])
        out[pl.ds(lon, 32, stride=step), :] = jnp.broadcast_to(line, (32, LATS))
    lane = lax.broadcasted_iota(jnp.int32, (32, LATS), 1)
    owner = lax.broadcasted_iota(jnp.int32, (32, LATS), 0)
    for rad in range(4):
        for row in range(4):
            at = rad * SENT + row * 32
            out[pl.ds(4 + rad * 5 + row, 32, stride=step), :] = sent[at : at + 32, :]
        marks = []
        for slot in range(2):
            at = rad * SENT + 128 + slot
            line = jnp.broadcast_to(sent[at : at + 1, :], (32, LATS))
            marks.append(
                jnp.sum(jnp.where(lane == owner + spot[1] * 32, line, 0.0), axis=1, keepdims=True)
            )
        out[pl.ds(8 + rad * 5, 32, stride=step), :] = jnp.where(lane < 64, marks[0], marks[1])


def join_body(spot, one, two, cond, base, out, head, copies, sems):
    rest = pltpu.make_async_copy(base, out.at[:, pl.ds(16, LATE - 16), :], sems.at[0])
    rest.start()
    source = one[...] + two[...]
    head[:12, :] = jnp.where(spot[0] % 2 == 1, source[12:], source[:12])
    head[12:, :] = cond[...]
    mine = head[...]
    for owner in range(32):
        copies[owner] = mine
    move = pltpu.make_async_copy(copies, out.at[:, pl.ds(0, 16), :], sems.at[1])
    move.start()
    move.wait()
    rest.wait()


def join(spot, one, two, cond, base):
    vmem = pl.BlockSpec(memory_space=pltpu.VMEM)
    plain = pl.BlockSpec(memory_space=pl.ANY)
    return pl.pallas_call(
        join_body,
        out_shape=arr(32, LATE, LATS),
        in_specs=[pl.BlockSpec(memory_space=pltpu.SMEM), vmem, vmem, vmem, plain],
        out_specs=plain,
        scratch_shapes=[
            pltpu.VMEM((16, LATS), F32),
            pltpu.VMEM((32, 16, LATS), F32),
            pltpu.SemaphoreType.DMA((2,)),
        ],
        compiler_params=pltpu.CompilerParams(vmem_limit_bytes=4 * 2**20),
        cost_estimate=pl.CostEstimate(flops=10**5, bytes_accessed=10**6, transcendentals=0),
    )(spot, one, two, cond, base)


def half_body(late, out):
    for row in range(HALF):
        out[row] = late[pl.ds(row, 32, stride=LATE), :]


def mark_body(late, cells, hot, tall):
    lane = lax.broadcasted_iota(jnp.int32, (32, LATS), 1).astype(F32)
    for rad in range(4):
        marks = late[pl.ds(HALF + rad * 5 + 4, 32, stride=LATE), :]
        for slot in range(2):
            row = marks if slot == 0 else pltpu.roll(marks, 64, axis=1)
            tall[slot, rad * 32 : rad * 32 + 32, :] = jnp.where(row == lane, 1.0, 0.0)
            for half in range(2):
                cells[(rad * 2 + slot) * 2 + half] = late[
                    pl.ds(HALF + rad * 5 + 2 * slot + half, 32, stride=LATE), :
                ].astype(jnp.int32)
    for slot in range(2):
        hot[:, slot * LATS : (slot + 1) * LATS] = jnp.transpose(tall[slot])[:ROWS_OWN]


def chunks():
    found = []
    at = 0
    for wide in range(1, WIDE - 1):
        far = max(LONS - wide, wide - 2 * LONS + 1, 0)
        count = PHASES - far
        found.append((wide, at, count))
        at += count
    return found, at


def pack_body(spot, low, own, high, near, away):
    found, rows = chunks()

    def pack(up, down):
        for plane in range(PLANES):
            for wide, start, count in found:
                ref = (low, own, high)[wide // LONS]
                up[plane, start : start + count, :] = ref[plane, wide % LONS, SHELLS - count :, :]
                down[plane, start : start + count, :] = ref[plane, wide % LONS, :count, :]
            up[plane, rows:, :] = jnp.zeros((32 - rows, LATS), F32)
            down[plane, rows:, :] = jnp.zeros((32 - rows, LATS), F32)

    @pl.when(spot[0] % 2 == 0)
    def _():
        pack(near, away)

    @pl.when(spot[0] % 2 == 1)
    def _():
        pack(away, near)


def main_body(low, own, high, above, below, from_low, from_high, out, cells, w, speeds):
    found, _ = chunks()
    lane = lax.broadcasted_iota(jnp.int32, (TALL, LATS), 1)

    def fill(plane, target):
        strip = jnp.where(lane % 8 < 4, from_low[plane], from_high[plane])
        for wide in range(WIDE):
            ref = (low, own, high)[wide // LONS]
            target[wide, :SHELLS, :LATS] = ref[plane, wide % LONS]
            target[wide, SHELLS:, :LATS] = jnp.zeros((TALL - SHELLS, LATS), F32)
            if 0 < wide < WIDE - 1:
                target[wide, :, LATS:] = halo_lanes(strip, wide)
            else:
                target[wide, :, LATS:] = jnp.zeros((TALL, LATS), F32)
        for wide, start, count in found:
            target[wide, SHELLS : SHELLS + count, :LATS] = above[plane, start : start + count, :]
            target[wide, TALL - count :, :LATS] = below[plane, start : start + count, :]

    for d in range(4):
        fill(FIELDS + d, speeds.at[d])
    for wide in range(1, WIDE - 1):
        made = weights([speeds[d, wide] for d in range(3)], speeds[3, wide])
        for i in range(7):
            w[i, wide] = made[i]

    def one(field, carry):
        fill(field, cells.at[0])
        for phase in range(PHASES):
            old = cells.at[phase % 2]
            new = cells.at[(phase + 1) % 2]
            for wide in range(phase + 1, WIDE - 1 - phase):
                c = old[wide]
                sides = [
                    c,
                    pltpu.roll(c, 1, axis=0),
                    pltpu.roll(c, TALL - 1, axis=0),
                    old[wide - 1],
                    old[wide + 1],
                    pltpu.roll(c, 1, axis=1),
                    pltpu.roll(c, 2 * LATS - 1, axis=1),
                ]
                if phase == PHASES - 1:
                    made = blend(
                        [w[i, wide, :SHELLS, :LATS] for i in range(7)],
                        *[side[:SHELLS, :LATS] for side in sides],
                    )
                    out[field, pl.ds(wide - LONS, SHELLS, stride=LONS), :] = made
                else:
                    new[wide] = blend([w[i, wide] for i in range(7)], *sides)
        return carry

    lax.fori_loop(0, FIELDS, one, 0)


def slot_body(owners, rows, maps, conductance, out):
    count = owners.shape[1]
    here = lax.broadcasted_iota(jnp.int32, (count, count), 0)
    there = lax.broadcasted_iota(jnp.int32, (count, count), 1)
    aimed = (here % 32) * 4 + here // 32 == owners[...]
    earlier = jnp.dot(
        aimed.astype(jnp.bfloat16), (here < there).astype(jnp.bfloat16), preferred_element_type=F32
    )
    cell = maps[...]
    small = (cell & 127).astype(F32).astype(jnp.bfloat16)
    large = (cell >> 7).astype(F32).astype(jnp.bfloat16)
    row = jnp.broadcast_to((rows[...] + 1).astype(F32), (8, count)).astype(jnp.bfloat16)
    marks = []
    lines = []
    for slot in range(2):
        pick = jnp.where(aimed & (earlier == float(slot)), 1.0, 0.0).astype(jnp.bfloat16)
        marks.append(
            lax.dot_general(row, pick, (((1,), (1,)), ((), ())), preferred_element_type=F32) - 1.0
        )
        made = jnp.dot(pick, small, preferred_element_type=F32) + 128.0 * jnp.dot(
            pick, large, preferred_element_type=F32
        )
        lines += [made[:, :128], made[:, 128:]]
    for rad in range(4):
        for j in range(4):
            at = rad * SENT + j * 32
            out[at : at + 32, :] = lines[j][rad * 32 : rad * 32 + 32]
        at = rad * SENT + 128
        out[at : at + 1, :] = marks[0][:1]
        out[at + 1 : at + 2, :] = marks[1][:1]
        out[at + 2 : at + 6, :] = conductance[...]
        out[at + 6 : at + 8, :] = jnp.zeros((2, LATS), F32)


def final_body(
    spot, mine, other, cells, hot, pot, foot, phi, east_w, west_w, north_w, south_w, start, picked
):
    devs, rads = 32, 4
    wide = rads * LATS
    lane = lax.broadcasted_iota(jnp.int32, (devs, wide), 1)

    odd = spot[0] % 2

    def gather(at, step):
        found = []
        for rad in range(rads):
            row = at + rad % 2 * step
            found.append(jnp.where(odd == rad // 2, mine[row], other[row]))
        return jnp.concatenate(found, axis=1)

    def lon_up(values, lon):
        return values[lon + 1] if lon < LONS - 1 else pltpu.roll(values[0], devs - 1, axis=0)

    def lon_down(values, lon):
        return values[lon - 1] if lon > 0 else pltpu.roll(values[LONS - 1], 1, axis=0)

    def lat_up(value):
        return pltpu.roll(value, wide - 1, axis=1)

    def lat_down(value):
        return pltpu.roll(value, 1, axis=1)

    cond = [gather(12 + lon, 4) for lon in range(LONS)]
    sources = [gather(lon, 4) for lon in range(LONS)]
    sources[LONS - 1] += pltpu.roll(gather(8, 1), devs - 1, axis=0)
    sources[0] -= pltpu.roll(gather(10, 1), 1, axis=0)
    last, first = lane == wide - 1, lane == 0
    for lon in range(LONS):
        source = sources[lon]
        c = cond[lon]
        east = 0.5 * (c + lon_up(cond, lon))
        west = 0.5 * (c + lon_down(cond, lon))
        north = 0.5 * (c + jnp.where(last, 0.0, lat_up(c)))
        south = 0.5 * (c + jnp.where(first, 0.0, lat_down(c)))
        scale = RELAX / (DAMPING * c + east + west + north + south)
        east_w[lon] = east * scale
        west_w[lon] = west * scale
        north_w[lon] = jnp.where(last, 0.0, north * scale)
        south_w[lon] = jnp.where(first, 0.0, south * scale)
        start[lon] = source * scale
        phi[0, lon] = source * scale

    def sweep(old, new):
        values = [phi[old, lon] for lon in range(LONS)]
        for lon in range(LONS):
            c = values[lon]
            phi[new, lon] = (
                (1.0 - RELAX) * c
                + start[lon]
                + (east_w[lon] * lon_up(values, lon) + west_w[lon] * lon_down(values, lon))
                + (north_w[lon] * lat_up(c) + south_w[lon] * lat_down(c))
            )

    for turn in range(SWEEPS - 1):
        sweep(turn % 2, (turn + 1) % 2)
    done = (SWEEPS - 1) % 2
    at_lon = lax.broadcasted_iota(jnp.int32, (devs, LATS), 0) == spot[2]
    for rad in range(rads):

        @pl.when(spot[1] == rad)
        def _():
            for lon in range(LONS):
                block = phi[done, lon, :, rad * LATS : (rad + 1) * LATS]
                pot[lon : lon + 1, :] = jnp.sum(
                    jnp.where(at_lon, block, 0.0), axis=0, keepdims=True
                )

    for rad in range(rads):
        table = [phi[done, lon, :, rad * LATS : (rad + 1) * LATS] for lon in range(LONS)]
        for slot in range(2):
            at = (slot * rads + rad) * devs
            for half in range(2):
                cell = cells[(rad * 2 + slot) * 2 + half]
                place, lon_at = cell & 127, cell >> 7
                value = jnp.zeros((devs, LATS), F32)
                for lon in range(LONS):
                    found = jnp.take_along_axis(
                        table[lon], place, axis=1, mode="promise_in_bounds"
                    )
                    value = jnp.where(lon_at == lon, found, value)
                picked[at : at + devs, 128 * half : 128 * half + 128] = value
    records = picked[...]
    rows = hot[...].astype(jnp.bfloat16)
    large = records.astype(jnp.bfloat16)
    small = (records - large.astype(F32)).astype(jnp.bfloat16)
    foot[...] = jnp.dot(rows, large, preferred_element_type=F32) + jnp.dot(
        rows, small, preferred_element_type=F32
    )


def shards(plasma_fields, velocity, resistivity, conductance, foot_map, foot_owner, foot_row):
    spot = jnp.stack([lax.axis_index("sec"), lax.axis_index("rad"), lax.axis_index("lon")])
    own, slots = first(
        plasma_fields.reshape(FIELDS, SHELLS * LONS, LATS),
        velocity,
        resistivity,
        foot_owner.reshape(1, -1),
        foot_row.reshape(1, -1),
        foot_map,
        conductance,
    )
    count = lax.axis_size("lon")
    wrap = [(i, (i + (1 if i % 2 else -1)) % count) for i in range(count)]
    first_swap = lax.ppermute(own, "lon", wrap)
    second_swap = lax.ppermute(own, "lon", [(i, i ^ 1) for i in range(count)])

    sent = lax.all_to_all(
        slots.reshape(4, SENT, LATS), "rad", split_axis=0, concat_axis=0, tiled=True
    )

    first_swap, second_swap, sent = lax.optimization_barrier((first_swap, second_swap, sent))
    odd = lax.axis_index("lon") % 2 == 1
    low = jnp.where(odd, second_swap, first_swap)
    high = jnp.where(odd, first_swap, second_swap)
    near_rows, away_rows = call(
        pack_body,
        (arr(PLANES, 32, LATS), arr(PLANES, 32, LATS)),
        (spot, low, own, high),
        smem=(0,),
    )
    away_rows = lax.ppermute(away_rows, "sec", [(1, 2), (2, 1)])
    raw = call(raw_body, arr(4 * RAW, LATS), (low, own, high))
    owner = lax.axis_index("sec") == 0

    def advance_inner(rows):
        gathered = lax.all_to_all(
            rows.reshape(4, RAW, LATS), "rad", split_axis=0, concat_axis=0, tiled=True
        )
        return call(
            inner_body,
            arr(24, LATS),
            (gathered.reshape(4 * RAW, LATS),),
            scratch=(pltpu.VMEM((6, WIDE, 8, 4 * LATS), F32),),
        )

    inner = lax.cond(owner, advance_inner, lambda rows: jnp.zeros((24, LATS), F32), raw)
    away_rows, inner = lax.optimization_barrier((away_rows, inner))
    far = lax.ppermute(inner, "sec", [(0, 3)])
    far = inner + far
    near = lax.ppermute(far, "sec", [(0, 1), (3, 2)])
    base, cond = call(
        base_body,
        (arr(32 * (LATE - 16), LATS), arr(LONS, LATS)),
        (spot, sent.reshape(4 * SENT, LATS)),
        smem=(0,),
    )
    late = join(spot, far, near, cond, base.reshape(32, LATE - 16, LATS))
    late, low, high, near_rows = lax.optimization_barrier((late, low, high, near_rows))
    near_rows = lax.ppermute(near_rows, "sec", [(0, 1), (1, 0), (2, 3), (3, 2)])

    odd = lax.axis_index("sec") % 2 == 1
    above = jnp.where(odd, away_rows, near_rows)
    below = jnp.where(odd, near_rows, away_rows)
    blocks = (low, own, high, above, below)
    edges = call(
        edge_body,
        arr(PLANES, TALL, LATS),
        blocks,
        scratch=(pltpu.VMEM((PLANES, WIDE, TALL, LATS), F32),),
    )
    from_low = lax.ppermute(edges, "rad", shift("rad", 1, False))
    from_high = lax.ppermute(edges, "rad", shift("rad", -1, False))
    late = lax.all_to_all(
        late, "lon", split_axis=0, concat_axis=0, tiled=True
    )

    advanced = call(
        main_body,
        arr(FIELDS, SHELLS * LONS, LATS),
        blocks + (from_low, from_high),
        scratch=(
            pltpu.VMEM((2, WIDE, TALL, 2 * LATS), F32),
            pltpu.VMEM((7, WIDE, TALL, 2 * LATS), F32),
            pltpu.VMEM((4, WIDE, TALL, 2 * LATS), F32),
        ),
    ).reshape(FIELDS, SHELLS, LONS, LATS)

    late, advanced = lax.optimization_barrier((late, advanced))
    late = late.reshape(32 * LATE, LATS)
    mine = call(half_body, arr(HALF, 32, LATS), (late,))
    other = lax.ppermute(mine, "sec", [(0, 1), (1, 0), (2, 3), (3, 2)])
    cells, hot = call(
        mark_body,
        (jax.ShapeDtypeStruct((16, 32, LATS), jnp.int32), arr(ROWS_OWN, 2 * LATS)),
        (late,),
        scratch=(pltpu.VMEM((2, LATS, LATS), F32),),
    )
    plane = pltpu.VMEM((LONS, 32, 4 * LATS), F32)
    potential, foot_table = call(
        final_body,
        (arr(LONS, LATS), arr(ROWS_OWN, 256)),
        (spot, mine, other, cells, hot),
        scratch=(
            pltpu.VMEM((2, LONS, 32, 4 * LATS), F32),
            plane,
            plane,
            plane,
            plane,
            plane,
            pltpu.VMEM((256, 256), F32),
        ),
        smem=(0,),
    )
    return (advanced, potential, foot_table)


def solution(mesh):
    in_specs = (
        P(None, "sec", "lon", "rad"),
        P(None, "sec", "lon", "rad"),
        P("sec", "lon", "rad"),
        P("lon", "rad"),
        P(("lon", "sec", "rad"), None),
        P(("lon", "sec", "rad"), None),
        P(("lon", "sec", "rad")),
    )
    out_specs = (P(None, "sec", "lon", "rad"), P("lon", "rad"), P(("lon", "sec", "rad"), None))
    return jax.shard_map(shards, mesh=mesh, in_specs=in_specs, out_specs=out_specs, check_vma=False)
```

```python
import jax
import jax.numpy as jnp
from jax import lax
from jax.experimental import pallas as pl
from jax.experimental.pallas import tpu as pltpu
from jax.sharding import PartitionSpec as P

PHASES = 4
SWEEPS = 8
ROWS_OWN = 32
COURANT = 0.25
DAMPING = 0.05
RELAX = 0.8

FIELDS = 8
PLANES = FIELDS + 4
SHELLS = 16
LONS = 4
LATS = 128
WIDE = 3 * LONS
LATE = 40
HALF = 20
RAW = 192
SENT = 136
TALL = SHELLS + 2 * PHASES
F32 = jnp.float32


def call(body, out_shape, args, scratch=(), smem=(), flops=10**6, traffic=10**6):
    specs = [
        pl.BlockSpec(memory_space=pltpu.SMEM if i in smem else pltpu.VMEM)
        for i in range(len(args))
    ]
    many = isinstance(out_shape, (tuple, list))
    vmem = pl.BlockSpec(memory_space=pltpu.VMEM)
    return pl.pallas_call(
        body,
        out_shape=out_shape,
        in_specs=specs,
        out_specs=[vmem] * len(out_shape) if many else vmem,
        scratch_shapes=list(scratch),
        compiler_params=pltpu.CompilerParams(vmem_limit_bytes=16 * 2**20),
        cost_estimate=pl.CostEstimate(flops=flops, bytes_accessed=traffic, transcendentals=0),
    )(*args)


def arr(*shape):
    return jax.ShapeDtypeStruct(shape, F32)


def where():
    return [lax.axis_index(axis) for axis in ("sec", "rad", "lon")]


def shift(axis, step, closed):
    count = lax.axis_size(axis)
    return [
        (i, (i + step) % count) for i in range(count) if closed or 0 <= i + step < count
    ]


def first_body(*refs):
    sources, (own, slots, plain), held, sems = refs[:7], refs[7:10], refs[10:17], refs[17]
    moves = [
        pltpu.make_async_copy(source, target, sems.at[i])
        for i, (source, target) in enumerate(zip(sources, held))
    ]
    for move in moves:
        move.start()
    fields, speeds, resist, owners, rows, maps, conductance = held
    for move in moves[1:3]:
        move.wait()
    for plane in range(4):
        for shell in range(SHELLS):
            found = speeds[plane, shell] if plane < 3 else resist[shell]
            plain[plane, shell * LONS : shell * LONS + LONS, :] = found.astype(F32)
    moves[0].wait()
    for plane in range(PLANES):
        for lon in range(LONS):
            at = pl.ds(lon, SHELLS, stride=LONS)
            if plane < FIELDS:
                own[plane, lon] = fields[plane, at, :]
            else:
                own[plane, lon] = plain[plane - FIELDS, at, :]
    for move in moves[3:]:
        move.wait()
    slot_body(owners, rows, maps, conductance, slots)


def first(*args):
    vmem = pl.BlockSpec(memory_space=pltpu.VMEM)
    return pl.pallas_call(
        first_body,
        out_shape=(arr(PLANES, LONS, SHELLS, LATS), arr(4 * SENT, LATS)),
        in_specs=[pl.BlockSpec(memory_space=pltpu.HBM)] * len(args),
        out_specs=[vmem, vmem],
        scratch_shapes=[pltpu.VMEM((4, SHELLS * LONS, LATS), F32)]
        + [pltpu.VMEM(arg.shape, arg.dtype) for arg in args]
        + [pltpu.SemaphoreType.DMA((len(args),))],
        compiler_params=pltpu.CompilerParams(vmem_limit_bytes=60 * 2**20),
        cost_estimate=pl.CostEstimate(flops=10**6, bytes_accessed=10**6, transcendentals=0),
    )(*args)


def edge_body(low, own, high, above, below, edges, tall):
    found, _ = chunks()
    group = lax.broadcasted_iota(jnp.int32, (TALL, LATS), 1) // 8
    for plane in range(PLANES):
        for wide in range(WIDE):
            ref = (low, own, high)[wide // LONS]
            tall[plane, wide, :SHELLS, :] = ref[plane, wide % LONS]
            tall[plane, wide, SHELLS:, :] = jnp.zeros((TALL - SHELLS, LATS), F32)
        for wide, start, count in found:
            tall[plane, wide, SHELLS : SHELLS + count, :] = above[plane, start : start + count, :]
            tall[plane, wide, TALL - count :, :] = below[plane, start : start + count, :]
    for plane in range(PLANES):
        packed = jnp.zeros((TALL, LATS), F32)
        for wide in range(1, WIDE - 1):
            turned = pltpu.roll(tall[plane, wide], 8 * wide + 4, axis=1)
            packed = jnp.where(group == wide, turned, packed)
        edges[plane] = packed


def halo_lanes(edges, wide):
    lane = lax.broadcasted_iota(jnp.int32, edges.shape, 1)
    turned = pltpu.roll(edges, (LATS - 8 * wide - 4) % LATS, axis=1)
    return jnp.where((lane < 4) | (lane >= LATS - 4), turned, 0.0)


def weights(speeds, resist):
    out = []
    total = None
    for speed in speeds:
        lower = COURANT * jnp.maximum(speed, 0.0) + resist
        upper = resist - COURANT * jnp.minimum(speed, 0.0)
        out += [lower, upper]
        total = lower + upper if total is None else total + lower + upper
    return [1.0 - total] + out


def blend(w, centre, shell_lo, shell_hi, lon_lo, lon_hi, lat_lo, lat_hi):
    return (
        w[0] * centre
        + (w[1] * shell_lo + w[2] * shell_hi)
        + (w[3] * lon_lo + w[4] * lon_hi)
        + (w[5] * lat_lo + w[6] * lat_hi)
    )


def raw_chunks():
    found = []
    at = 0
    for plane in (5, 6, 8, 9, 10, 11):
        reach = PHASES + 1 if plane < FIELDS else PHASES
        for wide in range(WIDE):
            count = reach - max(LONS - wide, wide - 2 * LONS + 1, 0)
            if count > 0:
                found.append((plane, wide, at, count))
                at += count
    return found


def raw_body(low, own, high, out):
    for plane, wide, at, count in raw_chunks():
        ref = (low, own, high)[wide // LONS]
        for block in range(4):
            row = block * RAW + at
            out[row : row + count, :] = ref[plane, wide % LONS, :count, :]


def inner_body(raw, out, cells):
    span = 4 * LATS
    lane = lax.broadcasted_iota(jnp.int32, (8, span), 1)
    bottom = lax.broadcasted_iota(jnp.int32, (8, span), 0) == 0
    first, last = lane == 0, lane == span - 1
    cells[...] = jnp.zeros(cells.shape, F32)
    order = (5, 6, 8, 9, 10, 11)
    for plane, wide, at, count in raw_chunks():
        for rad in range(4):
            cells[order.index(plane), wide, :count, rad * LATS : (rad + 1) * LATS] = raw[
                rad * RAW + at : rad * RAW + at + count, :
            ]
    w = [None] + [
        weights([cells[2 + d, wide] for d in range(3)], cells[5, wide])
        for wide in range(1, WIDE - 1)
    ]
    made = []
    for part in range(2):
        now = [cells[part, wide] for wide in range(WIDE)]
        for phase in range(PHASES):
            fresh = list(now)
            for wide in range(phase + 1, WIDE - 1 - phase):
                c = now[wide]
                fresh[wide] = blend(
                    w[wide],
                    c,
                    jnp.where(bottom, 0.0, pltpu.roll(c, 1, axis=0)),
                    pltpu.roll(c, 7, axis=0),
                    now[wide - 1],
                    now[wide + 1],
                    jnp.where(first, 0.0, pltpu.roll(c, 1, axis=1)),
                    jnp.where(last, 0.0, pltpu.roll(c, span - 1, axis=1)),
                )
            now = fresh
        made.append(now[LONS : 2 * LONS])
    blon, blat = made
    for lon in range(LONS):
        c = blon[lon]
        source = jnp.where(first, 0.0, pltpu.roll(c, 1, axis=1)) - jnp.where(
            last, 0.0, pltpu.roll(c, span - 1, axis=1)
        )
        if lon < LONS - 1:
            source = source + blat[lon + 1]
        if lon > 0:
            source = source - blat[lon - 1]
        for rad in range(4):
            part = slice(rad * LATS, (rad + 1) * LATS)
            at = rad // 2 * 12 + rad % 2 * 4 + lon
            out[at : at + 1, :] = source[0:1, part]
            at = rad // 2 * 12 + 8 + rad % 2
            if lon == 0:
                out[at : at + 1, :] = blat[0][0:1, part]
            if lon == LONS - 1:
                out[at + 2 : at + 3, :] = blat[LONS - 1][0:1, part]


def base_body(sent, out, cond):
    spot = where()
    step = LATE - 16
    odd = spot[0] % 2 == 1
    for lon in range(LONS):
        at = 130 + lon
        lines = [sent[rad * SENT + at : rad * SENT + at + 1, :] for rad in range(4)]
        cond[lon : lon + 1, :] = jnp.where(odd, lines[2], lines[0])
        line = jnp.where(odd, lines[3], lines[1])
        out[pl.ds(lon, 32, stride=step), :] = jnp.broadcast_to(line, (32, LATS))
    lane = lax.broadcasted_iota(jnp.int32, (32, LATS), 1)
    owner = lax.broadcasted_iota(jnp.int32, (32, LATS), 0)
    for rad in range(4):
        for row in range(4):
            at = rad * SENT + row * 32
            out[pl.ds(4 + rad * 5 + row, 32, stride=step), :] = sent[at : at + 32, :]
        marks = []
        for slot in range(2):
            at = rad * SENT + 128 + slot
            line = jnp.broadcast_to(sent[at : at + 1, :], (32, LATS))
            marks.append(
                jnp.sum(jnp.where(lane == owner + spot[1] * 32, line, 0.0), axis=1, keepdims=True)
            )
        out[pl.ds(8 + rad * 5, 32, stride=step), :] = jnp.where(lane < 64, marks[0], marks[1])


def join_body(one, two, cond, base, out, head, copies, sems):
    rest = pltpu.make_async_copy(base, out.at[:, pl.ds(16, LATE - 16), :], sems.at[0])
    rest.start()
    source = one[...] + two[...]
    spot = where()
    head[:12, :] = jnp.where(spot[0] % 2 == 1, source[12:], source[:12])
    head[12:, :] = cond[...]
    mine = head[...]
    for owner in range(32):
        copies[owner] = mine
    move = pltpu.make_async_copy(copies, out.at[:, pl.ds(0, 16), :], sems.at[1])
    move.start()
    move.wait()
    rest.wait()


def join(one, two, cond, base):
    vmem = pl.BlockSpec(memory_space=pltpu.VMEM)
    plain = pl.BlockSpec(memory_space=pl.ANY)
    return pl.pallas_call(
        join_body,
        out_shape=arr(32, LATE, LATS),
        in_specs=[vmem, vmem, vmem, plain],
        out_specs=plain,
        scratch_shapes=[
            pltpu.VMEM((16, LATS), F32),
            pltpu.VMEM((32, 16, LATS), F32),
            pltpu.SemaphoreType.DMA((2,)),
        ],
        compiler_params=pltpu.CompilerParams(vmem_limit_bytes=4 * 2**20),
        cost_estimate=pl.CostEstimate(flops=10**5, bytes_accessed=10**6, transcendentals=0),
    )(one, two, cond, base)


def half_body(late, out):
    for row in range(HALF):
        out[row] = late[pl.ds(row, 32, stride=LATE), :]


def mark_body(late, cells, hot, tall):
    lane = lax.broadcasted_iota(jnp.int32, (32, LATS), 1).astype(F32)
    for rad in range(4):
        marks = late[pl.ds(HALF + rad * 5 + 4, 32, stride=LATE), :]
        for slot in range(2):
            row = marks if slot == 0 else pltpu.roll(marks, 64, axis=1)
            tall[slot, rad * 32 : rad * 32 + 32, :] = jnp.where(row == lane, 1.0, 0.0)
            for half in range(2):
                cells[(rad * 2 + slot) * 2 + half] = late[
                    pl.ds(HALF + rad * 5 + 2 * slot + half, 32, stride=LATE), :
                ].astype(jnp.int32)
    for slot in range(2):
        hot[:, slot * LATS : (slot + 1) * LATS] = jnp.transpose(tall[slot])[:ROWS_OWN]


def chunks():
    found = []
    at = 0
    for wide in range(1, WIDE - 1):
        far = max(LONS - wide, wide - 2 * LONS + 1, 0)
        count = PHASES - far
        found.append((wide, at, count))
        at += count
    return found, at


def pack_body(low, own, high, near, away):
    found, rows = chunks()
    spot = where()

    def pack(up, down):
        for plane in range(PLANES):
            for wide, start, count in found:
                ref = (low, own, high)[wide // LONS]
                up[plane, start : start + count, :] = ref[plane, wide % LONS, SHELLS - count :, :]
                down[plane, start : start + count, :] = ref[plane, wide % LONS, :count, :]
            up[plane, rows:, :] = jnp.zeros((32 - rows, LATS), F32)
            down[plane, rows:, :] = jnp.zeros((32 - rows, LATS), F32)

    @pl.when(spot[0] % 2 == 0)
    def _():
        pack(near, away)

    @pl.when(spot[0] % 2 == 1)
    def _():
        pack(away, near)


def main_body(low, own, high, above, below, from_low, from_high, out, cells, w, speeds):
    found, _ = chunks()
    lane = lax.broadcasted_iota(jnp.int32, (TALL, LATS), 1)

    def fill(plane, target):
        strip = jnp.where(lane % 8 < 4, from_low[plane], from_high[plane])
        for wide in range(WIDE):
            ref = (low, own, high)[wide // LONS]
            target[wide, :SHELLS, :LATS] = ref[plane, wide % LONS]
            target[wide, SHELLS:, :LATS] = jnp.zeros((TALL - SHELLS, LATS), F32)
            if 0 < wide < WIDE - 1:
                target[wide, :, LATS:] = halo_lanes(strip, wide)
            else:
                target[wide, :, LATS:] = jnp.zeros((TALL, LATS), F32)
        for wide, start, count in found:
            target[wide, SHELLS : SHELLS + count, :LATS] = above[plane, start : start + count, :]
            target[wide, TALL - count :, :LATS] = below[plane, start : start + count, :]

    for d in range(4):
        fill(FIELDS + d, speeds.at[d])
    for wide in range(1, WIDE - 1):
        made = weights([speeds[d, wide] for d in range(3)], speeds[3, wide])
        for i in range(7):
            w[i, wide] = made[i]

    def one(field, carry):
        fill(field, cells.at[0])
        for phase in range(PHASES):
            old = cells.at[phase % 2]
            new = cells.at[(phase + 1) % 2]
            for wide in range(phase + 1, WIDE - 1 - phase):
                c = old[wide]
                sides = [
                    c,
                    pltpu.roll(c, 1, axis=0),
                    pltpu.roll(c, TALL - 1, axis=0),
                    old[wide - 1],
                    old[wide + 1],
                    pltpu.roll(c, 1, axis=1),
                    pltpu.roll(c, 2 * LATS - 1, axis=1),
                ]
                if phase == PHASES - 1:
                    made = blend(
                        [w[i, wide, :SHELLS, :LATS] for i in range(7)],
                        *[side[:SHELLS, :LATS] for side in sides],
                    )
                    out[field, pl.ds(wide - LONS, SHELLS, stride=LONS), :] = made
                else:
                    new[wide] = blend([w[i, wide] for i in range(7)], *sides)
        return carry

    lax.fori_loop(0, FIELDS, one, 0)


def slot_body(owners, rows, maps, conductance, out):
    count = owners.shape[1]
    here = lax.broadcasted_iota(jnp.int32, (count, count), 0)
    there = lax.broadcasted_iota(jnp.int32, (count, count), 1)
    aimed = (here % 32) * 4 + here // 32 == owners[...]
    earlier = jnp.dot(
        aimed.astype(jnp.bfloat16), (here < there).astype(jnp.bfloat16), preferred_element_type=F32
    )
    cell = maps[...]
    small = (cell & 127).astype(F32).astype(jnp.bfloat16)
    large = (cell >> 7).astype(F32).astype(jnp.bfloat16)
    row = jnp.broadcast_to((rows[...] + 1).astype(F32), (8, count)).astype(jnp.bfloat16)
    marks = []
    lines = []
    for slot in range(2):
        pick = jnp.where(aimed & (earlier == float(slot)), 1.0, 0.0).astype(jnp.bfloat16)
        marks.append(
            lax.dot_general(row, pick, (((1,), (1,)), ((), ())), preferred_element_type=F32) - 1.0
        )
        made = jnp.dot(pick, small, preferred_element_type=F32) + 128.0 * jnp.dot(
            pick, large, preferred_element_type=F32
        )
        lines += [made[:, :128], made[:, 128:]]
    for rad in range(4):
        for j in range(4):
            at = rad * SENT + j * 32
            out[at : at + 32, :] = lines[j][rad * 32 : rad * 32 + 32]
        at = rad * SENT + 128
        out[at : at + 1, :] = marks[0][:1]
        out[at + 1 : at + 2, :] = marks[1][:1]
        out[at + 2 : at + 6, :] = conductance[...]
        out[at + 6 : at + 8, :] = jnp.zeros((2, LATS), F32)


def final_body(
    mine, other, cells, hot, pot, foot, phi, east_w, west_w, north_w, south_w, start, picked
):
    devs, rads = 32, 4
    spot = where()
    wide = rads * LATS
    lane = lax.broadcasted_iota(jnp.int32, (devs, wide), 1)

    odd = spot[0] % 2

    def gather(at, step):
        found = []
        for rad in range(rads):
            row = at + rad % 2 * step
            found.append(jnp.where(odd == rad // 2, mine[row], other[row]))
        return jnp.concatenate(found, axis=1)

    def lon_up(values, lon):
        return values[lon + 1] if lon < LONS - 1 else pltpu.roll(values[0], devs - 1, axis=0)

    def lon_down(values, lon):
        return values[lon - 1] if lon > 0 else pltpu.roll(values[LONS - 1], 1, axis=0)

    def lat_up(value):
        return pltpu.roll(value, wide - 1, axis=1)

    def lat_down(value):
        return pltpu.roll(value, 1, axis=1)

    cond = [gather(12 + lon, 4) for lon in range(LONS)]
    sources = [gather(lon, 4) for lon in range(LONS)]
    sources[LONS - 1] += pltpu.roll(gather(8, 1), devs - 1, axis=0)
    sources[0] -= pltpu.roll(gather(10, 1), 1, axis=0)
    last, first = lane == wide - 1, lane == 0
    for lon in range(LONS):
        source = sources[lon]
        c = cond[lon]
        east = 0.5 * (c + lon_up(cond, lon))
        west = 0.5 * (c + lon_down(cond, lon))
        north = 0.5 * (c + jnp.where(last, 0.0, lat_up(c)))
        south = 0.5 * (c + jnp.where(first, 0.0, lat_down(c)))
        scale = RELAX / (DAMPING * c + east + west + north + south)
        east_w[lon] = east * scale
        west_w[lon] = west * scale
        north_w[lon] = jnp.where(last, 0.0, north * scale)
        south_w[lon] = jnp.where(first, 0.0, south * scale)
        start[lon] = source * scale
        phi[0, lon] = source * scale

    def sweep(old, new):
        values = [phi[old, lon] for lon in range(LONS)]
        for lon in range(LONS):
            c = values[lon]
            phi[new, lon] = (
                (1.0 - RELAX) * c
                + start[lon]
                + (east_w[lon] * lon_up(values, lon) + west_w[lon] * lon_down(values, lon))
                + (north_w[lon] * lat_up(c) + south_w[lon] * lat_down(c))
            )

    for turn in range(SWEEPS - 1):
        sweep(turn % 2, (turn + 1) % 2)
    done = (SWEEPS - 1) % 2
    at_lon = lax.broadcasted_iota(jnp.int32, (devs, LATS), 0) == spot[2]
    for rad in range(rads):

        @pl.when(spot[1] == rad)
        def _():
            for lon in range(LONS):
                block = phi[done, lon, :, rad * LATS : (rad + 1) * LATS]
                pot[lon : lon + 1, :] = jnp.sum(
                    jnp.where(at_lon, block, 0.0), axis=0, keepdims=True
                )

    for rad in range(rads):
        table = [phi[done, lon, :, rad * LATS : (rad + 1) * LATS] for lon in range(LONS)]
        for slot in range(2):
            at = (slot * rads + rad) * devs
            for half in range(2):
                cell = cells[(rad * 2 + slot) * 2 + half]
                place, lon_at = cell & 127, cell >> 7
                value = jnp.zeros((devs, LATS), F32)
                for lon in range(LONS):
                    found = jnp.take_along_axis(
                        table[lon], place, axis=1, mode="promise_in_bounds"
                    )
                    value = jnp.where(lon_at == lon, found, value)
                picked[at : at + devs, 128 * half : 128 * half + 128] = value
    records = picked[...]
    rows = hot[...].astype(jnp.bfloat16)
    large = records.astype(jnp.bfloat16)
    small = (records - large.astype(F32)).astype(jnp.bfloat16)
    foot[...] = jnp.dot(rows, large, preferred_element_type=F32) + jnp.dot(
        rows, small, preferred_element_type=F32
    )


def shards(plasma_fields, velocity, resistivity, conductance, foot_map, foot_owner, foot_row):
    own, slots = first(
        plasma_fields.reshape(FIELDS, SHELLS * LONS, LATS),
        velocity,
        resistivity,
        foot_owner.reshape(1, -1),
        foot_row.reshape(1, -1),
        foot_map,
        conductance,
    )
    count = lax.axis_size("lon")
    wrap = [(i, (i + (1 if i % 2 else -1)) % count) for i in range(count)]
    first_swap = lax.ppermute(own, "lon", wrap)
    second_swap = lax.ppermute(own, "lon", [(i, i ^ 1) for i in range(count)])

    sent = lax.all_to_all(
        slots.reshape(4, SENT, LATS), "rad", split_axis=0, concat_axis=0, tiled=True
    )

    first_swap, second_swap, sent = lax.optimization_barrier((first_swap, second_swap, sent))
    odd = lax.axis_index("lon") % 2 == 1
    low = jnp.where(odd, second_swap, first_swap)
    high = jnp.where(odd, first_swap, second_swap)
    near_rows, away_rows = call(
        pack_body,
        (arr(PLANES, 32, LATS), arr(PLANES, 32, LATS)),
        (low, own, high),
    )
    away_rows = lax.ppermute(away_rows, "sec", [(1, 2), (2, 1)])
    raw = call(raw_body, arr(4 * RAW, LATS), (low, own, high))
    owner = lax.axis_index("sec") == 0

    def advance_inner(rows):
        gathered = lax.all_to_all(
            rows.reshape(4, RAW, LATS), "rad", split_axis=0, concat_axis=0, tiled=True
        )
        return call(
            inner_body,
            arr(24, LATS),
            (gathered.reshape(4 * RAW, LATS),),
            scratch=(pltpu.VMEM((6, WIDE, 8, 4 * LATS), F32),),
        )

    inner = lax.cond(owner, advance_inner, lambda rows: jnp.zeros((24, LATS), F32), raw)
    away_rows, inner = lax.optimization_barrier((away_rows, inner))
    far = lax.ppermute(inner, "sec", [(0, 3)])
    far = inner + far
    near = lax.ppermute(far, "sec", [(0, 1), (3, 2)])
    base, cond = call(
        base_body,
        (arr(32 * (LATE - 16), LATS), arr(LONS, LATS)),
        (sent.reshape(4 * SENT, LATS),),
    )
    late = join(far, near, cond, base.reshape(32, LATE - 16, LATS))
    late, low, high, near_rows = lax.optimization_barrier((late, low, high, near_rows))
    near_rows = lax.ppermute(near_rows, "sec", [(0, 1), (1, 0), (2, 3), (3, 2)])

    odd = lax.axis_index("sec") % 2 == 1
    above = jnp.where(odd, away_rows, near_rows)
    below = jnp.where(odd, near_rows, away_rows)
    blocks = (low, own, high, above, below)
    edges = call(
        edge_body,
        arr(PLANES, TALL, LATS),
        blocks,
        scratch=(pltpu.VMEM((PLANES, WIDE, TALL, LATS), F32),),
    )
    from_low = lax.ppermute(edges, "rad", shift("rad", 1, False))
    from_high = lax.ppermute(edges, "rad", shift("rad", -1, False))
    late = lax.all_to_all(
        late, "lon", split_axis=0, concat_axis=0, tiled=True
    )

    advanced = call(
        main_body,
        arr(FIELDS, SHELLS * LONS, LATS),
        blocks + (from_low, from_high),
        scratch=(
            pltpu.VMEM((2, WIDE, TALL, 2 * LATS), F32),
            pltpu.VMEM((7, WIDE, TALL, 2 * LATS), F32),
            pltpu.VMEM((4, WIDE, TALL, 2 * LATS), F32),
        ),
    ).reshape(FIELDS, SHELLS, LONS, LATS)

    late, advanced = lax.optimization_barrier((late, advanced))
    late = late.reshape(32 * LATE, LATS)
    mine = call(half_body, arr(HALF, 32, LATS), (late,))
    other = lax.ppermute(mine, "sec", [(0, 1), (1, 0), (2, 3), (3, 2)])
    cells, hot = call(
        mark_body,
        (jax.ShapeDtypeStruct((16, 32, LATS), jnp.int32), arr(ROWS_OWN, 2 * LATS)),
        (late,),
        scratch=(pltpu.VMEM((2, LATS, LATS), F32),),
    )
    plane = pltpu.VMEM((LONS, 32, 4 * LATS), F32)
    potential, foot_table = call(
        final_body,
        (arr(LONS, LATS), arr(ROWS_OWN, 256)),
        (mine, other, cells, hot),
        scratch=(
            pltpu.VMEM((2, LONS, 32, 4 * LATS), F32),
            plane,
            plane,
            plane,
            plane,
            plane,
            pltpu.VMEM((256, 256), F32),
        ),
    )
    return (advanced, potential, foot_table)


def solution(mesh):
    in_specs = (
        P(None, "sec", "lon", "rad"),
        P(None, "sec", "lon", "rad"),
        P("sec", "lon", "rad"),
        P("lon", "rad"),
        P(("lon", "sec", "rad"), None),
        P(("lon", "sec", "rad"), None),
        P(("lon", "sec", "rad")),
    )
    out_specs = (P(None, "sec", "lon", "rad"), P("lon", "rad"), P(("lon", "sec", "rad"), None))
    return jax.shard_map(shards, mesh=mesh, in_specs=in_specs, out_specs=out_specs, check_vma=False)
```
